32 devices in a mesh: grp: 8 (over z, core), blk: 4 (over y, x).
Axes of the slice: x: 2, y: 2, z: 4, core: 2. Of those that a mesh axis runs over, the one named last changes fastest.
Arguments:
- slab: bfloat16 [2048, 32768], P(('grp', 'blk')), as said below
- pick_owner: int32 [2048, 1], P(('grp', 'blk')), may hold values from 0 to 3; in each aligned block of 64 rows (0 to 63, 64 to 127, ...) at most 32 rows name the same one
- pick_offset: int32 [2048], P(('grp', 'blk')), may hold values from 0 to 63
- wedge_id: int32 [2048], P(('grp', 'blk')), may hold values from 0 to 7
- live_count: int32 [32], P(('grp', 'blk')), may hold values from 16 to 64, as said below
- references: bfloat16 [192, 32768], P('blk')
- wedge: float32 [8, 32768], replicated, may hold values from 0.05 to 1
Outputs:
- new_refs: float32 [192, 32768], P('blk', 'grp')
The draws below stay inside these ranges and needn't reach their ends.
Inputs may be any that keep to these rules, and one draw needn't show every extreme that they name: `pick_owner`: on one device at most 32 slots name the same owner. `live_count`: live slots are the first ones of a device; some device has all 64 live. `slab`: coefficients of the tomogram blocks.
All inputs are finite; a program needn't handle non-finite values.
Results may differ from the reference program's by a relative error of at most 0.0036.
Values may be sent and summed in bfloat16 or wider, within the bound.
No kernel may reach another device: no remote copies, remote signals or barrier semaphores. Data moves between devices by JAX's collectives and lax.ppermute only.
A program may use at most 128 MiB of HBM per device.

```python
import math
import jax
import jax.numpy as jnp
import numpy as np
from jax import lax

V = 32768
REFS = 192
MASKS = 8
SLOTS = 64
CAP = 32
TOTAL = 2048
N_GRP = 8
N_BLK = 4
DEVICES = 32


def base_refs(key):
    amplitude = jnp.exp(jax.random.uniform(jax.random.fold_in(key, 11), (REFS, 1), jnp.float32, math.log(0.5), math.log(2.0)))
    return jax.random.normal(jax.random.fold_in(key, 12), (REFS, V), jnp.float32) * amplitude


def draw_references(key, part):
    return base_refs(key).astype(jnp.bfloat16)


def draw_slab(key, part):
    return (32.0 * jax.random.normal(jax.random.fold_in(key, 24), (TOTAL, V), jnp.float32)).astype(jnp.bfloat16)


def draw_live_count(key, part):
    counts = jax.random.randint(jax.random.fold_in(key, 31), (DEVICES,), SLOTS // 4, SLOTS + 1)
    full_device = jax.random.randint(jax.random.fold_in(key, 32), (), 0, DEVICES)
    device_ids = jnp.arange(DEVICES, dtype=jnp.int32)
    return jnp.where(device_ids == full_device, SLOTS, counts).astype(jnp.int32)


def plant(values, key, low, top_value):
    shape = values.shape
    spot = [jax.random.randint(jax.random.fold_in(key, axis), (), 0, shape[axis]) for axis in range(len(shape))]
    values = values.at[tuple(spot)].set(low)
    longest = shape.index(max(shape))
    spot[longest] = (spot[longest] + 1) % shape[longest]
    return values.at[tuple(spot)].set(top_value)


def routed_block(own_key, own, number, rows, count, top, bound, skew):
    sequence = jax.random.permutation(own_key, count)
    heavy_load, common = portions_of(count, rows * top, bound, skew, True), portions_of(count, rows * top, bound, skew, False)
    places = jnp.arange(count)

    def named(tallies, turn):
        used = int((tallies > 0).sum())
        fixed = max(1, used // 4)
        passed = fixed + (places - fixed + turn * (used - fixed)) % max(1, count - fixed)
        return jnp.zeros((count,), jnp.int32).at[sequence[jnp.where(places < fixed, places, passed)]].set(jnp.asarray(tallies, jnp.int32))

    tallies = jnp.where(number % 4 == 0, named(heavy_load, number // 4), named(common, number - number // 4 - 1))
    mixed = jax.random.permutation(jax.random.fold_in(own, 3), count)
    source_of, receiver = mixed[0:count // 2 * 2:2], mixed[1:count // 2 * 2:2]
    room = jnp.minimum(tallies[source_of] - 1, bound - tallies[receiver]) // 2
    room = jnp.where((source_of == sequence[0]) | (receiver == sequence[0]) | (tallies[receiver] == 0), 0, jnp.maximum(room, 0))
    passed = jax.random.randint(jax.random.fold_in(own, 4), (count // 2,), 0, 1 << 20) % (room + 1)
    tallies = tallies.at[source_of].add(-passed).at[receiver].add(passed)
    items = jnp.searchsorted(jnp.cumsum(tallies), jnp.arange(rows * top), side="right").astype(jnp.int32)
    table = items.reshape(top, rows).T
    table = table[jax.random.permutation(jax.random.fold_in(own, 1), rows)]
    turn = jax.random.randint(jax.random.fold_in(own, 2), (rows, 1), 0, top)
    return jnp.take_along_axis(table, (jnp.arange(top)[None, :] + turn) % top, axis=1)


def portions_of(amount, total, bound, slope, full):
    loads = [(1 << 20) // math.isqrt(rank ** slope) + 1 for rank in range(1, amount + 1)]
    largest = bound if full else min(bound, max(-(-total // amount), total * loads[0] // sum(loads)))
    least = 1 if total - largest >= amount - 1 else 0
    holding, spare = [largest] + [least] * (amount - 1), total - largest - least * (amount - 1)
    while spare > 0:
        free = [i for i in range(1, amount) if holding[i] < largest] or [i for i in range(1, amount) if holding[i] < bound]
        whole, left = sum([loads[i] for i in free]), spare
        for i in free:
            extra = min(bound - holding[i], max(1, left * loads[i] // whole), spare)
            holding[i] = holding[i] + extra
            spare = spare - extra
    return np.array(holding)


def setup_inputs(seed: int = 0) -> dict:
    arg_keys = jax.random.split(jax.random.key(seed), 8)
    slab = draw_slab(jax.random.fold_in(arg_keys[7], 71), 0)
    pick_owner_keys = jax.random.split(jax.random.fold_in(arg_keys[1], 1), TOTAL // SLOTS)
    pick_owner_turns = jax.random.permutation(jax.random.fold_in(arg_keys[1], 3), TOTAL // SLOTS)
    pick_owner = jax.vmap(lambda own, number: routed_block(jax.random.fold_in(arg_keys[1], 2), own, number, SLOTS, N_BLK, 1, CAP, 2))(pick_owner_keys, pick_owner_turns).reshape((TOTAL, 1))
    pick_offset = plant(jax.random.randint(arg_keys[2], (TOTAL,), 0, SLOTS), jax.random.fold_in(arg_keys[2], 1), 0, SLOTS - 1).astype(jnp.int32)
    wedge_id = plant(jax.random.randint(arg_keys[3], (TOTAL,), 0, MASKS), jax.random.fold_in(arg_keys[3], 1), 0, MASKS - 1).astype(jnp.int32)
    live_count = draw_live_count(jax.random.fold_in(arg_keys[7], 71), 0)
    references = draw_references(jax.random.fold_in(arg_keys[7], 71), 0)
    wedge = jnp.clip(jnp.exp(jax.random.uniform(arg_keys[6], (MASKS, V), jnp.float32, math.log(0.05), math.log(1.0))), 0.05, 1.0)
    return {"slab": slab, "pick_owner": pick_owner, "pick_offset": pick_offset, "wedge_id": wedge_id, "live_count": live_count, "references": references, "wedge": wedge}


def reference(slab, pick_owner, pick_offset, wedge_id, live_count, references, wedge):
    highest = lax.Precision.HIGHEST
    refs_float = references.astype(jnp.float32)
    wedge_norms = jnp.dot(wedge, (refs_float * refs_float).T, precision=highest)
    inv_noise = 1.0 / (32.0 * math.sqrt(V))
    owners_all = pick_owner[:, 0]
    slot_ids = jnp.arange(SLOTS, dtype=jnp.int32)
    table_ids = jnp.arange(MASKS, dtype=jnp.int32)

    def one_device(carry, device):
        accum, totals = carry
        first = (device * SLOTS).astype(jnp.int32)
        owners = lax.dynamic_slice_in_dim(owners_all, first, SLOTS)
        offsets = lax.dynamic_slice_in_dim(pick_offset, first, SLOTS)
        tables = lax.dynamic_slice_in_dim(wedge_id, first, SLOTS)
        group = device // N_BLK
        rows_index = ((group * N_BLK + owners) * SLOTS + offsets).astype(jnp.int32)
        blocks = jnp.take(slab, rows_index, axis=0)
        masks_hot = (tables[:, None] == table_ids[None, :]).astype(jnp.float32)
        weights = jnp.dot(masks_hot, wedge, precision=highest)
        scaled = (weights * blocks.astype(jnp.float32)).astype(jnp.bfloat16)
        correl = jnp.dot(scaled, references.T, preferred_element_type=jnp.float32)
        chosen_norms = jnp.dot(masks_hot, wedge_norms, precision=highest)
        scores = (correl - 0.5 * chosen_norms) * inv_noise
        posterior = jax.nn.softmax(scores, axis=1)
        live_mask = (slot_ids < live_count[device]).astype(jnp.float32)
        weighted = posterior * live_mask[:, None]
        weighted_b = weighted.astype(jnp.bfloat16)
        accum = accum + jnp.dot(weighted_b.T, scaled, preferred_element_type=jnp.float32)
        totals = totals + jnp.dot(weighted.T, masks_hot, precision=highest)
        return ((accum, totals), None)
    start = (jnp.zeros((REFS, V), jnp.float32), jnp.zeros((REFS, MASKS), jnp.float32))
    (accum, totals), _ = lax.scan(one_device, start, jnp.arange(N_GRP * N_BLK, dtype=jnp.int32))
    weight_sum = jnp.dot(totals, wedge, precision=highest)
    return accum / (weight_sum + 1.0)
```

```python
import functools
import math

import jax
import jax.numpy as jnp
from jax import lax
from jax.experimental import pallas as pl
from jax.experimental.pallas import tpu as pltpu
from jax.sharding import PartitionSpec as P

F32 = jnp.float32
BF16 = jnp.bfloat16
ROWS = (((1,), (0,)), ((), ()))
LANES = (((1,), (1,)), ((), ()))


def dot(left, right, dims=ROWS):
    return lax.dot_general(left, right, dims, preferred_element_type=F32)


def pieces_of(value, count):
    parts = []
    for _ in range(count):
        part = value.astype(BF16)
        value = value - part.astype(F32)
        parts.append(part)
    return parts


def iota(shape, axis):
    return lax.broadcasted_iota(jnp.int32, shape, axis).astype(F32)


def correl_kernel(blocks, seeded, place, slab, mate, wedge, *rest):
    refs, rest = rest[:blocks], rest[blocks:]
    seeds, rest = (rest[:3], rest[3:]) if seeded else ((), rest)
    own, other, norms, scaled, table = rest
    masks, rows, count = own.shape
    per_ref = count // blocks

    @pl.when(pl.program_id(0) == 0)
    def _():
        for i, target in enumerate((own, other, norms)):
            target[...] = seeds[i][...] if seeded else jnp.zeros_like(target)

    for p in range(blocks):
        if per_ref % 16 == 0:
            first = pl.multiple_of(place[1 + p] * per_ref, 16)
        else:
            first = p * per_ref
        table[pl.ds(first, per_ref), :] = refs[p][...]
    weights = wedge[...]
    for side, source in enumerate((slab, mate)):
        values = source[...].astype(F32)
        for w in range(masks):
            first = (side * masks + w) * rows
            scaled[first : first + rows, :] = (weights[w : w + 1, :] * values).astype(BF16)
    every = table[...]
    got = dot(scaled[...], every, LANES)
    for side, target in enumerate((own, other)):
        for w in range(masks):
            first = (side * masks + w) * rows
            target[w] += got[first : first + rows, :]
    wide = every.astype(F32)
    high, low = pieces_of(wide * wide, 2)
    lined = jnp.concatenate(pieces_of(weights, 3), axis=0)
    sums = dot(lined, high, LANES) + dot(lined, low, LANES)
    norms[...] += sums[:masks] + sums[masks : 2 * masks] + sums[2 * masks :]


def correl(place, slab, mate, wedge, refs, begin, tile, seeds):
    blocks = len(refs)
    rows, voxels = slab.shape
    masks = wedge.shape[0]
    per_ref = refs[0].shape[0]
    count = blocks * per_ref
    half = voxels // 2
    span = half // 2
    steps = span // tile
    shift = begin // tile

    def local(t, s):
        return (0, s[0] * (half // tile) + shift + t)

    in_specs = [
        pl.BlockSpec((rows, tile), local),
        pl.BlockSpec((rows, tile), lambda t, s: (0, shift + t)),
        pl.BlockSpec((masks, tile), local),
    ]
    for ref in refs:
        whole = ref.shape[1] == voxels
        in_specs.append(
            pl.BlockSpec((per_ref, tile), local if whole else (lambda t, s: (0, t)))
        )
    fixed3 = pl.BlockSpec((masks, rows, count), lambda t, s: (0, 0, 0))
    fixed2 = pl.BlockSpec((masks, count), lambda t, s: (0, 0))
    outs = [fixed3, fixed3, fixed2]
    if seeds:
        in_specs += outs
    return pl.pallas_call(
        functools.partial(correl_kernel, blocks, bool(seeds)),
        grid_spec=pltpu.PrefetchScalarGridSpec(
            num_scalar_prefetch=1,
            grid=(steps,),
            in_specs=in_specs,
            out_specs=outs,
            scratch_shapes=[
                pltpu.VMEM((2 * masks * rows, tile), BF16),
                pltpu.VMEM((count, tile), BF16),
            ],
        ),
        out_shape=[
            jax.ShapeDtypeStruct((masks, rows, count), F32),
            jax.ShapeDtypeStruct((masks, rows, count), F32),
            jax.ShapeDtypeStruct((masks, count), F32),
        ],
        cost_estimate=pl.CostEstimate(
            flops=2 * 2 * masks * rows * count * span,
            bytes_accessed=2 * span * (2 * rows + count + 2 * masks),
            transcendentals=0,
        ),
        name="correl",
    )(place, slab, mate, wedge, *refs, *seeds)


def weigh_kernel(scale, cap, place, own, got, own_norms, got_norms, meta, out, post):
    masks, rows, count = own.shape
    slots = meta.shape[1]
    info = meta[...].astype(F32)
    named = jnp.logical_and(info[0:1] == place[0].astype(F32), info[3:4] > 0.0)
    chosen = named.astype(F32)
    earlier = (iota((slots, slots), 0) < iota((slots, slots), 1)).astype(BF16)
    eight = jnp.broadcast_to(chosen, (8, slots)).astype(BF16)
    rank = dot(eight, earlier)[0:1]
    hit = jnp.logical_and(iota((cap, slots), 0) == rank, named)
    order = hit.astype(F32).astype(BF16)
    offset, wedge_id = info[1:2], info[2:3]
    listed = jnp.concatenate(
        [offset * chosen, wedge_id * chosen, chosen, jnp.zeros((5, slots), F32)], axis=0
    )
    columns = dot(order, listed.astype(BF16), LANES)
    slot_row, slot_wedge, slot_live = columns[:, 0:1], columns[:, 1:2], columns[:, 2:3]
    at = slot_wedge * rows + slot_row
    pick = jnp.logical_and(iota((cap, masks * rows), 1) == at, slot_live > 0.0)
    row_hot = jnp.logical_and(iota((rows, slots), 0) == offset, named).astype(F32).astype(BF16)
    wedge_hot = (iota((masks, slots), 0) == wedge_id).astype(F32).astype(BF16)
    tally = dot(row_hot, wedge_hot, LANES)
    norms = own_norms[...] + got_norms[...]
    mass = []
    for w in range(masks):
        score = (own[w] + got[w] - 0.5 * norms[w : w + 1]) * scale
        score = jnp.exp(score - jnp.max(score, axis=1, keepdims=True))
        share = score / jnp.sum(score, axis=1, keepdims=True)
        post[w * rows : (w + 1) * rows, :] = share.astype(BF16)
        mass.append(jnp.sum(share * tally[:, w : w + 1], axis=0, keepdims=True))
    out[...] = jnp.zeros_like(out)
    out[:cap, :count] = dot(pick.astype(F32).astype(BF16), post[...]).astype(BF16)
    left = out.shape[1] - count
    lane = iota((cap, left), 1)
    tail = jnp.where(lane == 0.0, slot_row, jnp.where(lane == 1.0, slot_wedge, 0.0))
    out[:cap, count:] = tail.astype(BF16)
    for i, part in enumerate(pieces_of(jnp.concatenate(mass, axis=0), 3)):
        out[cap + i * masks : cap + (i + 1) * masks, :count] = part


def weigh(place, own, got, own_norms, got_norms, meta, scale, cap, height, width):
    masks, rows, count = own.shape
    memory = [pl.BlockSpec(memory_space=pltpu.SMEM)] + [pl.BlockSpec(memory_space=pltpu.VMEM)] * 5
    return pl.pallas_call(
        functools.partial(weigh_kernel, scale, cap),
        in_specs=memory,
        out_specs=pl.BlockSpec(memory_space=pltpu.VMEM),
        out_shape=jax.ShapeDtypeStruct((height, width), BF16),
        scratch_shapes=[pltpu.VMEM((masks * rows, count), BF16)],
        cost_estimate=pl.CostEstimate(
            flops=masks * rows * count * 300, bytes_accessed=1 << 20, transcendentals=0
        ),
        name="weigh",
    )(place, own, got, own_norms, got_norms, meta)


def gather_kernel(cap, count, place, slab, weights, wedge, out, rows_hot, wedge_hot, turned, scaled):
    groups = weights.shape[0]
    rows = slab.shape[0] // groups
    masks = wedge.shape[0]

    @pl.when(pl.program_id(0) == 0)
    def _():
        for g in range(groups):
            tail = weights[g, :cap, count : count + 2].astype(F32)
            rows_hot[g] = (iota((cap, rows), 1) == tail[:, 0:1]).astype(F32).astype(BF16)
            hot = (iota((cap, masks), 1) == tail[:, 1:2]).astype(F32)
            wedge_hot[g] = jnp.concatenate([hot] * 3, axis=1).astype(BF16)
            turned[:, g * cap : (g + 1) * cap] = (
                weights[g, :cap, :count].astype(F32).T.astype(BF16)
            )

    lined = jnp.concatenate(pieces_of(wedge[...], 3), axis=0)
    for g in range(groups):
        values = dot(rows_hot[g], slab[g * rows : (g + 1) * rows, :])
        scaled[g * cap : (g + 1) * cap, :] = (dot(wedge_hot[g], lined) * values).astype(BF16)
    sums = dot(turned[...], scaled[...]).astype(BF16)
    per_ref = out.shape[1]
    for p in range(out.shape[0]):
        out[p] = sums[p * per_ref : (p + 1) * per_ref, :]


def gather(place, slab, weights, wedge, cap, blocks, count, tile):
    groups, height, width = weights.shape
    total, span = slab.shape
    masks = wedge.shape[0]
    per_ref = count // blocks
    steps = span // tile
    return pl.pallas_call(
        functools.partial(gather_kernel, cap, count),
        grid_spec=pltpu.PrefetchScalarGridSpec(
            num_scalar_prefetch=1,
            grid=(steps,),
            in_specs=[
                pl.BlockSpec((total, tile), lambda t, s: (0, t)),
                pl.BlockSpec((groups, height, width), lambda t, s: (0, 0, 0)),
                pl.BlockSpec((masks, tile), lambda t, s: (0, s[0] * steps + t)),
            ],
            out_specs=pl.BlockSpec((blocks, per_ref, tile), lambda t, s: (0, 0, t)),
            scratch_shapes=[
                pltpu.VMEM((groups, cap, total // groups), BF16),
                pltpu.VMEM((groups, cap, 3 * masks), BF16),
                pltpu.VMEM((count, groups * cap), BF16),
                pltpu.VMEM((groups * cap, tile), BF16),
            ],
        ),
        out_shape=jax.ShapeDtypeStruct((blocks, per_ref, span), BF16),
        cost_estimate=pl.CostEstimate(
            flops=6 * groups * cap * count * span,
            bytes_accessed=2 * span * (total + count),
            transcendentals=0,
        ),
        name="gather",
    )(place, slab, weights, wedge)


def spread(value, axis):
    size = lax.axis_size(axis)
    copies = jnp.broadcast_to(value[None], (size, *value.shape))
    return lax.all_to_all(copies, axis, split_axis=0, concat_axis=0, tiled=True)


def per_device(slab, pick_owner, pick_offset, wedge_id, live_count, references, wedge):
    slot_count, voxels = slab.shape
    masks = wedge.shape[0]
    per_ref = references.shape[0]
    groups = lax.axis_size("grp")
    blocks = lax.axis_size("blk")
    count = per_ref * blocks
    per_vox = voxels // groups
    half = voxels // 2
    span = half // 2
    cap = 2 * slot_count
    height = -(-(cap + 3 * masks) // 16) * 16
    width = -(-(count + 2) // 128) * 128
    group = lax.axis_index("grp")
    block = lax.axis_index("blk")
    core = group % 2
    swap = [(g, g ^ 1) for g in range(groups)]

    columns = lax.all_to_all(slab, "grp", split_axis=1, concat_axis=0, tiled=True)

    live = (jnp.arange(slot_count, dtype=jnp.int32) < live_count[0]).astype(jnp.int32)
    mine = jnp.stack([pick_owner[:, 0], pick_offset, wedge_id, live])
    meta = spread(mine, "blk").transpose(1, 0, 2).reshape(4, blocks * slot_count)

    mate = lax.ppermute(lax.dynamic_slice_in_dim(slab, (1 - core) * half, half, 1), "grp", swap)
    stretches = [
        lax.dynamic_slice_in_dim(references, core * half + i * span, span, 1) for i in range(2)
    ]
    if blocks == 4:
        near = [[(b, b ^ 1) for b in range(4)], [(b, b ^ 2) for b in range(4)]]
        sides = [[lax.ppermute(s, "blk", near[i]) for i in range(2)] for s in stretches]
        across = [
            lax.ppermute(sides[0][0], "blk", near[1]),
            lax.ppermute(sides[1][1], "blk", near[0]),
        ]
        tables = [[references, *sides[i], across[i]] for i in range(2)]
        order = [block ^ p for p in range(4)]
    else:
        tables = []
        for s in stretches:
            everyone = spread(s, "blk")
            tables.append([everyone[p] for p in range(blocks)])
        order = [jnp.int32(p) for p in range(blocks)]
    place = jnp.stack([core, *order]).astype(jnp.int32)
    tile = min(1024, span)
    sums = ()
    for i in range(2):
        sums = correl(place, slab, mate, wedge, tables[i], i * span, tile, sums)
    own, other, norms = sums
    got = lax.ppermute(other, "grp", swap)
    got_norms = lax.ppermute(norms, "grp", swap)
    scale = 1.0 / (32.0 * math.sqrt(voxels))
    weights = weigh(
        block.reshape(1).astype(jnp.int32), own, got, norms, got_norms, meta, scale, cap, height, width
    )
    everyone = spread(weights, "grp")

    mass = everyone[:, cap : cap + 3 * masks, :count].astype(F32)
    mass = mass.reshape(groups * 3, masks, blocks, per_ref).sum(0).transpose(1, 0, 2)
    mass = lax.all_to_all(mass, "blk", split_axis=0, concat_axis=0, tiled=True).sum(0)

    shares = gather(
        group.reshape(1).astype(jnp.int32), columns, everyone, wedge, cap, blocks, count, min(512, per_vox)
    )
    shares = lax.all_to_all(shares, "blk", split_axis=0, concat_axis=0, tiled=True)
    summed = shares.astype(F32).sum(0)
    wedge_cols = lax.dynamic_slice_in_dim(wedge, group * per_vox, per_vox, 1)
    weight_sum = jnp.dot(mass.T, wedge_cols, precision=lax.Precision.HIGHEST)
    return summed / (weight_sum + 1.0)


def solution(mesh):
    placed = (
        P(("grp", "blk"), None),
        P(("grp", "blk"), None),
        P(("grp", "blk")),
        P(("grp", "blk")),
        P(("grp", "blk")),
        P("blk", None),
        P(),
    )
    return jax.shard_map(
        per_device, mesh=mesh, in_specs=placed, out_specs=P("blk", "grp"), check_vma=False
    )
```

```python
import functools
import math

import jax
import jax.numpy as jnp
from jax import lax
from jax.experimental import pallas as pl
from jax.experimental.pallas import tpu as pltpu
from jax.sharding import Mesh
from jax.sharding import PartitionSpec as P

F32 = jnp.float32
BF16 = jnp.bfloat16
ROWS = (((1,), (0,)), ((), ()))
LANES = (((1,), (1,)), ((), ()))
VMEM = pl.BlockSpec(memory_space=pltpu.VMEM)
SMEM = pl.BlockSpec(memory_space=pltpu.SMEM)
SPLIT = 4


def dot(left, right, dims=ROWS):
    return lax.dot_general(left, right, dims, preferred_element_type=F32)


def pieces_of(value, count):
    parts = []
    for _ in range(count):
        part = value.astype(BF16)
        value = value - part.astype(F32)
        parts.append(part)
    return parts


def iota(shape, axis):
    return lax.broadcasted_iota(jnp.int32, shape, axis).astype(F32)


def hot(mask):
    return mask.astype(F32).astype(BF16)


def cost(flops, moved):
    return pl.CostEstimate(flops=int(flops), bytes_accessed=int(moved), transcendentals=0)


def cut_kernel(place, source, out):
    out[...] = source[...]


def cut(place, source, begin, count, per_vox):
    rows = source.shape[0]
    return pl.pallas_call(
        cut_kernel,
        grid_spec=pltpu.PrefetchScalarGridSpec(
            num_scalar_prefetch=1,
            grid=(count,),
            in_specs=[pl.BlockSpec((rows, per_vox), lambda t, s: (0, 2 * (begin + t) + s[0]))],
            out_specs=pl.BlockSpec((rows, per_vox), lambda t, s: (0, t)),
        ),
        out_shape=jax.ShapeDtypeStruct((rows, count * per_vox), source.dtype),
        cost_estimate=cost(0, 4 * rows * count * per_vox),
        name="cut",
    )(place, source)


def deal_kernel(place, source, *outs):
    for p, out in enumerate(outs):

        @pl.when(pl.program_id(0) == p)
        def _(out=out):
            out[...] = source[:, : out.shape[1]]


def deal(place, slab, groups, keep):
    rows, voxels = slab.shape
    return pl.pallas_call(
        deal_kernel,
        grid_spec=pltpu.PrefetchScalarGridSpec(
            num_scalar_prefetch=1,
            grid=(groups,),
            in_specs=[pl.BlockSpec((rows, voxels // groups), lambda t, s: (0, s[1] ^ t))],
            out_specs=[pl.BlockSpec((rows, keep), lambda t, s: (0, 0))] * groups,
        ),
        out_shape=[jax.ShapeDtypeStruct((rows, keep), slab.dtype)] * groups,
        cost_estimate=cost(0, 4 * rows * groups * keep),
        name="deal",
    )(place, slab)


def lists_kernel(place, meta, out):
    cap = out.shape[1]
    slots = meta.shape[1]
    info = meta[...].astype(F32)
    named = jnp.logical_and(info[0:1] == place[0].astype(F32), info[3:4] > 0.0)
    chosen = named.astype(F32)
    earlier = hot(iota((slots, slots), 0) < iota((slots, slots), 1))
    rank = dot(jnp.broadcast_to(chosen, (8, slots)).astype(BF16), earlier)[0:1]
    order = hot(jnp.logical_and(iota((cap, slots), 0) == rank, named))
    listed = jnp.concatenate(
        [info[1:2] * chosen, info[2:3] * chosen, chosen, jnp.zeros((5, slots), F32)], axis=0
    )
    out[...] = dot(listed.astype(BF16), order, LANES)


def lists_of(place, meta, cap):
    return pl.pallas_call(
        lists_kernel,
        in_specs=[SMEM, VMEM],
        out_specs=VMEM,
        out_shape=jax.ShapeDtypeStruct((8, cap), F32),
        cost_estimate=cost(1 << 22, 1 << 18),
        name="lists",
    )(place, meta)


def columns_of(listed):
    cap = listed.shape[1]
    eye = hot(iota((cap, cap), 0) == iota((cap, cap), 1))
    return dot(eye, listed.astype(BF16), LANES)


def select_kernel(sources, place, *rest):
    blocks, (listed, wedge, out, rows_hot, wedge_hot) = rest[:sources], rest[sources:]
    lists, cap, rows = rows_hot.shape
    masks = wedge.shape[0]

    @pl.when(pl.program_id(0) == 0)
    def _():
        for g in range(lists):
            columns = columns_of(listed[g])
            rows_hot[g] = hot(iota((cap, rows), 1) == columns[:, 0:1])
            marks = (iota((cap, masks), 1) == columns[:, 1:2]).astype(F32)
            wedge_hot[g] = jnp.concatenate([marks] * 3, axis=1).astype(BF16)

    lined = jnp.concatenate(pieces_of(wedge[...], 3), axis=0)
    for g in range(lists):
        values = dot(rows_hot[g], blocks[g][...])
        out[g * cap : (g + 1) * cap, :] = (dot(wedge_hot[g], lined) * values).astype(BF16)


def select(place, blocks, block_specs, listed, wedge, wedge_spec, rows, tile, steps):
    lists, _, cap = listed.shape
    masks = wedge.shape[0]
    return pl.pallas_call(
        functools.partial(select_kernel, len(blocks)),
        grid_spec=pltpu.PrefetchScalarGridSpec(
            num_scalar_prefetch=1,
            grid=(steps,),
            in_specs=[
                *block_specs,
                pl.BlockSpec((lists, 8, cap), lambda t, s: (0, 0, 0)),
                wedge_spec,
            ],
            out_specs=pl.BlockSpec((lists * cap, tile), lambda t, s: (0, t)),
            scratch_shapes=[
                pltpu.VMEM((lists, cap, rows), BF16),
                pltpu.VMEM((lists, cap, 3 * masks), BF16),
            ],
        ),
        out_shape=jax.ShapeDtypeStruct((lists * cap, steps * tile), BF16),
        cost_estimate=cost(
            4 * lists * cap * 256 * steps * tile, 2 * lists * (cap + rows) * steps * tile
        ),
        name="select",
    )(place, *blocks, listed, wedge)


def correl_kernel(blocks, seeded, place, scaled, wedge, *rest):
    refs, rest = rest[:blocks], rest[blocks:]
    seeds, rest = (rest[:3], rest[3:]) if seeded else ((), rest)
    own, other, norms, table = rest
    cap, count = own.shape
    masks = wedge.shape[0]
    per_ref = count // blocks

    @pl.when(pl.program_id(0) == 0)
    def _():
        for i, target in enumerate((own, other, norms)):
            target[...] = seeds[i][...] if seeded else jnp.zeros_like(target)

    for p in range(blocks):
        table[p * per_ref : (p + 1) * per_ref, :] = refs[p][...]
    every = table[...]
    got = dot(scaled[...], every, LANES)
    own[...] += got[:cap]
    other[...] += got[cap:]
    wide = every.astype(F32)
    high, low = pieces_of(wide * wide, 2)
    lined = jnp.concatenate(pieces_of(wedge[...], 3), axis=0)
    sums = dot(lined, high, LANES) + dot(lined, low, LANES)
    norms[...] += sums[:masks] + sums[masks : 2 * masks] + sums[2 * masks :]


def correl(place, scaled, wedge, wedge_spec, refs, shift, tile, steps, seeds):
    blocks = len(refs)
    cap = scaled.shape[0] // 2
    masks = wedge.shape[0]
    per_ref = refs[0].shape[0]
    count = blocks * per_ref
    in_specs = [pl.BlockSpec((2 * cap, tile), lambda t, s: (0, shift + t)), wedge_spec]
    in_specs += [pl.BlockSpec((per_ref, tile), lambda t, s: (0, t))] * blocks
    shapes = [(cap, count), (cap, count), (masks, count)]
    outs = [pl.BlockSpec(shape, lambda t, s: (0, 0)) for shape in shapes]
    if seeds:
        in_specs += outs
    return pl.pallas_call(
        functools.partial(correl_kernel, blocks, bool(seeds)),
        grid_spec=pltpu.PrefetchScalarGridSpec(
            num_scalar_prefetch=1,
            grid=(steps,),
            in_specs=in_specs,
            out_specs=outs,
            scratch_shapes=[pltpu.VMEM((count, tile), BF16)],
        ),
        out_shape=[jax.ShapeDtypeStruct(shape, F32) for shape in shapes],
        cost_estimate=cost(
            8 * cap * count * steps * tile, 2 * steps * tile * (2 * cap + count + 2 * masks)
        ),
        name="correl",
    )(place, scaled, wedge, *refs, *seeds)


def weigh_kernel(scale, masks, own, got, own_norms, got_norms, listed, out):
    cap = own.shape[0]
    columns = columns_of(listed[...])
    marks = (iota((cap, masks), 1) == columns[:, 1:2]).astype(F32)
    wedge_hot = jnp.concatenate([marks] * 3, axis=1).astype(BF16)
    norms = jnp.concatenate(pieces_of(own_norms[...] + got_norms[...], 3), axis=0)
    score = (own[...] + got[...] - 0.5 * dot(wedge_hot, norms)) * scale
    score = jnp.exp(score - jnp.max(score, axis=1, keepdims=True))
    share = score / jnp.sum(score, axis=1, keepdims=True) * columns[:, 2:3]
    out[...] = share.T.astype(BF16)


def weigh(own, got, own_norms, got_norms, listed, scale):
    cap, count = own.shape
    return pl.pallas_call(
        functools.partial(weigh_kernel, scale, own_norms.shape[0]),
        in_specs=[VMEM] * 5,
        out_specs=VMEM,
        out_shape=jax.ShapeDtypeStruct((count, cap), BF16),
        cost_estimate=cost(1 << 24, 1 << 18),
        name="weigh",
    )(own, got, own_norms, got_norms, listed)


def blend_kernel(lists, blocks, masks, place, *rest):
    weights, rest = rest[:lists], rest[lists:]
    listed, scaled, rest = rest[0], rest[1], rest[2:]
    outs, masses, turned = rest[:blocks], rest[blocks:-1], rest[-1]
    cap = weights[0].shape[1]
    per_ref = outs[0].shape[-2]

    @pl.when(pl.program_id(0) == 0)
    def _():
        for g in range(lists):
            turned[:, g * cap : (g + 1) * cap] = weights[g][...]
        for p, mass in enumerate(masses):
            total = jnp.zeros(mass.shape, F32)
            for g in range(lists):
                marks = hot(iota((masks, cap), 0) == listed[g, 1:2, :])
                total = total + dot(weights[g][p * per_ref : (p + 1) * per_ref, :], marks, LANES)
            mass[...] = total

    sums = dot(turned[...], scaled[...]).astype(BF16)
    for p, out in enumerate(outs):
        out[...] = sums[p * per_ref : (p + 1) * per_ref, :].reshape(out.shape)


def blend(place, weights, listed, scaled, masks, blocks, tile, steps, index, deep):
    lists = len(weights)
    count, cap = weights[0].shape
    per_ref = count // blocks
    if deep:
        shape = (steps, per_ref, tile)
        spec = pl.BlockSpec((1, per_ref, tile), lambda t, s: (t, 0, 0))
        masses = 0
    else:
        shape = (per_ref, steps * tile)
        spec = pl.BlockSpec((per_ref, tile), lambda t, s: (0, t))
        masses = blocks
    return pl.pallas_call(
        functools.partial(blend_kernel, lists, blocks, masks),
        grid_spec=pltpu.PrefetchScalarGridSpec(
            num_scalar_prefetch=1,
            grid=(steps,),
            in_specs=[pl.BlockSpec((count, cap), lambda t, s: (0, 0))] * lists
            + [
                pl.BlockSpec((lists, 8, cap), lambda t, s: (0, 0, 0)),
                pl.BlockSpec((lists * cap, tile), index),
            ],
            out_specs=[spec] * blocks
            + [pl.BlockSpec((per_ref, masks), lambda t, s: (0, 0))] * masses,
            scratch_shapes=[pltpu.VMEM((count, lists * cap), BF16)],
        ),
        out_shape=[jax.ShapeDtypeStruct(shape, BF16)] * blocks
        + [jax.ShapeDtypeStruct((per_ref, masks), F32)] * masses,
        cost_estimate=cost(
            2 * lists * cap * count * steps * tile, 2 * (lists * cap + count) * steps * tile
        ),
        name="blend",
    )(place, *weights, listed, scaled)


def fold_kernel(parts, *refs):
    sources, outs = refs[:parts], refs[parts:]
    for t, out in enumerate(outs):
        total = sources[0][t].astype(F32)
        for source in sources[1:]:
            total = total + source[t].astype(F32)
        out[...] = total.astype(BF16)


def fold(parts):
    layers, per_ref, tile = parts[0].shape
    return pl.pallas_call(
        functools.partial(fold_kernel, len(parts)),
        in_specs=[VMEM] * len(parts),
        out_specs=[VMEM] * layers,
        out_shape=[jax.ShapeDtypeStruct((per_ref, tile), BF16)] * layers,
        cost_estimate=cost(0, 2 * (len(parts) + 1) * layers * per_ref * tile),
        name="fold",
    )(*parts)


def finish_kernel(blocks, place, *rest):
    shares, masses, rest = rest[:blocks], rest[blocks : 2 * blocks], rest[2 * blocks :]
    apart, wedge, out = rest[:-2], rest[-2], rest[-1]
    mass = masses[0][...]
    for part in masses[1:]:
        mass = mass + part[...]
    below = jnp.ones(out.shape, F32)
    for w in range(wedge.shape[0]):
        below = below + mass[:, w : w + 1] * wedge[w : w + 1, :]

    def emit(parts):
        total = parts[0][...].astype(F32)
        for part in parts[1:]:
            total = total + part[...].astype(F32)
        out[...] = total / below

    last = pl.num_programs(0) - 1

    @pl.when(pl.program_id(0) < last)
    def _():
        emit(shares)

    @pl.when(pl.program_id(0) == last)
    def _():
        emit(apart)


def finish(place, shares, masses, apart, wedge, tile):
    per_ref = shares[0].shape[0]
    masks = wedge.shape[0]
    blocks = len(shares)
    return pl.pallas_call(
        functools.partial(finish_kernel, blocks),
        grid_spec=pltpu.PrefetchScalarGridSpec(
            num_scalar_prefetch=1,
            grid=(SPLIT,),
            in_specs=[pl.BlockSpec((per_ref, tile), lambda t, s: (0, jnp.minimum(t, SPLIT - 2)))]
            * blocks
            + [pl.BlockSpec((per_ref, masks), lambda t, s: (0, 0))] * blocks
            + [pl.BlockSpec((per_ref, tile), lambda t, s: (0, 0))] * len(apart)
            + [pl.BlockSpec((masks, tile), lambda t, s: (0, s[1] * SPLIT + t))],
            out_specs=pl.BlockSpec((per_ref, tile), lambda t, s: (0, t)),
        ),
        out_shape=jax.ShapeDtypeStruct((per_ref, SPLIT * tile), F32),
        cost_estimate=cost(0, 8 * per_ref * SPLIT * tile),
        name="finish",
    )(place, *shares, *masses, *apart, wedge)


GRP = ("lay", "core")


def passed(values, axis, size):
    return [values[0]] + [
        lax.ppermute(values[p], axis, [(d, d ^ p) for d in range(size)]) for p in range(1, size)
    ]


def per_device(slab, pick_owner, pick_offset, wedge_id, live_count, references, wedge):
    slot_count, voxels = slab.shape
    masks = wedge.shape[0]
    layers = lax.axis_size("lay")
    groups = 2 * layers
    blocks = lax.axis_size("blk")
    per_vox = voxels // groups
    tile = per_vox // SPLIT
    keep = per_vox - tile
    half_steps = voxels // 2 // tile
    cap = 2 * slot_count
    block = lax.axis_index("blk").astype(jnp.int32)
    core = lax.axis_index("core").astype(jnp.int32)
    layer = lax.axis_index("lay").astype(jnp.int32)
    place = jnp.stack([core, layer * 2 + core, layer, block])

    stretches = [cut(place[:1], references, i * layers // 2, layers // 2, per_vox) for i in range(2)]
    if blocks == 4:
        near = [[(b, b ^ 1) for b in range(4)], [(b, b ^ 2) for b in range(4)]]
        sides = [[lax.ppermute(stretches[0], "blk", near[i]) for i in range(2)]]
        sides += [[lax.ppermute(stretches[1], "blk", near[i]) for i in range(2)]]
        across = [
            lax.ppermute(sides[0][0], "blk", near[1]),
            lax.ppermute(sides[1][1], "blk", near[0]),
        ]
        tables = [[stretches[i], *sides[i], across[i]] for i in range(2)]
    else:
        tables = [passed([s] * blocks, "blk", blocks) for s in stretches]

    columns = passed(deal(place, slab, groups, keep), GRP, groups)
    live = (jnp.arange(slot_count, dtype=jnp.int32) < live_count[0]).astype(jnp.int32)
    mine = jnp.stack([pick_owner[:, 0], pick_offset, wedge_id, live])
    meta = jnp.concatenate(passed([mine] * blocks, "blk", blocks), axis=1)
    mate = lax.ppermute(
        cut(1 - place[:1], slab, 0, layers, per_vox), "core", [(0, 1), (1, 0)]
    )

    listed = lists_of(block.reshape(1), meta, cap)
    pair = jnp.stack(passed([listed] * 2, "core", 2))
    all_lists = jnp.concatenate(passed([pair] * layers, "lay", layers), axis=0)

    def local(t, s):
        return (0, (2 * (t // SPLIT) + s[0]) * SPLIT + t % SPLIT)

    scaled = select(
        place,
        [slab, mate],
        [
            pl.BlockSpec((slot_count, tile), local),
            pl.BlockSpec((slot_count, tile), lambda t, s: (0, t)),
        ],
        pair,
        wedge,
        pl.BlockSpec((masks, tile), local),
        slot_count,
        tile,
        half_steps,
    )
    sums = ()
    for i in range(2):
        shift = i * half_steps // 2
        spec = pl.BlockSpec((masks, tile), lambda t, s, shift=shift: local(shift + t, s))
        sums = correl(place, scaled, wedge, spec, tables[i], shift, tile, half_steps // 2, sums)
    own, other, norms = sums
    got = lax.ppermute(other, "core", [(0, 1), (1, 0)])
    got_norms = lax.ppermute(norms, "core", [(0, 1), (1, 0)])
    scale = 1.0 / (32.0 * math.sqrt(voxels))
    weights = weigh(own, got, norms, got_norms, listed, scale)
    all_weights = passed([weights] * groups, GRP, groups)

    chosen = select(
        place,
        columns,
        [pl.BlockSpec((slot_count, tile), lambda t, s: (0, t))] * groups,
        all_lists,
        wedge,
        pl.BlockSpec((masks, tile), lambda t, s: (0, s[1] * SPLIT + t)),
        slot_count,
        tile,
        SPLIT - 1,
    )

    apart = blend(
        place,
        all_weights[:2],
        pair,
        scaled,
        masks,
        blocks,
        tile,
        layers,
        lambda t, s: (0, (s[2] ^ t) * SPLIT + SPLIT - 1),
        True,
    )
    apart = passed(apart, "blk", blocks)
    apart = fold(apart)
    apart = passed(apart, "lay", layers)

    mixed = blend(
        place, all_weights, all_lists, chosen, masks, blocks, tile, SPLIT - 1,
        lambda t, s: (0, t), False,
    )
    shares = passed(mixed[:blocks], "blk", blocks)
    masses = passed(mixed[blocks:], "blk", blocks)
    return finish(place, shares, masses, apart, wedge, tile)


def solution(mesh):
    groups, blocks = mesh.shape["grp"], mesh.shape["blk"]
    fine = Mesh(mesh.devices.reshape(groups // 2, 2, blocks), ("lay", "core", "blk"))
    every = ("lay", "core", "blk")
    placed = (P(every, None), P(every, None), P(every), P(every), P(every), P("blk", None), P())

    return jax.shard_map(
        per_device, mesh=fine, in_specs=placed, out_specs=P("blk", GRP), check_vma=False
    )
```

```python
import functools
import math

import jax
import jax.numpy as jnp
from jax import lax
from jax.experimental import pallas as pl
from jax.experimental.pallas import tpu as pltpu
from jax.sharding import Mesh
from jax.sharding import PartitionSpec as P

F32 = jnp.float32
BF16 = jnp.bfloat16
ROWS = (((1,), (0,)), ((), ()))
LANES = (((1,), (1,)), ((), ()))
VMEM = pl.BlockSpec(memory_space=pltpu.VMEM)
SMEM = pl.BlockSpec(memory_space=pltpu.SMEM)
SPLIT = 4


def dot(left, right, dims=ROWS):
    return lax.dot_general(left, right, dims, preferred_element_type=F32)


def pieces_of(value, count):
    parts = []
    for _ in range(count):
        part = value.astype(BF16)
        value = value - part.astype(F32)
        parts.append(part)
    return parts


def iota(shape, axis):
    return lax.broadcasted_iota(jnp.int32, shape, axis).astype(F32)


def hot(mask):
    return mask.astype(F32).astype(BF16)


def cost(flops, moved):
    return pl.CostEstimate(flops=int(flops), bytes_accessed=int(moved), transcendentals=0)


def cut_kernel(place, refs, slab, *rest):
    outs, held, came, went = rest[:3], rest[3:6], rest[6], rest[7]
    layers, per_vox = held[2].shape[0], held[2].shape[2]
    core = place[0]

    def start(which):
        source, side = (slab, 1 - core) if which == 2 else (refs, core)
        first = layers // 2 if which == 1 else 0
        copies = []
        for z in range(held[which].shape[0]):
            at = pl.multiple_of((2 * (first + z) + side) * per_vox, per_vox)
            copy = pltpu.make_async_copy(
                source.at[:, pl.ds(at, per_vox)], held[which].at[z], came.at[which, z]
            )
            copy.start()
            copies.append(copy)
        return copies

    coming = [start(which) for which in range(3)]
    going = []
    for which in range(3):
        for z, copy in enumerate(coming[which]):
            copy.wait()
            leave = pltpu.make_async_copy(
                held[which].at[z],
                outs[which].at[:, pl.ds(z * per_vox, per_vox)],
                went.at[which, z],
            )
            leave.start()
            going.append(leave)
    for leave in going:
        leave.wait()


def cut(place, refs, slab, layers, per_vox):
    anywhere = pl.BlockSpec(memory_space=pl.ANY)
    shapes = [
        (layers // 2, refs.shape[0]),
        (layers // 2, refs.shape[0]),
        (layers, slab.shape[0]),
    ]
    return pl.pallas_call(
        cut_kernel,
        in_specs=[SMEM, anywhere, anywhere],
        out_specs=[anywhere] * 3,
        out_shape=[jax.ShapeDtypeStruct((r, n * per_vox), BF16) for n, r in shapes],
        scratch_shapes=[pltpu.VMEM((n, r, per_vox), BF16) for n, r in shapes]
        + [pltpu.SemaphoreType.DMA((3, layers))] * 2,
        cost_estimate=cost(0, 4 * sum(n * r for n, r in shapes) * per_vox),
        name="cut",
    )(place, refs, slab)


def deal_kernel(place, slab, *rest):
    peers = len(rest) - 3
    outs, held, came, went = rest[:peers], rest[peers], rest[peers + 1], rest[peers + 2]
    keep = held.shape[2]
    per_vox = slab.shape[1] // (peers + 1)
    coming = []
    for p in range(peers):
        at = pl.multiple_of((place[1] ^ (p + 1)) * per_vox, per_vox)
        copy = pltpu.make_async_copy(slab.at[:, pl.ds(at, keep)], held.at[p], came.at[p])
        copy.start()
        coming.append(copy)
    going = []
    for p in range(peers):
        coming[p].wait()
        leave = pltpu.make_async_copy(held.at[p], outs[p], went.at[p])
        leave.start()
        going.append(leave)
    for leave in going:
        leave.wait()


def deal(place, slab, groups, keep):
    rows = slab.shape[0]
    anywhere = pl.BlockSpec(memory_space=pl.ANY)
    peers = groups - 1
    return pl.pallas_call(
        deal_kernel,
        in_specs=[SMEM, anywhere],
        out_specs=[anywhere] * peers,
        out_shape=[jax.ShapeDtypeStruct((rows, keep), BF16)] * peers,
        scratch_shapes=[pltpu.VMEM((peers, rows, keep), BF16)]
        + [pltpu.SemaphoreType.DMA((peers,))] * 2,
        cost_estimate=cost(0, 4 * rows * peers * keep),
        name="deal",
    )(place, slab)


def lists_kernel(place, meta, out):
    cap = out.shape[1]
    slots = meta.shape[1]
    info = meta[...].astype(F32)
    named = jnp.logical_and(info[0:1] == place[0].astype(F32), info[3:4] > 0.0)
    chosen = named.astype(F32)
    earlier = hot(iota((slots, slots), 0) < iota((slots, slots), 1))
    rank = dot(jnp.broadcast_to(chosen, (8, slots)).astype(BF16), earlier)[0:1]
    order = hot(jnp.logical_and(iota((cap, slots), 0) == rank, named))
    listed = jnp.concatenate(
        [info[1:2] * chosen, info[2:3] * chosen, chosen, jnp.zeros((5, slots), F32)], axis=0
    )
    out[...] = dot(listed.astype(BF16), order, LANES)


def lists_of(place, meta, cap):
    return pl.pallas_call(
        lists_kernel,
        in_specs=[SMEM, VMEM],
        out_specs=VMEM,
        out_shape=jax.ShapeDtypeStruct((8, cap), F32),
        cost_estimate=cost(1 << 22, 1 << 18),
        name="lists",
    )(place, meta)


def columns_of(listed):
    cap = listed.shape[1]
    eye = hot(iota((cap, cap), 0) == iota((cap, cap), 1))
    return dot(eye, listed.astype(BF16), LANES)


def select_kernel(count, place, *rest):
    blocks, pairs, wedge, out = rest[:count], rest[count:-4], rest[-4], rest[-3]
    rows_hot, wedge_hot = rest[-2:]
    bunches, height, depth = rows_hot.shape
    cap = wedge_hot.shape[0] // count
    rows = blocks[0].shape[0]
    bunch = depth // rows
    masks = wedge.shape[0]

    @pl.when(pl.program_id(0) == 0)
    def _():
        rows_hot[...] = jnp.zeros_like(rows_hot)
        for g in range(count):
            columns = columns_of(pairs[g // 2][g % 2])
            n, at = g // bunch, g % bunch
            rows_hot[n, at * cap : (at + 1) * cap, at * rows : (at + 1) * rows] = hot(
                iota((cap, rows), 1) == columns[:, 0:1]
            )
            marks = (iota((cap, masks), 1) == columns[:, 1:2]).astype(F32)
            wedge_hot[g * cap : (g + 1) * cap, :] = jnp.concatenate([marks] * 3, axis=1).astype(
                BF16
            )

    lined = jnp.concatenate(pieces_of(wedge[...], 3), axis=0)
    weights = dot(wedge_hot[...], lined)
    for n in range(bunches):
        stack = [blocks[n * bunch + i][...] for i in range(bunch)]
        values = dot(rows_hot[n], jnp.concatenate(stack, axis=0))
        part = slice(n * height, (n + 1) * height)
        out[part, :] = (weights[part] * values).astype(BF16)


def select(place, blocks, block_specs, pairs, wedge, wedge_spec, rows, tile, steps):
    count = len(blocks)
    cap = pairs[0].shape[2]
    masks = wedge.shape[0]
    bunch = min(count, 256 // rows)
    return pl.pallas_call(
        functools.partial(select_kernel, count),
        grid_spec=pltpu.PrefetchScalarGridSpec(
            num_scalar_prefetch=1,
            grid=(steps,),
            in_specs=[
                *block_specs,
                *[pl.BlockSpec((2, 8, cap), lambda t, s: (0, 0, 0))] * len(pairs),
                wedge_spec,
            ],
            out_specs=pl.BlockSpec((count * cap, tile), lambda t, s: (0, t)),
            scratch_shapes=[
                pltpu.VMEM((count // bunch, bunch * cap, bunch * rows), BF16),
                pltpu.VMEM((count * cap, 3 * masks), BF16),
            ],
        ),
        out_shape=jax.ShapeDtypeStruct((count * cap, steps * tile), BF16),
        cost_estimate=cost(
            4 * count * cap * 256 * steps * tile, 2 * count * (cap + rows) * steps * tile
        ),
        name="select",
    )(place, *blocks, *pairs, wedge)


def correl_kernel(blocks, seeded, place, scaled, wedge, *rest):
    refs, rest = rest[:blocks], rest[blocks:]
    seeds, rest = (rest[:3], rest[3:]) if seeded else ((), rest)
    own, other, norms, table = rest
    cap, count = own.shape
    masks = wedge.shape[0]
    per_ref = count // blocks

    @pl.when(pl.program_id(0) == 0)
    def _():
        for i, target in enumerate((own, other, norms)):
            target[...] = seeds[i][...] if seeded else jnp.zeros_like(target)

    for p in range(blocks):
        table[p * per_ref : (p + 1) * per_ref, :] = refs[p][...]
    every = table[...]
    got = dot(scaled[...], every, LANES)
    own[...] += got[:cap]
    other[:cap, :] += got[cap:]
    wide = every.astype(F32)
    high, low = pieces_of(wide * wide, 2)
    lined = jnp.concatenate(pieces_of(wedge[...], 3), axis=0)
    sums = dot(high, lined, LANES) + dot(low, lined, LANES)
    norms[:, :masks] += sums[:, :masks] + sums[:, masks : 2 * masks] + sums[:, 2 * masks :]

    @pl.when(pl.program_id(0) == pl.num_programs(0) - 1)
    def _():
        other[cap:, :] = norms[...].T[:masks]


def correl(place, scaled, wedge, wedge_spec, refs, shift, tile, steps, seeds):
    blocks = len(refs)
    cap = scaled.shape[0] // 2
    masks = wedge.shape[0]
    per_ref = refs[0].shape[0]
    count = blocks * per_ref
    in_specs = [pl.BlockSpec((2 * cap, tile), lambda t, s: (0, shift + t)), wedge_spec]
    in_specs += [pl.BlockSpec((per_ref, tile), lambda t, s: (0, t))] * blocks
    shapes = [(cap, count), (cap + masks, count), (count, 128)]
    outs = [pl.BlockSpec(shape, lambda t, s: (0, 0)) for shape in shapes]
    if seeds:
        in_specs += outs
    return pl.pallas_call(
        functools.partial(correl_kernel, blocks, bool(seeds)),
        grid_spec=pltpu.PrefetchScalarGridSpec(
            num_scalar_prefetch=1,
            grid=(steps,),
            in_specs=in_specs,
            out_specs=outs,
            scratch_shapes=[pltpu.VMEM((count, tile), BF16)],
        ),
        out_shape=[jax.ShapeDtypeStruct(shape, F32) for shape in shapes],
        cost_estimate=cost(
            8 * cap * count * steps * tile, 2 * steps * tile * (2 * cap + count + 2 * masks)
        ),
        name="correl",
    )(place, scaled, wedge, *refs, *seeds)


def weigh_kernel(scale, own, sent, got, pair, out):
    cap = own.shape[0]
    masks = sent.shape[0] - cap
    columns = columns_of(pair[0])
    marks = (iota((cap, masks), 1) == columns[:, 1:2]).astype(F32)
    wedge_hot = jnp.concatenate([marks] * 3, axis=1).astype(BF16)
    norms = jnp.concatenate(pieces_of(sent[cap:, :] + got[cap:, :], 3), axis=0)
    score = (own[...] + got[:cap, :] - 0.5 * dot(wedge_hot, norms)) * scale
    score = jnp.exp(score - jnp.max(score, axis=1, keepdims=True))
    share = score / jnp.sum(score, axis=1, keepdims=True) * columns[:, 2:3]
    out[...] = share.T.astype(BF16)


def weigh(own, sent, got, pair, scale):
    cap, count = own.shape
    return pl.pallas_call(
        functools.partial(weigh_kernel, scale),
        in_specs=[VMEM] * 4,
        out_specs=VMEM,
        out_shape=jax.ShapeDtypeStruct((count, cap), BF16),
        cost_estimate=cost(1 << 24, 1 << 18),
        name="weigh",
    )(own, sent, got, pair)


def blend_kernel(lists, blocks, masks, steps, place, *rest):
    weights, rest = rest[:lists], rest[lists:]
    pairs, scaled = rest[: -blocks - 2], rest[-blocks - 2]
    outs, turned = rest[-blocks - 1 : -1], rest[-1]
    cap = weights[0].shape[1]
    per_ref = outs[0].shape[-2]

    @pl.when(pl.program_id(0) == 0)
    def _():
        for g in range(lists):
            turned[:, g * cap : (g + 1) * cap] = weights[g][...]

    @pl.when(pl.program_id(0) < steps)
    def _():
        sums = dot(turned[...], scaled[...]).astype(BF16)
        for p, out in enumerate(outs):
            out[...] = sums[p * per_ref : (p + 1) * per_ref, :].reshape(out.shape)

    if pairs:

        @pl.when(pl.program_id(0) == steps)
        def _():
            total = jnp.zeros((turned.shape[0], masks), F32)
            for g in range(lists):
                marks = hot(iota((masks, cap), 0) == pairs[g // 2][g % 2, 1:2, :])
                total = total + dot(turned[:, g * cap : (g + 1) * cap], marks, LANES)
            parts = jnp.concatenate(pieces_of(total, 3), axis=1)
            for p, out in enumerate(outs):
                out[:, : 3 * masks] = parts[p * per_ref : (p + 1) * per_ref, :]


def blend(place, weights, pairs, scaled, masks, blocks, tile, steps, index):
    lists = len(weights)
    count, cap = weights[0].shape
    per_ref = count // blocks
    if pairs:
        shape = (per_ref, steps * tile + 128)
        spec = pl.BlockSpec((per_ref, tile), lambda t, s: (0, t))
    else:
        shape = (steps, per_ref, tile)
        spec = pl.BlockSpec((1, per_ref, tile), lambda t, s: (t, 0, 0))
    return pl.pallas_call(
        functools.partial(blend_kernel, lists, blocks, masks, steps),
        grid_spec=pltpu.PrefetchScalarGridSpec(
            num_scalar_prefetch=1,
            grid=(steps + (1 if pairs else 0),),
            in_specs=[pl.BlockSpec((count, cap), lambda t, s: (0, 0))] * lists
            + [pl.BlockSpec((2, 8, cap), lambda t, s: (0, 0, 0))] * len(pairs)
            + [pl.BlockSpec((lists * cap, tile), index)],
            out_specs=[spec] * blocks,
            scratch_shapes=[pltpu.VMEM((count, lists * cap), BF16)],
        ),
        out_shape=[jax.ShapeDtypeStruct(shape, BF16)] * blocks,
        cost_estimate=cost(
            2 * lists * cap * count * steps * tile, 2 * (lists * cap + count) * steps * tile
        ),
        name="blend",
    )(place, *weights, *pairs, scaled)


def fold_kernel(parts, *refs):
    sources, outs = refs[:parts], refs[parts:]
    for t, out in enumerate(outs):
        total = sources[0][t].astype(F32)
        for source in sources[1:]:
            total = total + source[t].astype(F32)
        out[...] = total.astype(BF16)


def fold(parts):
    layers, per_ref, tile = parts[0].shape
    return pl.pallas_call(
        functools.partial(fold_kernel, len(parts)),
        in_specs=[VMEM] * len(parts),
        out_specs=[VMEM] * layers,
        out_shape=[jax.ShapeDtypeStruct((per_ref, tile), BF16)] * layers,
        cost_estimate=cost(0, 2 * (len(parts) + 1) * layers * per_ref * tile),
        name="fold",
    )(*parts)


def finish_kernel(blocks, place, *rest):
    shares, masses, rest = rest[:blocks], rest[blocks : 2 * blocks], rest[2 * blocks :]
    apart, wedge, out = rest[:-2], rest[-2], rest[-1]
    masks = wedge.shape[0]
    mass = masses[0][...].astype(F32)
    for part in masses[1:]:
        mass = mass + part[...].astype(F32)
    mass = mass[:, :masks] + mass[:, masks : 2 * masks] + mass[:, 2 * masks : 3 * masks]
    below = jnp.ones(out.shape, F32)
    for w in range(masks):
        below = below + mass[:, w : w + 1] * wedge[w : w + 1, :]

    def emit(parts):
        total = parts[0][...].astype(F32)
        for part in parts[1:]:
            total = total + part[...].astype(F32)
        out[...] = total / below

    last = pl.num_programs(0) - 1

    @pl.when(pl.program_id(0) < last)
    def _():
        emit(shares)

    @pl.when(pl.program_id(0) == last)
    def _():
        emit(apart)


def finish(place, shares, apart, wedge, tile):
    per_ref, width = shares[0].shape
    masks = wedge.shape[0]
    blocks = len(shares)
    return pl.pallas_call(
        functools.partial(finish_kernel, blocks),
        grid_spec=pltpu.PrefetchScalarGridSpec(
            num_scalar_prefetch=1,
            grid=(SPLIT,),
            in_specs=[pl.BlockSpec((per_ref, tile), lambda t, s: (0, jnp.minimum(t, SPLIT - 2)))]
            * blocks
            + [pl.BlockSpec((per_ref, 128), lambda t, s: (0, width // 128 - 1))] * blocks
            + [pl.BlockSpec((per_ref, tile), lambda t, s: (0, 0))] * len(apart)
            + [pl.BlockSpec((masks, tile), lambda t, s: (0, s[1] * SPLIT + t))],
            out_specs=pl.BlockSpec((per_ref, tile), lambda t, s: (0, t)),
        ),
        out_shape=jax.ShapeDtypeStruct((per_ref, SPLIT * tile), F32),
        cost_estimate=cost(0, 8 * per_ref * SPLIT * tile),
        name="finish",
    )(place, *shares, *shares, *apart, wedge)


GRP = ("lay", "core")


def passed(values, axis, size):
    return [values[0]] + [
        lax.ppermute(values[p], axis, [(d, d ^ p) for d in range(size)]) for p in range(1, size)
    ]


def per_device(slab, pick_owner, pick_offset, wedge_id, live_count, references, wedge):
    slot_count, voxels = slab.shape
    masks = wedge.shape[0]
    layers = lax.axis_size("lay")
    groups = 2 * layers
    blocks = lax.axis_size("blk")
    per_vox = voxels // groups
    tile = per_vox // SPLIT
    keep = per_vox - tile
    half_steps = voxels // 2 // tile
    cap = 2 * slot_count
    block = lax.axis_index("blk").astype(jnp.int32)
    core = lax.axis_index("core").astype(jnp.int32)
    layer = lax.axis_index("lay").astype(jnp.int32)
    place = jnp.stack([core, layer * 2 + core, layer, block])

    live = (jnp.arange(slot_count, dtype=jnp.int32) < live_count[0]).astype(jnp.int32)
    mine = jnp.stack([pick_owner[:, 0], pick_offset, wedge_id, live])
    meta = jnp.concatenate(passed([mine] * blocks, "blk", blocks), axis=1)
    low, high, aside = cut(place, references, slab, layers, per_vox)
    stretches = [low, high]
    if blocks == 4:
        near = [[(b, b ^ 1) for b in range(4)], [(b, b ^ 2) for b in range(4)]]
        sides = [[lax.ppermute(low, "blk", near[i]) for i in range(2)]]
        sides += [[lax.ppermute(high, "blk", near[i]) for i in range(2)]]
        across = [
            lax.ppermute(sides[0][0], "blk", near[1]),
            lax.ppermute(sides[1][1], "blk", near[0]),
        ]
        tables = [[stretches[i], *sides[i], across[i]] for i in range(2)]
    else:
        tables = [passed([s] * blocks, "blk", blocks) for s in stretches]
    mate = lax.ppermute(aside, "core", [(0, 1), (1, 0)])
    columns = passed([slab, *deal(place, slab, groups, keep)], GRP, groups)

    listed = lists_of(block.reshape(1), meta, cap)
    pair = jnp.stack(passed([listed] * 2, "core", 2))
    pairs = passed([pair] * layers, "lay", layers)

    def local(t, s, split=SPLIT):
        return (0, (2 * (t // split) + s[0]) * split + t % split)

    wide = functools.partial(local, split=SPLIT // 2)
    scaled = select(
        place,
        [slab, mate],
        [
            pl.BlockSpec((slot_count, 2 * tile), wide),
            pl.BlockSpec((slot_count, 2 * tile), lambda t, s: (0, t)),
        ],
        [pair],
        wedge,
        pl.BlockSpec((masks, 2 * tile), wide),
        slot_count,
        2 * tile,
        half_steps // 2,
    )
    sums = ()
    for i in range(2):
        shift = i * half_steps // 2
        spec = pl.BlockSpec((masks, tile), lambda t, s, shift=shift: local(shift + t, s))
        sums = correl(place, scaled, wedge, spec, tables[i], shift, tile, half_steps // 2, sums)
    own, other, _ = sums
    got = lax.ppermute(other, "core", [(0, 1), (1, 0)])
    weights = weigh(own, other, got, pair, 1.0 / (32.0 * math.sqrt(voxels)))
    all_weights = passed([weights] * groups, GRP, groups)

    chosen = select(
        place,
        columns,
        [pl.BlockSpec((slot_count, tile), lambda t, s: (0, s[1] * SPLIT + t))]
        + [pl.BlockSpec((slot_count, tile), lambda t, s: (0, t))] * (groups - 1),
        pairs,
        wedge,
        pl.BlockSpec((masks, tile), lambda t, s: (0, s[1] * SPLIT + t)),
        slot_count,
        tile,
        SPLIT - 1,
    )

    apart = blend(
        place,
        all_weights[:2],
        [],
        scaled,
        masks,
        blocks,
        tile,
        layers,
        lambda t, s: (0, (s[2] ^ t) * SPLIT + SPLIT - 1),
    )
    apart = passed(apart, "blk", blocks)
    apart = fold(apart)
    apart = passed(apart, "lay", layers)

    shares = blend(
        place,
        all_weights,
        pairs,
        chosen,
        masks,
        blocks,
        tile,
        SPLIT - 1,
        lambda t, s: (0, jnp.minimum(t, SPLIT - 2)),
    )
    shares = passed(shares, "blk", blocks)
    return finish(place, shares, apart, wedge, tile)


def solution(mesh):
    groups, blocks = mesh.shape["grp"], mesh.shape["blk"]
    fine = Mesh(mesh.devices.reshape(groups // 2, 2, blocks), ("lay", "core", "blk"))
    every = ("lay", "core", "blk")
    placed = (P(every, None), P(every, None), P(every), P(every), P(every), P("blk", None), P())

    return jax.shard_map(
        per_device, mesh=fine, in_specs=placed, out_specs=P("blk", GRP), check_vma=False
    )
```

```python
import functools
import math

import jax
import jax.numpy as jnp
from jax import lax
from jax.experimental import pallas as pl
from jax.experimental.pallas import tpu as pltpu
from jax.sharding import Mesh
from jax.sharding import PartitionSpec as P

F32 = jnp.float32
BF16 = jnp.bfloat16
ROWS = (((1,), (0,)), ((), ()))
LANES = (((1,), (1,)), ((), ()))
VMEM = pl.BlockSpec(memory_space=pltpu.VMEM)
SMEM = pl.BlockSpec(memory_space=pltpu.SMEM)
SPLIT = 4


def dot(left, right, dims=ROWS):
    return lax.dot_general(left, right, dims, preferred_element_type=F32)


def pieces_of(value, count):
    parts = []
    for _ in range(count):
        part = value.astype(BF16)
        value = value - part.astype(F32)
        parts.append(part)
    return parts


def iota(shape, axis):
    return lax.broadcasted_iota(jnp.int32, shape, axis).astype(F32)


def hot(mask):
    return mask.astype(F32).astype(BF16)


def cost(flops, moved):
    return pl.CostEstimate(flops=int(flops), bytes_accessed=int(moved), transcendentals=0)


def cut_kernel(place, refs, slab, *rest):
    outs, held, came, went = rest[:3], rest[3:6], rest[6], rest[7]
    layers, per_vox = held[2].shape[0], held[2].shape[2]
    core = place[0]

    def start(which):
        source, side = (slab, 1 - core) if which == 2 else (refs, core)
        first = layers // 2 if which == 1 else 0
        copies = []
        for z in range(held[which].shape[0]):
            at = pl.multiple_of((2 * (first + z) + side) * per_vox, per_vox)
            copy = pltpu.make_async_copy(
                source.at[:, pl.ds(at, per_vox)], held[which].at[z], came.at[which, z]
            )
            copy.start()
            copies.append(copy)
        return copies

    coming = [start(which) for which in range(3)]
    going = []
    for which in range(3):
        for z, copy in enumerate(coming[which]):
            copy.wait()
            leave = pltpu.make_async_copy(
                held[which].at[z],
                outs[which].at[:, pl.ds(z * per_vox, per_vox)],
                went.at[which, z],
            )
            leave.start()
            going.append(leave)
    for leave in going:
        leave.wait()


def cut(place, refs, slab, layers, per_vox):
    anywhere = pl.BlockSpec(memory_space=pl.ANY)
    shapes = [
        (layers // 2, refs.shape[0]),
        (layers // 2, refs.shape[0]),
        (layers, slab.shape[0]),
    ]
    return pl.pallas_call(
        cut_kernel,
        in_specs=[SMEM, anywhere, anywhere],
        out_specs=[anywhere] * 3,
        out_shape=[jax.ShapeDtypeStruct((r, n * per_vox), BF16) for n, r in shapes],
        scratch_shapes=[pltpu.VMEM((n, r, per_vox), BF16) for n, r in shapes]
        + [pltpu.SemaphoreType.DMA((3, layers))] * 2,
        cost_estimate=cost(0, 4 * sum(n * r for n, r in shapes) * per_vox),
        name="cut",
    )(place, refs, slab)


def deal_kernel(place, slab, mate, *rest):
    peers = len(rest) - 3
    outs, held, came, went = rest[:peers], rest[peers], rest[peers + 1], rest[peers + 2]
    rows = slab.shape[0]
    keep = held.shape[2]
    per_vox = mate.shape[1] // (peers + 1)
    coming = []
    for p in range(peers):
        layer = place[2] ^ (p + 1)
        mine = pl.multiple_of((2 * layer + place[0]) * per_vox, per_vox)
        theirs = pl.multiple_of(layer * per_vox, per_vox)
        pair = [
            pltpu.make_async_copy(
                slab.at[:, pl.ds(mine, keep)], held.at[p, pl.ds(0, rows)], came.at[p, 0]
            ),
            pltpu.make_async_copy(
                mate.at[:, pl.ds(theirs, keep)], held.at[p, pl.ds(rows, rows)], came.at[p, 1]
            ),
        ]
        for copy in pair:
            copy.start()
        coming.append(pair)
    going = []
    for p in range(peers):
        for copy in coming[p]:
            copy.wait()
        leave = pltpu.make_async_copy(held.at[p], outs[p], went.at[p])
        leave.start()
        going.append(leave)
    for leave in going:
        leave.wait()


def deal(place, slab, mate, layers, keep):
    rows = slab.shape[0]
    anywhere = pl.BlockSpec(memory_space=pl.ANY)
    peers = layers - 1
    return pl.pallas_call(
        deal_kernel,
        in_specs=[SMEM, anywhere, anywhere],
        out_specs=[anywhere] * peers,
        out_shape=[jax.ShapeDtypeStruct((2 * rows, keep), BF16)] * peers,
        scratch_shapes=[
            pltpu.VMEM((peers, 2 * rows, keep), BF16),
            pltpu.SemaphoreType.DMA((peers, 2)),
            pltpu.SemaphoreType.DMA((peers,)),
        ],
        cost_estimate=cost(0, 8 * rows * peers * keep),
        name="deal",
    )(place, slab, mate)


def brief_kernel(live, refs, wedge, owner, offset, wedge_id, out, sums):
    masks = wedge.shape[0]
    per_ref = refs.shape[0]
    slots = owner.shape[1]

    @pl.when(pl.program_id(0) == 0)
    def _():
        sums[...] = jnp.zeros_like(sums)

    wide = refs[...].astype(F32)
    high, low = pieces_of(wide * wide, 2)
    lined = jnp.concatenate(pieces_of(wedge[...], 3), axis=0)
    sums[...] += dot(lined, high, LANES) + dot(lined, low, LANES)

    @pl.when(pl.program_id(0) == pl.num_programs(0) - 1)
    def _():
        out[...] = jnp.zeros_like(out)
        out[0:1, :] = jnp.full((1, out.shape[1]), -1.0, F32)
        out[0:1, :slots] = owner[...].astype(F32)
        out[1:2, :slots] = offset[...].astype(F32)
        out[2:3, :slots] = wedge_id[...].astype(F32)
        out[3:4, :slots] = (iota((1, slots), 1) < live[0].astype(F32)).astype(F32)
        out[8 : 8 + masks, :per_ref] = (
            sums[:masks] + sums[masks : 2 * masks] + sums[2 * masks : 3 * masks]
        )


def brief(live, refs, wedge, owner, offset, wedge_id, tile):
    per_ref, voxels = refs.shape
    masks = wedge.shape[0]
    slots = owner.shape[1]
    height = -(-(8 + masks) // 8) * 8
    row = pl.BlockSpec((1, slots), lambda t, s: (0, 0))
    return pl.pallas_call(
        brief_kernel,
        grid_spec=pltpu.PrefetchScalarGridSpec(
            num_scalar_prefetch=1,
            grid=(voxels // tile,),
            in_specs=[
                pl.BlockSpec((per_ref, tile), lambda t, s: (0, t)),
                pl.BlockSpec((masks, tile), lambda t, s: (0, t)),
                row,
                row,
                row,
            ],
            out_specs=pl.BlockSpec((height, 128), lambda t, s: (0, 0)),
            scratch_shapes=[pltpu.VMEM((3 * masks, per_ref), F32)],
        ),
        out_shape=jax.ShapeDtypeStruct((height, 128), F32),
        cost_estimate=cost(12 * masks * per_ref * voxels, 2 * voxels * (per_ref + 2 * masks)),
        name="brief",
    )(live, refs, wedge, owner, offset, wedge_id)


def lists_kernel(place, *rest):
    notes, out = rest[:-1], rest[-1]
    cap = out.shape[1]
    slots = notes[0].shape[1]
    earlier = hot(iota((slots, slots), 0) < iota((slots, slots), 1))
    before = jnp.zeros((1, 1), F32)
    total = jnp.zeros(out.shape, F32)
    for note in notes:
        info = note[0:4, :]
        named = jnp.logical_and(info[0:1] == place[3].astype(F32), info[3:4] > 0.0)
        chosen = named.astype(F32)
        rank = dot(jnp.broadcast_to(chosen, (8, slots)).astype(BF16), earlier)[0:1] + before
        order = hot(jnp.logical_and(iota((cap, slots), 0) == rank, named))
        listed = jnp.concatenate(
            [info[1:2] * chosen, info[2:3] * chosen, chosen, jnp.zeros((5, slots), F32)], axis=0
        )
        total = total + dot(listed.astype(BF16), order, LANES)
        before = before + jnp.sum(chosen, axis=1, keepdims=True)
    out[...] = total


def lists_of(place, notes, cap):
    return pl.pallas_call(
        lists_kernel,
        in_specs=[SMEM] + [VMEM] * len(notes),
        out_specs=VMEM,
        out_shape=jax.ShapeDtypeStruct((8, cap), F32),
        cost_estimate=cost(1 << 22, 1 << 18),
        name="lists",
    )(place, *notes)


def columns_of(listed):
    cap = listed.shape[1]
    eye = hot(iota((cap, cap), 0) == iota((cap, cap), 1))
    return dot(eye, listed.astype(BF16), LANES)


def select_kernel(sources, place, *rest):
    blocks, pairs, wedge, out = rest[:sources], rest[sources:-4], rest[-4], rest[-3]
    rows_hot, wedge_hot = rest[-2:]
    bunches, height, depth = rows_hot.shape
    count = 2 * len(pairs)
    cap = wedge_hot.shape[0] // count
    bunch = height // cap
    rows = depth // bunch
    masks = wedge.shape[0]

    @pl.when(pl.program_id(0) == 0)
    def _():
        rows_hot[...] = jnp.zeros_like(rows_hot)
        for g in range(count):
            columns = columns_of(pairs[g // 2][g % 2])
            n, at = g // bunch, g % bunch
            rows_hot[n, at * cap : (at + 1) * cap, at * rows : (at + 1) * rows] = hot(
                iota((cap, rows), 1) == columns[:, 0:1]
            )
            marks = (iota((cap, masks), 1) == columns[:, 1:2]).astype(F32)
            wedge_hot[g * cap : (g + 1) * cap, :] = jnp.concatenate([marks] * 3, axis=1).astype(
                BF16
            )

    lined = jnp.concatenate(pieces_of(wedge[...], 3), axis=0)
    weights = dot(wedge_hot[...], lined)
    taken = 0
    for n in range(bunches):
        stack, have = [], 0
        while have < depth:
            stack.append(blocks[taken][...])
            have += blocks[taken].shape[0]
            taken += 1
        values = dot(rows_hot[n], jnp.concatenate(stack, axis=0) if len(stack) > 1 else stack[0])
        part = slice(n * height, (n + 1) * height)
        out[part, :] = (weights[part] * values).astype(BF16)


def select(place, blocks, block_specs, pairs, wedge, wedge_spec, rows, tile, steps):
    count = 2 * len(pairs)
    cap = pairs[0].shape[2]
    masks = wedge.shape[0]
    bunch = min(count, 256 // rows)
    return pl.pallas_call(
        functools.partial(select_kernel, len(blocks)),
        grid_spec=pltpu.PrefetchScalarGridSpec(
            num_scalar_prefetch=1,
            grid=(steps,),
            in_specs=[
                *block_specs,
                *[pl.BlockSpec((2, 8, cap), lambda t, s: (0, 0, 0))] * len(pairs),
                wedge_spec,
            ],
            out_specs=pl.BlockSpec((count * cap, tile), lambda t, s: (0, t)),
            scratch_shapes=[
                pltpu.VMEM((count // bunch, bunch * cap, bunch * rows), BF16),
                pltpu.VMEM((count * cap, 3 * masks), BF16),
            ],
        ),
        out_shape=jax.ShapeDtypeStruct((count * cap, steps * tile), BF16),
        cost_estimate=cost(
            4 * count * cap * 256 * steps * tile, 2 * count * (cap + rows) * steps * tile
        ),
        name="select",
    )(place, *blocks, *pairs, wedge)


def correl_kernel(blocks, scaled, *rest):
    refs, out, table = rest[:-2], rest[-2], rest[-1]
    per_ref = refs[0].shape[0]
    step = pl.program_id(0)
    half = pl.num_programs(0) // 2

    @pl.when(step == 0)
    def _():
        out[...] = jnp.zeros_like(out)

    def fill(side):
        for p in range(blocks):
            table[p * per_ref : (p + 1) * per_ref, :] = refs[2 * p + side][...]

    @pl.when(step < half)
    def _():
        fill(0)

    @pl.when(step >= half)
    def _():
        fill(1)

    out[...] += dot(scaled[...], table[...], LANES)


def correl(scaled, tables, tile):
    height, span = scaled.shape
    blocks = len(tables[0])
    per_ref = tables[0][0].shape[0]
    count = blocks * per_ref
    steps = span // tile
    half = steps // 2
    sides = [
        pl.BlockSpec((per_ref, tile), lambda t: (0, jnp.minimum(t, half - 1))),
        pl.BlockSpec((per_ref, tile), lambda t: (0, jnp.maximum(t - half, 0))),
    ]
    refs = [tables[i][p] for p in range(blocks) for i in range(2)]
    return pl.pallas_call(
        functools.partial(correl_kernel, blocks),
        grid=(steps,),
        in_specs=[pl.BlockSpec((height, tile), lambda t: (0, t))] + sides * blocks,
        out_specs=pl.BlockSpec((height, count), lambda t: (0, 0)),
        out_shape=jax.ShapeDtypeStruct((height, count), F32),
        scratch_shapes=[pltpu.VMEM((count, tile), BF16)],
        cost_estimate=cost(2 * height * count * span, 2 * span * (height + count)),
        name="correl",
    )(scaled, *refs)


def weigh_kernel(scale, masks, own, got, pair, *rest):
    notes, out = rest[:-1], rest[-1]
    count, cap = out.shape[1], out.shape[2]
    per_ref = count // len(notes)
    lanes = notes[0].shape[1]
    norms = jnp.zeros((3 * masks, count), F32)
    for p, note in enumerate(notes):
        parts = jnp.concatenate(pieces_of(note[8 : 8 + masks, :], 3), axis=0)
        shifted = hot(
            jnp.logical_and(
                iota((lanes, count), 0) + float(p * per_ref) == iota((lanes, count), 1),
                iota((lanes, count), 0) < float(per_ref),
            )
        )
        norms = norms + dot(parts, shifted)
    norms = norms.astype(BF16)
    for side in range(2):
        columns = columns_of(pair[side])
        marks = (iota((cap, masks), 1) == columns[:, 1:2]).astype(F32)
        wedge_hot = jnp.concatenate([marks] * 3, axis=1).astype(BF16)
        mine = own[side * cap : (side + 1) * cap, :] + got[(1 - side) * cap : (2 - side) * cap, :]
        score = (mine - 0.5 * dot(wedge_hot, norms)) * scale
        score = jnp.exp(score - jnp.max(score, axis=1, keepdims=True))
        share = score / jnp.sum(score, axis=1, keepdims=True) * columns[:, 2:3]
        out[side] = share.T.astype(BF16)


def weigh(own, got, pair, notes, masks, scale):
    cap, count = own.shape[0] // 2, own.shape[1]
    return pl.pallas_call(
        functools.partial(weigh_kernel, scale, masks),
        in_specs=[VMEM] * (3 + len(notes)),
        out_specs=VMEM,
        out_shape=jax.ShapeDtypeStruct((2, count, cap), BF16),
        cost_estimate=cost(1 << 24, 1 << 18),
        name="weigh",
    )(own, got, pair, *notes)


def blend_kernel(layers, parts, blocks, masks, steps, place, *rest):
    weights, rest = rest[:layers], rest[layers:]
    scaled, pairs = rest[:parts], rest[parts : -blocks - 1]
    outs, turned = rest[-blocks - 1 : -1], rest[-1]
    cap = weights[0].shape[2]
    per_ref = outs[0].shape[-2]

    @pl.when(pl.program_id(0) == 0)
    def _():
        for g in range(2 * layers):
            turned[:, g * cap : (g + 1) * cap] = weights[g // 2][g % 2]

    @pl.when(pl.program_id(0) < steps)
    def _():
        first = 0
        sums = 0.0
        for part in scaled:
            sums = sums + dot(turned[:, first : first + part.shape[0]], part[...])
            first += part.shape[0]
        sums = sums.astype(BF16)
        for p, out in enumerate(outs):
            out[...] = sums[p * per_ref : (p + 1) * per_ref, :].reshape(out.shape)

    if pairs:

        @pl.when(pl.program_id(0) == steps)
        def _():
            total = jnp.zeros((turned.shape[0], masks), F32)
            for g in range(2 * layers):
                marks = hot(iota((masks, cap), 0) == pairs[g // 2][g % 2, 1:2, :])
                total = total + dot(turned[:, g * cap : (g + 1) * cap], marks, LANES)
            split = jnp.concatenate(pieces_of(total, 3), axis=1)
            for p, out in enumerate(outs):
                out[:, : 3 * masks] = split[p * per_ref : (p + 1) * per_ref, :]


def blend(place, weights, pairs, scaled, masks, blocks, tile, steps, index):
    layers = len(weights)
    _, count, cap = weights[0].shape
    per_ref = count // blocks
    if pairs:
        shape = (per_ref, steps * tile + 128)
        spec = pl.BlockSpec((per_ref, tile), lambda t, s: (0, t))
    else:
        shape = (steps, per_ref, tile)
        spec = pl.BlockSpec((1, per_ref, tile), lambda t, s: (t, 0, 0))
    return pl.pallas_call(
        functools.partial(blend_kernel, layers, len(scaled), blocks, masks, steps),
        grid_spec=pltpu.PrefetchScalarGridSpec(
            num_scalar_prefetch=1,
            grid=(steps + (1 if pairs else 0),),
            in_specs=[pl.BlockSpec((2, count, cap), lambda t, s: (0, 0, 0))] * layers
            + [pl.BlockSpec((part.shape[0], tile), index) for part in scaled]
            + [pl.BlockSpec((2, 8, cap), lambda t, s: (0, 0, 0))] * len(pairs),
            out_specs=[spec] * blocks,
            scratch_shapes=[pltpu.VMEM((count, 2 * layers * cap), BF16)],
        ),
        out_shape=[jax.ShapeDtypeStruct(shape, BF16)] * blocks,
        cost_estimate=cost(
            4 * layers * cap * count * steps * tile, 2 * (2 * layers * cap + count) * steps * tile
        ),
        name="blend",
    )(place, *weights, *scaled, *pairs)


def fold_kernel(parts, *refs):
    sources, outs = refs[:parts], refs[parts:]
    for t, out in enumerate(outs):
        total = sources[0][t].astype(F32)
        for source in sources[1:]:
            total = total + source[t].astype(F32)
        out[...] = total.astype(BF16)


def fold(parts):
    layers, per_ref, tile = parts[0].shape
    return pl.pallas_call(
        functools.partial(fold_kernel, len(parts)),
        in_specs=[VMEM] * len(parts),
        out_specs=[VMEM] * layers,
        out_shape=[jax.ShapeDtypeStruct((per_ref, tile), BF16)] * layers,
        cost_estimate=cost(0, 2 * (len(parts) + 1) * layers * per_ref * tile),
        name="fold",
    )(*parts)


def finish_kernel(blocks, place, *rest):
    shares, apart = rest[:blocks], rest[blocks:-6]
    wedge, out, tables, held, came, went = rest[-6:]
    masks = wedge.shape[0]
    span = tables.shape[1]
    tile = held.shape[2]
    at = pl.multiple_of(place[1] * span, span)
    fetch = pltpu.make_async_copy(wedge.at[:, pl.ds(at, span)], tables, came)
    fetch.start()
    keep = span - tile
    mass = 0.0
    for part in shares:
        mass = mass + part[:, keep : keep + 3 * masks].astype(F32)
    mass = mass[:, :masks] + mass[:, masks : 2 * masks] + mass[:, 2 * masks : 3 * masks]
    fetch.wait()
    leaves = []
    for t in range(SPLIT):
        cols = slice(t * tile, (t + 1) * tile)
        below = jnp.ones(held.shape[1:], F32)
        for w in range(masks):
            below = below + mass[:, w : w + 1] * tables[w : w + 1, cols]
        total = 0.0
        for part in shares if t < SPLIT - 1 else apart:
            total = total + (part[:, cols] if t < SPLIT - 1 else part[...]).astype(F32)
        held[t] = total / below
        leave = pltpu.make_async_copy(held.at[t], out.at[:, pl.ds(t * tile, tile)], went.at[t])
        leave.start()
        leaves.append(leave)
    for leave in leaves:
        leave.wait()


def finish(place, shares, apart, wedge, tile):
    per_ref = shares[0].shape[0]
    masks = wedge.shape[0]
    blocks = len(shares)
    anywhere = pl.BlockSpec(memory_space=pl.ANY)
    return pl.pallas_call(
        functools.partial(finish_kernel, blocks),
        in_specs=[SMEM] + [VMEM] * (blocks + len(apart)) + [anywhere],
        out_specs=anywhere,
        out_shape=jax.ShapeDtypeStruct((per_ref, SPLIT * tile), F32),
        scratch_shapes=[
            pltpu.VMEM((masks, SPLIT * tile), F32),
            pltpu.VMEM((SPLIT, per_ref, tile), F32),
            pltpu.SemaphoreType.DMA,
            pltpu.SemaphoreType.DMA((SPLIT,)),
        ],
        cost_estimate=cost(0, 8 * per_ref * SPLIT * tile),
        name="finish",
    )(place, *shares, *apart, wedge)


GRP = ("lay", "core")


def passed(values, axis, size):
    return [values[0]] + [
        lax.ppermute(values[p], axis, [(d, d ^ p) for d in range(size)]) for p in range(1, size)
    ]


def per_device(slab, pick_owner, pick_offset, wedge_id, live_count, references, wedge):
    slot_count, voxels = slab.shape
    masks = wedge.shape[0]
    layers = lax.axis_size("lay")
    groups = 2 * layers
    blocks = lax.axis_size("blk")
    per_vox = voxels // groups
    tile = per_vox // SPLIT
    keep = per_vox - tile
    half_steps = voxels // 2 // tile
    cap = 2 * slot_count
    block = lax.axis_index("blk").astype(jnp.int32)
    core = lax.axis_index("core").astype(jnp.int32)
    layer = lax.axis_index("lay").astype(jnp.int32)
    place = jnp.stack([core, layer * 2 + core, layer, block])

    low, high, aside = cut(place, references, slab, layers, per_vox)
    mate = lax.ppermute(aside, "core", [(0, 1), (1, 0)])
    if blocks == 4:
        over_x, over_y = [(b, b ^ 1) for b in range(4)], [(b, b ^ 2) for b in range(4)]
        low_x = lax.ppermute(low, "blk", over_x)
        high_y = lax.ppermute(high, "blk", over_y)
        high_x = lax.ppermute(high, "blk", over_x)
        low_y = lax.ppermute(low, "blk", over_y)
        low_xy = lax.ppermute(low_x, "blk", over_y)
        high_xy = lax.ppermute(high_y, "blk", over_x)
        tables = [[low, low_x, low_y, low_xy], [high, high_x, high_y, high_xy]]
    else:
        tables = [passed([s] * blocks, "blk", blocks) for s in (low, high)]
    far = deal(place, slab, mate, layers, keep)
    nearby = layers // 2
    pieces = [None] * layers
    for p in range(1, layers):
        pieces[p] = lax.ppermute(far[p - 1], "lay", [(z, z ^ p) for z in range(layers)])
    note = brief(
        live_count,
        references,
        wedge,
        pick_owner.reshape(1, slot_count),
        pick_offset.reshape(1, slot_count),
        wedge_id.reshape(1, slot_count),
        per_vox,
    )
    notes = passed([note] * blocks, "blk", blocks)
    listed = lists_of(place, notes, cap)
    pair = jnp.stack(passed([listed] * 2, "core", 2))
    pairs = passed([pair] * layers, "lay", layers)

    def local(t, s, split=SPLIT):
        return (0, (2 * (t // split) + s[0]) * split + t % split)

    def here(t, s):
        return (0, s[1] * SPLIT + t)

    wide = functools.partial(local, split=SPLIT // 2)
    scaled = select(
        place,
        [slab, mate],
        [
            pl.BlockSpec((slot_count, 2 * tile), wide),
            pl.BlockSpec((slot_count, 2 * tile), lambda t, s: (0, t)),
        ],
        [pair],
        wedge,
        pl.BlockSpec((masks, 2 * tile), wide),
        slot_count,
        2 * tile,
        half_steps // 2,
    )
    sums = correl(scaled, tables, tile)
    got = lax.ppermute(sums, "core", [(0, 1), (1, 0)])
    weights = weigh(sums, got, pair, notes, masks, 1.0 / (32.0 * math.sqrt(voxels)))
    all_weights = passed([weights] * layers, "lay", layers)

    received = pl.BlockSpec((2 * slot_count, tile), lambda t, s: (0, t))
    near_rows = select(
        place,
        [slab, mate, *pieces[1:nearby]],
        [
            pl.BlockSpec((slot_count, tile), here),
            pl.BlockSpec((slot_count, tile), lambda t, s: (0, s[2] * SPLIT + t)),
        ]
        + [received] * (nearby - 1),
        pairs[:nearby],
        wedge,
        pl.BlockSpec((masks, tile), here),
        slot_count,
        tile,
        SPLIT - 1,
    )
    far_rows = select(
        place,
        pieces[nearby:],
        [received] * (layers - nearby),
        pairs[nearby:],
        wedge,
        pl.BlockSpec((masks, tile), here),
        slot_count,
        tile,
        SPLIT - 1,
    )

    apart = blend(
        place,
        all_weights[:1],
        [],
        [scaled],
        masks,
        blocks,
        tile,
        layers,
        lambda t, s: (0, (s[2] ^ t) * SPLIT + SPLIT - 1),
    )
    apart = passed(apart, "blk", blocks)
    apart = fold(apart)
    apart = passed(apart, "lay", layers)

    shares = blend(
        place,
        all_weights,
        pairs,
        [near_rows, far_rows],
        masks,
        blocks,
        tile,
        SPLIT - 1,
        lambda t, s: (0, jnp.minimum(t, SPLIT - 2)),
    )
    shares = passed(shares, "blk", blocks)
    return finish(place, shares, apart, wedge, tile)


def solution(mesh):
    groups, blocks = mesh.shape["grp"], mesh.shape["blk"]
    fine = Mesh(mesh.devices.reshape(groups // 2, 2, blocks), ("lay", "core", "blk"))
    every = ("lay", "core", "blk")
    placed = (P(every, None), P(every, None), P(every), P(every), P(every), P("blk", None), P())

    return jax.shard_map(
        per_device, mesh=fine, in_specs=placed, out_specs=P("blk", GRP), check_vma=False
    )
```

```python
import functools
import math

import jax
import jax.numpy as jnp
from jax import lax
from jax.experimental import pallas as pl
from jax.experimental.pallas import tpu as pltpu
from jax.sharding import Mesh
from jax.sharding import PartitionSpec as P

F32 = jnp.float32
BF16 = jnp.bfloat16
ROWS = (((1,), (0,)), ((), ()))
LANES = (((1,), (1,)), ((), ()))
VMEM = pl.BlockSpec(memory_space=pltpu.VMEM)
SMEM = pl.BlockSpec(memory_space=pltpu.SMEM)
SPLIT = 4


def dot(left, right, dims=ROWS):
    return lax.dot_general(left, right, dims, preferred_element_type=F32)


def pieces_of(value, count):
    parts = []
    for _ in range(count):
        part = value.astype(BF16)
        value = value - part.astype(F32)
        parts.append(part)
    return parts


def iota(shape, axis):
    return lax.broadcasted_iota(jnp.int32, shape, axis).astype(F32)


def hot(mask):
    return mask.astype(F32).astype(BF16)


def cost(flops, moved):
    return pl.CostEstimate(flops=int(flops), bytes_accessed=int(moved), transcendentals=0)


def cut_kernel(place, refs, slab, *rest):
    outs, held, came, went = rest[:3], rest[3:6], rest[6], rest[7]
    layers, per_vox = held[2].shape[0], held[2].shape[2]
    core = place[0]

    def start(which):
        source, side = (slab, 1 - core) if which == 2 else (refs, core)
        first = layers // 2 if which == 1 else 0
        copies = []
        for z in range(held[which].shape[0]):
            at = pl.multiple_of((2 * (first + z) + side) * per_vox, per_vox)
            copy = pltpu.make_async_copy(
                source.at[:, pl.ds(at, per_vox)], held[which].at[z], came.at[which, z]
            )
            copy.start()
            copies.append(copy)
        return copies

    coming = [start(which) for which in range(3)]
    going = []
    for which in range(3):
        for z, copy in enumerate(coming[which]):
            copy.wait()
            leave = pltpu.make_async_copy(
                held[which].at[z],
                outs[which].at[:, pl.ds(z * per_vox, per_vox)],
                went.at[which, z],
            )
            leave.start()
            going.append(leave)
    for leave in going:
        leave.wait()


def cut(place, refs, slab, layers, per_vox):
    anywhere = pl.BlockSpec(memory_space=pl.ANY)
    shapes = [
        (layers // 2, refs.shape[0]),
        (layers // 2, refs.shape[0]),
        (layers, slab.shape[0]),
    ]
    return pl.pallas_call(
        cut_kernel,
        in_specs=[SMEM, anywhere, anywhere],
        out_specs=[anywhere] * 3,
        out_shape=[jax.ShapeDtypeStruct((r, n * per_vox), BF16) for n, r in shapes],
        scratch_shapes=[pltpu.VMEM((n, r, per_vox), BF16) for n, r in shapes]
        + [pltpu.SemaphoreType.DMA((3, layers))] * 2,
        cost_estimate=cost(0, 4 * sum(n * r for n, r in shapes) * per_vox),
        name="cut",
    )(place, refs, slab)


def deal_kernel(place, slab, mate, *rest):
    peers = len(rest) - 3
    outs, held, came, went = rest[:peers], rest[peers], rest[peers + 1], rest[peers + 2]
    rows = slab.shape[0]
    keep = held.shape[2]
    per_vox = mate.shape[1] // (peers + 1)
    coming = []
    for p in range(peers):
        layer = place[2] ^ (p + 1)
        mine = pl.multiple_of((2 * layer + place[0]) * per_vox, per_vox)
        theirs = pl.multiple_of(layer * per_vox, per_vox)
        pair = [
            pltpu.make_async_copy(
                slab.at[:, pl.ds(mine, keep)], held.at[p, pl.ds(0, rows)], came.at[p, 0]
            ),
            pltpu.make_async_copy(
                mate.at[:, pl.ds(theirs, keep)], held.at[p, pl.ds(rows, rows)], came.at[p, 1]
            ),
        ]
        for copy in pair:
            copy.start()
        coming.append(pair)
    going = []
    for p in range(peers):
        for copy in coming[p]:
            copy.wait()
        leave = pltpu.make_async_copy(held.at[p], outs[p], went.at[p])
        leave.start()
        going.append(leave)
    for leave in going:
        leave.wait()


def deal(place, slab, mate, layers, keep):
    rows = slab.shape[0]
    anywhere = pl.BlockSpec(memory_space=pl.ANY)
    peers = layers - 1
    return pl.pallas_call(
        deal_kernel,
        in_specs=[SMEM, anywhere, anywhere],
        out_specs=[anywhere] * peers,
        out_shape=[jax.ShapeDtypeStruct((2 * rows, keep), BF16)] * peers,
        scratch_shapes=[
            pltpu.VMEM((peers, 2 * rows, keep), BF16),
            pltpu.SemaphoreType.DMA((peers, 2)),
            pltpu.SemaphoreType.DMA((peers,)),
        ],
        cost_estimate=cost(0, 8 * rows * peers * keep),
        name="deal",
    )(place, slab, mate)


def brief_kernel(live, refs, wedge, owner, offset, wedge_id, out, sums):
    masks = wedge.shape[0]
    per_ref = refs.shape[0]
    slots = owner.shape[1]

    @pl.when(pl.program_id(0) == 0)
    def _():
        sums[...] = jnp.zeros_like(sums)

    wide = refs[...].astype(F32)
    high, low = pieces_of(wide * wide, 2)
    lined = jnp.concatenate(pieces_of(wedge[...], 3), axis=0)
    sums[...] += dot(lined, high, LANES) + dot(lined, low, LANES)

    @pl.when(pl.program_id(0) == pl.num_programs(0) - 1)
    def _():
        out[...] = jnp.zeros_like(out)
        out[0:1, :] = jnp.full((1, out.shape[1]), -1.0, F32)
        out[0:1, :slots] = owner[...].astype(F32)
        out[1:2, :slots] = offset[...].astype(F32)
        out[2:3, :slots] = wedge_id[...].astype(F32)
        out[3:4, :slots] = (iota((1, slots), 1) < live[0].astype(F32)).astype(F32)
        out[8 : 8 + masks, :per_ref] = (
            sums[:masks] + sums[masks : 2 * masks] + sums[2 * masks : 3 * masks]
        )


def brief(live, refs, wedge, owner, offset, wedge_id, tile):
    per_ref, voxels = refs.shape
    masks = wedge.shape[0]
    slots = owner.shape[1]
    height = -(-(8 + masks) // 8) * 8
    row = pl.BlockSpec((1, slots), lambda t, s: (0, 0))
    return pl.pallas_call(
        brief_kernel,
        grid_spec=pltpu.PrefetchScalarGridSpec(
            num_scalar_prefetch=1,
            grid=(voxels // tile,),
            in_specs=[
                pl.BlockSpec((per_ref, tile), lambda t, s: (0, t)),
                pl.BlockSpec((masks, tile), lambda t, s: (0, t)),
                row,
                row,
                row,
            ],
            out_specs=pl.BlockSpec((height, 128), lambda t, s: (0, 0)),
            scratch_shapes=[pltpu.VMEM((3 * masks, per_ref), F32)],
        ),
        out_shape=jax.ShapeDtypeStruct((height, 128), F32),
        cost_estimate=cost(12 * masks * per_ref * voxels, 2 * voxels * (per_ref + 2 * masks)),
        name="brief",
    )(live, refs, wedge, owner, offset, wedge_id)


def lists_kernel(place, *rest):
    notes, out = rest[:-1], rest[-1]
    cap = out.shape[1]
    slots = notes[0].shape[1]
    earlier = hot(iota((slots, slots), 0) < iota((slots, slots), 1))
    before = jnp.zeros((1, 1), F32)
    total = jnp.zeros(out.shape, F32)
    for note in notes:
        info = note[0:4, :]
        named = jnp.logical_and(info[0:1] == place[3].astype(F32), info[3:4] > 0.0)
        chosen = named.astype(F32)
        rank = dot(jnp.broadcast_to(chosen, (8, slots)).astype(BF16), earlier)[0:1] + before
        order = hot(jnp.logical_and(iota((cap, slots), 0) == rank, named))
        listed = jnp.concatenate(
            [info[1:2] * chosen, info[2:3] * chosen, chosen, jnp.zeros((5, slots), F32)], axis=0
        )
        total = total + dot(listed.astype(BF16), order, LANES)
        before = before + jnp.sum(chosen, axis=1, keepdims=True)
    out[...] = total


def lists_of(place, notes, cap):
    return pl.pallas_call(
        lists_kernel,
        in_specs=[SMEM] + [VMEM] * len(notes),
        out_specs=VMEM,
        out_shape=jax.ShapeDtypeStruct((8, cap), F32),
        cost_estimate=cost(1 << 22, 1 << 18),
        name="lists",
    )(place, *notes)


def columns_of(listed):
    cap = listed.shape[1]
    eye = hot(iota((cap, cap), 0) == iota((cap, cap), 1))
    return dot(eye, listed.astype(BF16), LANES)


def select_kernel(sources, place, *rest):
    blocks, pairs, wedge, out = rest[:sources], rest[sources:-4], rest[-4], rest[-3]
    rows_hot, wedge_hot = rest[-2:]
    bunches, height, depth = rows_hot.shape
    count = 2 * len(pairs)
    cap = wedge_hot.shape[0] // count
    bunch = height // cap
    rows = depth // bunch
    masks = wedge.shape[0]

    @pl.when(pl.program_id(0) == 0)
    def _():
        rows_hot[...] = jnp.zeros_like(rows_hot)
        for g in range(count):
            columns = columns_of(pairs[g // 2][g % 2])
            n, at = g // bunch, g % bunch
            rows_hot[n, at * cap : (at + 1) * cap, at * rows : (at + 1) * rows] = hot(
                iota((cap, rows), 1) == columns[:, 0:1]
            )
            marks = (iota((cap, masks), 1) == columns[:, 1:2]).astype(F32)
            wedge_hot[g * cap : (g + 1) * cap, :] = jnp.concatenate([marks] * 3, axis=1).astype(
                BF16
            )

    tile = out.shape[1]

    def part_of(ref):
        if ref.shape[1] == tile:
            return ref[...]
        return ref[:, pl.ds(pl.multiple_of(pl.program_id(0) * tile, 128), tile)]

    lined = jnp.concatenate(pieces_of(part_of(wedge), 3), axis=0)
    weights = dot(wedge_hot[...], lined)
    taken = 0
    for n in range(bunches):
        stack, have = [], 0
        while have < depth:
            stack.append(part_of(blocks[taken]))
            have += blocks[taken].shape[0]
            taken += 1
        values = dot(rows_hot[n], jnp.concatenate(stack, axis=0) if len(stack) > 1 else stack[0])
        part = slice(n * height, (n + 1) * height)
        out[part, :] = (weights[part] * values).astype(BF16)


def select(place, blocks, block_specs, pairs, wedge, wedge_spec, rows, tile, steps):
    count = 2 * len(pairs)
    cap = pairs[0].shape[2]
    masks = wedge.shape[0]
    bunch = max(n for n in (2, 4) if count % n == 0 and n * rows <= 256)
    return pl.pallas_call(
        functools.partial(select_kernel, len(blocks)),
        grid_spec=pltpu.PrefetchScalarGridSpec(
            num_scalar_prefetch=1,
            grid=(steps,),
            in_specs=[
                *block_specs,
                *[pl.BlockSpec((2, 8, cap), lambda t, s: (0, 0, 0))] * len(pairs),
                wedge_spec,
            ],
            out_specs=pl.BlockSpec((count * cap, tile), lambda t, s: (0, t)),
            scratch_shapes=[
                pltpu.VMEM((count // bunch, bunch * cap, bunch * rows), BF16),
                pltpu.VMEM((count * cap, 3 * masks), BF16),
            ],
        ),
        out_shape=jax.ShapeDtypeStruct((count * cap, steps * tile), BF16),
        cost_estimate=cost(
            4 * count * cap * 256 * steps * tile, 2 * count * (cap + rows) * steps * tile
        ),
        name="select",
    )(place, *blocks, *pairs, wedge)


def correl_kernel(blocks, scaled, *rest):
    refs, out, table = rest[:-2], rest[-2], rest[-1]
    per_ref = refs[0].shape[0]
    step = pl.program_id(0)
    half = pl.num_programs(0) // 2

    @pl.when(step == 0)
    def _():
        out[...] = jnp.zeros_like(out)

    def fill(side):
        for p in range(blocks):
            table[p * per_ref : (p + 1) * per_ref, :] = refs[2 * p + side][...]

    @pl.when(step < half)
    def _():
        fill(0)

    @pl.when(step >= half)
    def _():
        fill(1)

    out[...] += dot(scaled[...], table[...], LANES)


def correl(scaled, tables, tile):
    height, span = scaled.shape
    blocks = len(tables[0])
    per_ref = tables[0][0].shape[0]
    count = blocks * per_ref
    steps = span // tile
    half = steps // 2
    sides = [
        pl.BlockSpec((per_ref, tile), lambda t: (0, jnp.minimum(t, half - 1))),
        pl.BlockSpec((per_ref, tile), lambda t: (0, jnp.maximum(t - half, 0))),
    ]
    refs = [tables[i][p] for p in range(blocks) for i in range(2)]
    return pl.pallas_call(
        functools.partial(correl_kernel, blocks),
        grid=(steps,),
        in_specs=[pl.BlockSpec((height, tile), lambda t: (0, t))] + sides * blocks,
        out_specs=pl.BlockSpec((height, count), lambda t: (0, 0)),
        out_shape=jax.ShapeDtypeStruct((height, count), F32),
        scratch_shapes=[pltpu.VMEM((count, tile), BF16)],
        cost_estimate=cost(2 * height * count * span, 2 * span * (height + count)),
        name="correl",
    )(scaled, *refs)


def weigh_kernel(scale, masks, own, got, pair, *rest):
    notes, out = rest[:-1], rest[-1]
    count, cap = out.shape[1], out.shape[2]
    per_ref = count // len(notes)
    lanes = notes[0].shape[1]
    norms = jnp.zeros((3 * masks, count), F32)
    for p, note in enumerate(notes):
        parts = jnp.concatenate(pieces_of(note[8 : 8 + masks, :], 3), axis=0)
        shifted = hot(
            jnp.logical_and(
                iota((lanes, count), 0) + float(p * per_ref) == iota((lanes, count), 1),
                iota((lanes, count), 0) < float(per_ref),
            )
        )
        norms = norms + dot(parts, shifted)
    norms = norms.astype(BF16)
    for side in range(2):
        columns = columns_of(pair[side])
        marks = (iota((cap, masks), 1) == columns[:, 1:2]).astype(F32)
        wedge_hot = jnp.concatenate([marks] * 3, axis=1).astype(BF16)
        mine = own[side * cap : (side + 1) * cap, :] + got[(1 - side) * cap : (2 - side) * cap, :]
        score = (mine - 0.5 * dot(wedge_hot, norms)) * scale
        score = jnp.exp(score - jnp.max(score, axis=1, keepdims=True))
        share = score / jnp.sum(score, axis=1, keepdims=True) * columns[:, 2:3]
        out[side] = share.T.astype(BF16)


def weigh(own, got, pair, notes, masks, scale):
    cap, count = own.shape[0] // 2, own.shape[1]
    return pl.pallas_call(
        functools.partial(weigh_kernel, scale, masks),
        in_specs=[VMEM] * (3 + len(notes)),
        out_specs=VMEM,
        out_shape=jax.ShapeDtypeStruct((2, count, cap), BF16),
        cost_estimate=cost(1 << 24, 1 << 18),
        name="weigh",
    )(own, got, pair, *notes)


def blend_kernel(layers, parts, blocks, masks, steps, place, *rest):
    weights, rest = rest[:layers], rest[layers:]
    scaled, pairs = rest[:parts], rest[parts : -blocks - 1]
    outs, turned = rest[-blocks - 1 : -1], rest[-1]
    cap = weights[0].shape[2]
    per_ref = outs[0].shape[-2]

    @pl.when(pl.program_id(0) == 0)
    def _():
        for g in range(2 * layers):
            turned[:, g * cap : (g + 1) * cap] = weights[g // 2][g % 2]

    @pl.when(pl.program_id(0) < steps)
    def _():
        first = 0
        sums = 0.0
        for part in scaled:
            sums = sums + dot(turned[:, first : first + part.shape[0]], part[...])
            first += part.shape[0]
        sums = sums.astype(BF16)
        for p, out in enumerate(outs):
            out[...] = sums[p * per_ref : (p + 1) * per_ref, :].reshape(out.shape)

    if pairs:

        @pl.when(pl.program_id(0) == steps)
        def _():
            total = jnp.zeros((turned.shape[0], masks), F32)
            for g in range(2 * layers):
                marks = hot(iota((masks, cap), 0) == pairs[g // 2][g % 2, 1:2, :])
                total = total + dot(turned[:, g * cap : (g + 1) * cap], marks, LANES)
            split = jnp.concatenate(pieces_of(total, 3), axis=1)
            for p, out in enumerate(outs):
                out[:, : 3 * masks] = split[p * per_ref : (p + 1) * per_ref, :]


def blend(place, weights, pairs, scaled, masks, blocks, tile, steps, index):
    layers = len(weights)
    _, count, cap = weights[0].shape
    per_ref = count // blocks
    if pairs:
        shape = (per_ref, steps * tile + 128)
        spec = pl.BlockSpec((per_ref, tile), lambda t, s: (0, t))
    else:
        shape = (steps, per_ref, tile)
        spec = pl.BlockSpec((1, per_ref, tile), lambda t, s: (t, 0, 0))
    return pl.pallas_call(
        functools.partial(blend_kernel, layers, len(scaled), blocks, masks, steps),
        grid_spec=pltpu.PrefetchScalarGridSpec(
            num_scalar_prefetch=1,
            grid=(steps + (1 if pairs else 0),),
            in_specs=[pl.BlockSpec((2, count, cap), lambda t, s: (0, 0, 0))] * layers
            + [pl.BlockSpec((part.shape[0], tile), index) for part in scaled]
            + [pl.BlockSpec((2, 8, cap), lambda t, s: (0, 0, 0))] * len(pairs),
            out_specs=[spec] * blocks,
            scratch_shapes=[pltpu.VMEM((count, 2 * layers * cap), BF16)],
        ),
        out_shape=[jax.ShapeDtypeStruct(shape, BF16)] * blocks,
        cost_estimate=cost(
            4 * layers * cap * count * steps * tile, 2 * (2 * layers * cap + count) * steps * tile
        ),
        name="blend",
    )(place, *weights, *scaled, *pairs)


def fold_kernel(parts, *refs):
    sources, outs = refs[:parts], refs[parts:]
    for t, out in enumerate(outs):
        total = sources[0][t].astype(F32)
        for source in sources[1:]:
            total = total + source[t].astype(F32)
        out[...] = total.astype(BF16)


def fold(parts):
    layers, per_ref, tile = parts[0].shape
    return pl.pallas_call(
        functools.partial(fold_kernel, len(parts)),
        in_specs=[VMEM] * len(parts),
        out_specs=[VMEM] * layers,
        out_shape=[jax.ShapeDtypeStruct((per_ref, tile), BF16)] * layers,
        cost_estimate=cost(0, 2 * (len(parts) + 1) * layers * per_ref * tile),
        name="fold",
    )(*parts)


def finish_kernel(blocks, place, *rest):
    shares, apart = rest[:blocks], rest[blocks:-6]
    wedge, out, tables, held, came, went = rest[-6:]
    masks = wedge.shape[0]
    span = tables.shape[1]
    tile = held.shape[2]
    at = pl.multiple_of(place[1] * span, span)
    fetch = pltpu.make_async_copy(wedge.at[:, pl.ds(at, span)], tables, came)
    fetch.start()
    keep = span - tile
    mass = 0.0
    for part in shares:
        mass = mass + part[:, keep : keep + 3 * masks].astype(F32)
    mass = mass[:, :masks] + mass[:, masks : 2 * masks] + mass[:, 2 * masks : 3 * masks]
    fetch.wait()
    leaves = []
    for t in range(SPLIT):
        cols = slice(t * tile, (t + 1) * tile)
        below = jnp.ones(held.shape[1:], F32)
        for w in range(masks):
            below = below + mass[:, w : w + 1] * tables[w : w + 1, cols]
        total = 0.0
        for part in shares if t < SPLIT - 1 else apart:
            total = total + (part[:, cols] if t < SPLIT - 1 else part[...]).astype(F32)
        held[t] = total / below
        leave = pltpu.make_async_copy(held.at[t], out.at[:, pl.ds(t * tile, tile)], went.at[t])
        leave.start()
        leaves.append(leave)
    for leave in leaves:
        leave.wait()


def finish(place, shares, apart, wedge, tile):
    per_ref = shares[0].shape[0]
    masks = wedge.shape[0]
    blocks = len(shares)
    anywhere = pl.BlockSpec(memory_space=pl.ANY)
    return pl.pallas_call(
        functools.partial(finish_kernel, blocks),
        in_specs=[SMEM] + [VMEM] * (blocks + len(apart)) + [anywhere],
        out_specs=anywhere,
        out_shape=jax.ShapeDtypeStruct((per_ref, SPLIT * tile), F32),
        scratch_shapes=[
            pltpu.VMEM((masks, SPLIT * tile), F32),
            pltpu.VMEM((SPLIT, per_ref, tile), F32),
            pltpu.SemaphoreType.DMA,
            pltpu.SemaphoreType.DMA((SPLIT,)),
        ],
        cost_estimate=cost(0, 8 * per_ref * SPLIT * tile),
        name="finish",
    )(place, *shares, *apart, wedge)


GRP = ("lay", "core")


def passed(values, axis, size):
    return [values[0]] + [
        lax.ppermute(values[p], axis, [(d, d ^ p) for d in range(size)]) for p in range(1, size)
    ]


def per_device(slab, pick_owner, pick_offset, wedge_id, live_count, references, wedge):
    slot_count, voxels = slab.shape
    masks = wedge.shape[0]
    layers = lax.axis_size("lay")
    groups = 2 * layers
    blocks = lax.axis_size("blk")
    per_vox = voxels // groups
    tile = per_vox // SPLIT
    keep = per_vox - tile
    half = voxels // 2
    cap = 2 * slot_count
    block = lax.axis_index("blk").astype(jnp.int32)
    core = lax.axis_index("core").astype(jnp.int32)
    layer = lax.axis_index("lay").astype(jnp.int32)
    place = jnp.stack([core, layer * 2 + core, layer, block])

    low, high, aside = cut(place, references, slab, layers, per_vox)
    mate = lax.ppermute(aside, "core", [(0, 1), (1, 0)])
    if blocks == 4:
        over_x, over_y = [(b, b ^ 1) for b in range(4)], [(b, b ^ 2) for b in range(4)]
        low_x = lax.ppermute(low, "blk", over_x)
        high_y = lax.ppermute(high, "blk", over_y)
        high_x = lax.ppermute(high, "blk", over_x)
        low_y = lax.ppermute(low, "blk", over_y)
        low_xy = lax.ppermute(low_x, "blk", over_y)
        high_xy = lax.ppermute(high_y, "blk", over_x)
        tables = [[low, low_x, low_y, low_xy], [high, high_x, high_y, high_xy]]
    else:
        tables = [passed([s] * blocks, "blk", blocks) for s in (low, high)]
    far = deal(place, slab, mate, layers, keep)
    pieces = [None] * layers
    for p in range(1, layers):
        pieces[p] = lax.ppermute(far[p - 1], "lay", [(z, z ^ p) for z in range(layers)])
    note = brief(
        live_count,
        references,
        wedge,
        pick_owner.reshape(1, slot_count),
        pick_offset.reshape(1, slot_count),
        wedge_id.reshape(1, slot_count),
        2 * per_vox,
    )
    notes = passed([note] * blocks, "blk", blocks)
    listed = lists_of(place, notes, cap)
    pair = jnp.stack(passed([listed] * 2, "core", 2))

    scaled = select(
        place,
        [slab, mate],
        [
            pl.BlockSpec((slot_count, per_vox), lambda t, s: (0, 2 * t + s[0])),
            pl.BlockSpec((slot_count, per_vox), lambda t, s: (0, t)),
        ],
        [pair],
        wedge,
        pl.BlockSpec((masks, per_vox), lambda t, s: (0, 2 * t + s[0])),
        slot_count,
        per_vox,
        layers,
    )
    here = pl.BlockSpec((masks, per_vox), lambda t, s: (0, s[1]))
    near_rows = select(
        place,
        [slab, mate],
        [
            pl.BlockSpec((slot_count, per_vox), lambda t, s: (0, s[1])),
            pl.BlockSpec((slot_count, per_vox), lambda t, s: (0, s[2])),
        ],
        [pair],
        wedge,
        here,
        slot_count,
        keep // 2,
        2,
    )
    pairs = passed([pair] * layers, "lay", layers)
    sums = correl(scaled, tables, half // 4)
    got = lax.ppermute(sums, "core", [(0, 1), (1, 0)])
    weights = weigh(sums, got, pair, notes, masks, 1.0 / (32.0 * math.sqrt(voxels)))
    all_weights = passed([weights] * layers, "lay", layers)

    far_rows = select(
        place,
        pieces[1:],
        [pl.BlockSpec((2 * slot_count, keep // 2), lambda t, s: (0, t))] * (layers - 1),
        pairs[1:],
        wedge,
        here,
        slot_count,
        keep // 2,
        2,
    )

    apart = blend(
        place,
        all_weights[:1],
        [],
        [scaled],
        masks,
        blocks,
        tile,
        layers,
        lambda t, s: (0, (s[2] ^ t) * SPLIT + SPLIT - 1),
    )
    apart = passed(apart, "blk", blocks)
    apart = fold(apart)
    apart = passed(apart, "lay", layers)

    shares = blend(
        place,
        all_weights,
        pairs,
        [near_rows, far_rows],
        masks,
        blocks,
        keep // 2,
        2,
        lambda t, s: (0, jnp.minimum(t, 1)),
    )
    shares = passed(shares, "blk", blocks)
    return finish(place, shares, apart, wedge, tile)


def solution(mesh):
    groups, blocks = mesh.shape["grp"], mesh.shape["blk"]
    fine = Mesh(mesh.devices.reshape(groups // 2, 2, blocks), ("lay", "core", "blk"))
    every = ("lay", "core", "blk")
    placed = (P(every, None), P(every, None), P(every), P(every), P(every), P("blk", None), P())

    return jax.shard_map(
        per_device, mesh=fine, in_specs=placed, out_specs=P("blk", GRP), check_vma=False
    )
```

```python
import functools
import math

import jax
import jax.numpy as jnp
from jax import lax
from jax.experimental import pallas as pl
from jax.experimental.pallas import tpu as pltpu
from jax.sharding import Mesh
from jax.sharding import PartitionSpec as P

F32 = jnp.float32
BF16 = jnp.bfloat16
ROWS = (((1,), (0,)), ((), ()))
LANES = (((1,), (1,)), ((), ()))
VMEM = pl.BlockSpec(memory_space=pltpu.VMEM)
SMEM = pl.BlockSpec(memory_space=pltpu.SMEM)
HBM = pl.BlockSpec(memory_space=pltpu.HBM)
SPLIT = 4


def dot(left, right, dims=ROWS):
    return lax.dot_general(left, right, dims, preferred_element_type=F32)


def pieces_of(value, count):
    parts = []
    for _ in range(count):
        part = value.astype(BF16)
        value = value - part.astype(F32)
        parts.append(part)
    return parts


def iota(shape, axis):
    return lax.broadcasted_iota(jnp.int32, shape, axis).astype(F32)


def hot(mask):
    return mask.astype(F32).astype(BF16)


def room(mebibytes):
    return pltpu.CompilerParams(vmem_limit_bytes=mebibytes << 20)


def cost(flops, moved):
    return pl.CostEstimate(flops=int(flops), bytes_accessed=int(moved), transcendentals=0)


def cut_kernel(place, refs, slab, *rest):
    outs, came = rest[:3], rest[3]
    layers = came.shape[1]
    per_vox = outs[2].shape[1] // layers
    core = place[0]
    copies = []
    for which, out in enumerate(outs):
        source, side = (slab, 1 - core) if which == 2 else (refs, core)
        first = layers // 2 if which == 1 else 0
        for z in range(out.shape[1] // per_vox):
            at = pl.multiple_of((2 * (first + z) + side) * per_vox, per_vox)
            copy = pltpu.make_async_copy(
                source.at[:, pl.ds(at, per_vox)],
                out.at[:, pl.ds(z * per_vox, per_vox)],
                came.at[which, z],
            )
            copy.start()
            copies.append(copy)
    for copy in copies:
        copy.wait()


def cut(place, refs, slab, layers, per_vox):
    shapes = [
        (layers // 2, refs.shape[0]),
        (layers // 2, refs.shape[0]),
        (layers, slab.shape[0]),
    ]
    return pl.pallas_call(
        cut_kernel,
        in_specs=[SMEM, HBM, HBM],
        out_specs=[VMEM] * 3,
        out_shape=[jax.ShapeDtypeStruct((r, n * per_vox), BF16) for n, r in shapes],
        scratch_shapes=[pltpu.SemaphoreType.DMA((3, layers))],
        compiler_params=room(16),
        cost_estimate=cost(0, 4 * sum(n * r for n, r in shapes) * per_vox),
        name="cut",
    )(place, refs, slab)


def deal_kernel(place, slab, mate, *rest):
    outs, came = rest[:-1], rest[-1]
    rows = slab.shape[0]
    keep = outs[0].shape[1]
    per_vox = mate.shape[1] // (len(outs) + 1)
    copies = []
    for p, out in enumerate(outs):
        layer = place[2] ^ (p + 1)
        mine = pl.multiple_of((2 * layer + place[0]) * per_vox, per_vox)
        theirs = pl.multiple_of(layer * per_vox, per_vox)
        copies += [
            pltpu.make_async_copy(
                slab.at[:, pl.ds(mine, keep)], out.at[pl.ds(0, rows)], came.at[p, 0]
            ),
            pltpu.make_async_copy(
                mate.at[:, pl.ds(theirs, keep)], out.at[pl.ds(rows, rows)], came.at[p, 1]
            ),
        ]
    for copy in copies:
        copy.start()
    for copy in copies:
        copy.wait()


def deal(place, slab, mate, layers, keep):
    rows = slab.shape[0]
    anywhere = pl.BlockSpec(memory_space=pl.ANY)
    peers = layers - 1
    return pl.pallas_call(
        deal_kernel,
        in_specs=[SMEM, HBM, anywhere],
        out_specs=[VMEM] * peers,
        out_shape=[jax.ShapeDtypeStruct((2 * rows, keep), BF16)] * peers,
        scratch_shapes=[pltpu.SemaphoreType.DMA((peers, 2))],
        compiler_params=room(16),
        cost_estimate=cost(0, 8 * rows * peers * keep),
        name="deal",
    )(place, slab, mate)


def brief_kernel(live, refs, wedge, owner, offset, wedge_id, out, sums):
    masks = wedge.shape[0]
    per_ref = refs.shape[0]
    slots = owner.shape[1]

    @pl.when(pl.program_id(0) == 0)
    def _():
        sums[...] = jnp.zeros_like(sums)

    wide = refs[...].astype(F32)
    high, low = pieces_of(wide * wide, 2)
    lined = jnp.concatenate(pieces_of(wedge[...], 3), axis=0)
    sums[...] += dot(lined, high, LANES) + dot(lined, low, LANES)

    @pl.when(pl.program_id(0) == pl.num_programs(0) - 1)
    def _():
        out[...] = jnp.zeros_like(out)
        out[0:1, :] = jnp.full((1, out.shape[1]), -1.0, F32)
        out[0:1, :slots] = owner[...].astype(F32)
        out[1:2, :slots] = offset[...].astype(F32)
        out[2:3, :slots] = wedge_id[...].astype(F32)
        out[3:4, :slots] = (iota((1, slots), 1) < live[0].astype(F32)).astype(F32)
        out[8 : 8 + masks, :per_ref] = (
            sums[:masks] + sums[masks : 2 * masks] + sums[2 * masks : 3 * masks]
        )


def brief(live, refs, wedge, owner, offset, wedge_id, tile):
    per_ref, voxels = refs.shape
    masks = wedge.shape[0]
    slots = owner.shape[1]
    height = -(-(8 + masks) // 8) * 8
    row = pl.BlockSpec((1, slots), lambda t, s: (0, 0))
    return pl.pallas_call(
        brief_kernel,
        grid_spec=pltpu.PrefetchScalarGridSpec(
            num_scalar_prefetch=1,
            grid=(voxels // tile,),
            in_specs=[
                pl.BlockSpec((per_ref, tile), lambda t, s: (0, t)),
                pl.BlockSpec((masks, tile), lambda t, s: (0, t)),
                row,
                row,
                row,
            ],
            out_specs=pl.BlockSpec((height, 128), lambda t, s: (0, 0)),
            scratch_shapes=[pltpu.VMEM((3 * masks, per_ref), F32)],
        ),
        out_shape=jax.ShapeDtypeStruct((height, 128), F32),
        cost_estimate=cost(12 * masks * per_ref * voxels, 2 * voxels * (per_ref + 2 * masks)),
        compiler_params=room(16),
        name="brief",
    )(live, refs, wedge, owner, offset, wedge_id)


def lists_kernel(place, *rest):
    notes, out = rest[:-1], rest[-1]
    cap = out.shape[1]
    slots = notes[0].shape[1]
    earlier = hot(iota((slots, slots), 0) < iota((slots, slots), 1))
    before = jnp.zeros((1, 1), F32)
    total = jnp.zeros(out.shape, F32)
    for note in notes:
        info = note[0:4, :]
        named = jnp.logical_and(info[0:1] == place[3].astype(F32), info[3:4] > 0.0)
        chosen = named.astype(F32)
        rank = dot(jnp.broadcast_to(chosen, (8, slots)).astype(BF16), earlier)[0:1] + before
        order = hot(jnp.logical_and(iota((cap, slots), 0) == rank, named))
        listed = jnp.concatenate(
            [info[1:2] * chosen, info[2:3] * chosen, chosen, jnp.zeros((5, slots), F32)], axis=0
        )
        total = total + dot(listed.astype(BF16), order, LANES)
        before = before + jnp.sum(chosen, axis=1, keepdims=True)
    out[...] = total


def lists_of(place, notes, cap):
    return pl.pallas_call(
        lists_kernel,
        in_specs=[SMEM] + [VMEM] * len(notes),
        out_specs=VMEM,
        out_shape=jax.ShapeDtypeStruct((8, cap), F32),
        cost_estimate=cost(1 << 22, 1 << 18),
        compiler_params=room(8),
        name="lists",
    )(place, *notes)


def columns_of(listed):
    cap = listed.shape[1]
    eye = hot(iota((cap, cap), 0) == iota((cap, cap), 1))
    return dot(eye, listed.astype(BF16), LANES)


def select_kernel(sources, place, *rest):
    blocks, pairs, wedge, out = rest[:sources], rest[sources:-4], rest[-4], rest[-3]
    rows_hot, wedge_hot = rest[-2:]
    bunches, height, depth = rows_hot.shape
    count = 2 * len(pairs)
    cap = wedge_hot.shape[0] // count
    bunch = height // cap
    rows = depth // bunch
    masks = wedge.shape[0]

    @pl.when(pl.program_id(0) == 0)
    def _():
        rows_hot[...] = jnp.zeros_like(rows_hot)
        for g in range(count):
            columns = columns_of(pairs[g // 2][g % 2])
            n, at = g // bunch, g % bunch
            rows_hot[n, at * cap : (at + 1) * cap, at * rows : (at + 1) * rows] = hot(
                iota((cap, rows), 1) == columns[:, 0:1]
            )
            marks = (iota((cap, masks), 1) == columns[:, 1:2]).astype(F32)
            wedge_hot[g * cap : (g + 1) * cap, :] = jnp.concatenate([marks] * 3, axis=1).astype(
                BF16
            )

    tile = out.shape[1] // pl.num_programs(0)
    at = pl.multiple_of(pl.program_id(0) * tile, 128)

    def part_of(ref):
        if ref.shape[1] == tile:
            return ref[...]
        return ref[:, pl.ds(at, tile)]

    lined = jnp.concatenate(pieces_of(part_of(wedge), 3), axis=0)
    weights = dot(wedge_hot[...], lined)
    taken = 0
    for n in range(bunches):
        stack, have = [], 0
        while have < depth:
            stack.append(part_of(blocks[taken]))
            have += blocks[taken].shape[0]
            taken += 1
        values = dot(rows_hot[n], jnp.concatenate(stack, axis=0) if len(stack) > 1 else stack[0])
        part = slice(n * height, (n + 1) * height)
        out[part, pl.ds(at, tile)] = (weights[part] * values).astype(BF16)


def select(place, blocks, block_specs, pairs, wedge, wedge_spec, rows, tile, steps):
    count = 2 * len(pairs)
    cap = pairs[0].shape[2]
    masks = wedge.shape[0]
    bunch = max(n for n in (2, 4) if count % n == 0 and n * rows <= 256)
    return pl.pallas_call(
        functools.partial(select_kernel, len(blocks)),
        grid_spec=pltpu.PrefetchScalarGridSpec(
            num_scalar_prefetch=1,
            grid=(steps,),
            in_specs=[
                *block_specs,
                *[pl.BlockSpec((2, 8, cap), lambda t, s: (0, 0, 0))] * len(pairs),
                wedge_spec,
            ],
            out_specs=VMEM,
            scratch_shapes=[
                pltpu.VMEM((count // bunch, bunch * cap, bunch * rows), BF16),
                pltpu.VMEM((count * cap, 3 * masks), BF16),
            ],
        ),
        out_shape=jax.ShapeDtypeStruct((count * cap, steps * tile), BF16),
        cost_estimate=cost(
            4 * count * cap * 256 * steps * tile, 2 * count * (cap + rows) * steps * tile
        ),
        compiler_params=room(32),
        name="select",
    )(place, *blocks, *pairs, wedge)


def correl_kernel(blocks, tile, scaled, *rest):
    refs, out, table = rest[:-2], rest[-2], rest[-1]
    per_ref, span = refs[0].shape
    out[...] = jnp.zeros_like(out)
    for side in range(2):

        def step(t, carry, side=side):
            at = pl.multiple_of(t * tile, tile)
            for p in range(blocks):
                table[p * per_ref : (p + 1) * per_ref, :] = refs[2 * p + side][:, pl.ds(at, tile)]
            rows = scaled[:, pl.ds(pl.multiple_of(side * span + t * tile, tile), tile)]
            out[...] += dot(rows, table[...], LANES)
            return carry

        lax.fori_loop(0, span // tile, step, 0)


def correl(scaled, tables, tile):
    height, span = scaled.shape
    blocks = len(tables[0])
    count = blocks * tables[0][0].shape[0]
    refs = [tables[i][p] for p in range(blocks) for i in range(2)]
    return pl.pallas_call(
        functools.partial(correl_kernel, blocks, tile),
        in_specs=[VMEM] * (1 + len(refs)),
        out_specs=VMEM,
        out_shape=jax.ShapeDtypeStruct((height, count), F32),
        scratch_shapes=[pltpu.VMEM((count, tile), BF16)],
        compiler_params=room(24),
        cost_estimate=cost(2 * height * count * span, 2 * span * (height + count)),
        name="correl",
    )(scaled, *refs)


def weigh_kernel(scale, masks, own, got, pair, *rest):
    notes, out = rest[:-1], rest[-1]
    count, cap = out.shape[1], out.shape[2]
    per_ref = count // len(notes)
    lanes = notes[0].shape[1]
    norms = jnp.zeros((3 * masks, count), F32)
    for p, note in enumerate(notes):
        parts = jnp.concatenate(pieces_of(note[8 : 8 + masks, :], 3), axis=0)
        shifted = hot(
            jnp.logical_and(
                iota((lanes, count), 0) + float(p * per_ref) == iota((lanes, count), 1),
                iota((lanes, count), 0) < float(per_ref),
            )
        )
        norms = norms + dot(parts, shifted)
    norms = norms.astype(BF16)
    for side in range(2):
        columns = columns_of(pair[side])
        marks = (iota((cap, masks), 1) == columns[:, 1:2]).astype(F32)
        wedge_hot = jnp.concatenate([marks] * 3, axis=1).astype(BF16)
        mine = own[side * cap : (side + 1) * cap, :] + got[(1 - side) * cap : (2 - side) * cap, :]
        score = (mine - 0.5 * dot(wedge_hot, norms)) * scale
        score = jnp.exp(score - jnp.max(score, axis=1, keepdims=True))
        share = score / jnp.sum(score, axis=1, keepdims=True) * columns[:, 2:3]
        out[side] = share.T.astype(BF16)


def weigh(own, got, pair, notes, masks, scale):
    cap, count = own.shape[0] // 2, own.shape[1]
    return pl.pallas_call(
        functools.partial(weigh_kernel, scale, masks),
        in_specs=[VMEM] * (3 + len(notes)),
        out_specs=VMEM,
        out_shape=jax.ShapeDtypeStruct((2, count, cap), BF16),
        cost_estimate=cost(1 << 24, 1 << 18),
        compiler_params=room(16),
        name="weigh",
    )(own, got, pair, *notes)


def blend_kernel(layers, parts, blocks, masks, starts, place, *rest):
    weights, rest = rest[:layers], rest[layers:]
    scaled, pairs = rest[:parts], rest[parts : -blocks - 1]
    outs, turned = rest[-blocks - 1 : -1], rest[-1]
    cap = weights[0].shape[2]
    per_ref, tile = outs[0].shape[1:] if not pairs else (outs[0].shape[0], starts[1])
    for g in range(2 * layers):
        turned[:, g * cap : (g + 1) * cap] = weights[g // 2][g % 2]

    def mix(at):
        first, sums = 0, 0.0
        for part in scaled:
            height = part.shape[0]
            sums = sums + dot(turned[:, first : first + height], part[:, pl.ds(at, tile)])
            first += height
        return sums.astype(BF16)

    if pairs:

        def step(t, carry):
            at = pl.multiple_of(t * tile, tile)
            sums = mix(at)
            for p, out in enumerate(outs):
                out[:, pl.ds(at, tile)] = sums[p * per_ref : (p + 1) * per_ref, :]
            return carry

        lax.fori_loop(0, starts[0], step, 0)
        total = jnp.zeros((turned.shape[0], masks), F32)
        for g in range(2 * layers):
            marks = hot(iota((masks, cap), 0) == pairs[g // 2][g % 2, 1:2, :])
            total = total + dot(turned[:, g * cap : (g + 1) * cap], marks, LANES)
        split = jnp.concatenate(pieces_of(total, 3), axis=1)
        split = jnp.concatenate(
            [split, jnp.zeros((split.shape[0], 128 - split.shape[1]), BF16)], axis=1
        )
        for p, out in enumerate(outs):
            out[:, starts[0] * tile :] = split[p * per_ref : (p + 1) * per_ref, :]
    else:
        stretch = scaled[0].shape[1] // starts[0]

        def step(t, carry):
            sums = mix(pl.multiple_of((place[2] ^ t) * stretch + stretch - tile, 128))
            for p, out in enumerate(outs):
                out[t] = sums[p * per_ref : (p + 1) * per_ref, :]
            return carry

        lax.fori_loop(0, starts[0], step, 0)


def blend(place, weights, pairs, scaled, masks, blocks, tile, steps):
    layers = len(weights)
    _, count, cap = weights[0].shape
    per_ref = count // blocks
    shape = (per_ref, steps * tile + 128) if pairs else (steps, per_ref, tile)
    return pl.pallas_call(
        functools.partial(blend_kernel, layers, len(scaled), blocks, masks, (steps, tile)),
        in_specs=[SMEM] + [VMEM] * (layers + len(scaled) + len(pairs)),
        out_specs=[VMEM] * blocks,
        out_shape=[jax.ShapeDtypeStruct(shape, BF16)] * blocks,
        scratch_shapes=[pltpu.VMEM((count, 2 * layers * cap), BF16)],
        compiler_params=room(24),
        cost_estimate=cost(
            4 * layers * cap * count * steps * tile, 2 * (2 * layers * cap + count) * steps * tile
        ),
        name="blend",
    )(place, *weights, *scaled, *pairs)


def fold_kernel(parts, *refs):
    sources, outs = refs[:parts], refs[parts:]
    for t, out in enumerate(outs):
        total = sources[0][t].astype(F32)
        for source in sources[1:]:
            total = total + source[t].astype(F32)
        out[...] = total.astype(BF16)


def fold(parts):
    layers, per_ref, tile = parts[0].shape
    return pl.pallas_call(
        functools.partial(fold_kernel, len(parts)),
        in_specs=[VMEM] * len(parts),
        out_specs=[VMEM] * layers,
        out_shape=[jax.ShapeDtypeStruct((per_ref, tile), BF16)] * layers,
        cost_estimate=cost(0, 2 * (len(parts) + 1) * layers * per_ref * tile),
        compiler_params=room(16),
        name="fold",
    )(*parts)


def finish_kernel(blocks, place, *rest):
    shares, apart = rest[:blocks], rest[blocks:-6]
    wedge, out, tables, held, came, went = rest[-6:]
    masks = wedge.shape[0]
    span = tables.shape[1]
    tile = held.shape[2]
    at = pl.multiple_of(place[1] * span, span)
    fetch = pltpu.make_async_copy(wedge.at[:, pl.ds(at, span)], tables, came)
    fetch.start()
    keep = span - tile
    mass = 0.0
    for part in shares:
        mass = mass + part[:, keep : keep + 3 * masks].astype(F32)
    mass = mass[:, :masks] + mass[:, masks : 2 * masks] + mass[:, 2 * masks : 3 * masks]
    fetch.wait()
    leaves = []
    for t in range(SPLIT):
        cols = slice(t * tile, (t + 1) * tile)
        below = jnp.ones(held.shape[1:], F32)
        for w in range(masks):
            below = below + mass[:, w : w + 1] * tables[w : w + 1, cols]
        total = 0.0
        for part in shares if t < SPLIT - 1 else apart:
            total = total + (part[:, cols] if t < SPLIT - 1 else part[...]).astype(F32)
        held[t] = total / below
        leave = pltpu.make_async_copy(held.at[t], out.at[:, pl.ds(t * tile, tile)], went.at[t])
        leave.start()
        leaves.append(leave)
    for leave in leaves:
        leave.wait()


def finish(place, shares, apart, wedge, tile):
    per_ref = shares[0].shape[0]
    masks = wedge.shape[0]
    blocks = len(shares)
    return pl.pallas_call(
        functools.partial(finish_kernel, blocks),
        in_specs=[SMEM] + [VMEM] * (blocks + len(apart)) + [HBM],
        out_specs=HBM,
        out_shape=jax.ShapeDtypeStruct((per_ref, SPLIT * tile), F32),
        scratch_shapes=[
            pltpu.VMEM((masks, SPLIT * tile), F32),
            pltpu.VMEM((SPLIT, per_ref, tile), F32),
            pltpu.SemaphoreType.DMA,
            pltpu.SemaphoreType.DMA((SPLIT,)),
        ],
        cost_estimate=cost(0, 8 * per_ref * SPLIT * tile),
        compiler_params=room(16),
        name="finish",
    )(place, *shares, *apart, wedge)


GRP = ("lay", "core")


def passed(values, axis, size):
    return [values[0]] + [
        lax.ppermute(values[p], axis, [(d, d ^ p) for d in range(size)]) for p in range(1, size)
    ]


def per_device(slab, pick_owner, pick_offset, wedge_id, live_count, references, wedge):
    slot_count, voxels = slab.shape
    masks = wedge.shape[0]
    layers = lax.axis_size("lay")
    groups = 2 * layers
    blocks = lax.axis_size("blk")
    per_vox = voxels // groups
    tile = per_vox // SPLIT
    keep = per_vox - tile
    half = voxels // 2
    cap = 2 * slot_count
    block = lax.axis_index("blk").astype(jnp.int32)
    core = lax.axis_index("core").astype(jnp.int32)
    layer = lax.axis_index("lay").astype(jnp.int32)
    place = jnp.stack([core, layer * 2 + core, layer, block])

    low, high, aside = cut(place, references, slab, layers, per_vox)
    mate = lax.ppermute(aside, "core", [(0, 1), (1, 0)])
    if blocks == 4:
        over_x, over_y = [(b, b ^ 1) for b in range(4)], [(b, b ^ 2) for b in range(4)]
        low_x = lax.ppermute(low, "blk", over_x)
        high_y = lax.ppermute(high, "blk", over_y)
        high_x = lax.ppermute(high, "blk", over_x)
        low_y = lax.ppermute(low, "blk", over_y)
        low_xy = lax.ppermute(low_x, "blk", over_y)
        high_xy = lax.ppermute(high_y, "blk", over_x)
        tables = [[low, low_x, low_y, low_xy], [high, high_x, high_y, high_xy]]
    else:
        tables = [passed([s] * blocks, "blk", blocks) for s in (low, high)]
    far = deal(place, slab, mate, layers, keep)
    pieces = [None] * layers
    for p in range(1, layers):
        pieces[p] = lax.ppermute(far[p - 1], "lay", [(z, z ^ p) for z in range(layers)])
    note = brief(
        live_count,
        references,
        wedge,
        pick_owner.reshape(1, slot_count),
        pick_offset.reshape(1, slot_count),
        wedge_id.reshape(1, slot_count),
        2 * per_vox,
    )
    notes = passed([note] * blocks, "blk", blocks)
    listed = lists_of(place, notes, cap)
    pair = jnp.stack(passed([listed] * 2, "core", 2))

    scaled = select(
        place,
        [slab, mate],
        [
            pl.BlockSpec((slot_count, per_vox), lambda t, s: (0, 2 * t + s[0])),
            pl.BlockSpec((slot_count, per_vox), lambda t, s: (0, t)),
        ],
        [pair],
        wedge,
        pl.BlockSpec((masks, per_vox), lambda t, s: (0, 2 * t + s[0])),
        slot_count,
        per_vox,
        layers,
    )
    here = pl.BlockSpec((masks, per_vox), lambda t, s: (0, s[1]))
    near_rows = select(
        place,
        [slab, mate],
        [
            pl.BlockSpec((slot_count, per_vox), lambda t, s: (0, s[1])),
            pl.BlockSpec((slot_count, per_vox), lambda t, s: (0, s[2])),
        ],
        [pair],
        wedge,
        here,
        slot_count,
        keep // 2,
        2,
    )
    pairs = passed([pair] * layers, "lay", layers)
    sums = correl(scaled, tables, half // 8)
    got = lax.ppermute(sums, "core", [(0, 1), (1, 0)])
    weights = weigh(sums, got, pair, notes, masks, 1.0 / (32.0 * math.sqrt(voxels)))
    all_weights = passed([weights] * layers, "lay", layers)

    far_rows = select(
        place,
        pieces[1:],
        [VMEM] * (layers - 1),
        pairs[1:],
        wedge,
        here,
        slot_count,
        keep // 2,
        2,
    )

    apart = blend(place, all_weights[:1], [], [scaled], masks, blocks, tile, layers)
    apart = passed(apart, "blk", blocks)
    apart = fold(apart)
    apart = passed(apart, "lay", layers)

    shares = blend(
        place, all_weights, pairs, [near_rows, far_rows], masks, blocks, keep // 4, 4
    )
    shares = passed(shares, "blk", blocks)
    return finish(place, shares, apart, wedge, tile)


def solution(mesh):
    groups, blocks = mesh.shape["grp"], mesh.shape["blk"]
    fine = Mesh(mesh.devices.reshape(groups // 2, 2, blocks), ("lay", "core", "blk"))
    every = ("lay", "core", "blk")
    placed = (P(every, None), P(every, None), P(every), P(every), P(every), P("blk", None), P())

    return jax.shard_map(
        per_device, mesh=fine, in_specs=placed, out_specs=P("blk", GRP), check_vma=False
    )
```

```python
import functools
import math

import jax
import jax.numpy as jnp
from jax import lax
from jax.experimental import pallas as pl
from jax.experimental.pallas import tpu as pltpu
from jax.sharding import Mesh
from jax.sharding import PartitionSpec as P

F32 = jnp.float32
BF16 = jnp.bfloat16
ROWS = (((1,), (0,)), ((), ()))
LANES = (((1,), (1,)), ((), ()))
VMEM = pl.BlockSpec(memory_space=pltpu.VMEM)
SMEM = pl.BlockSpec(memory_space=pltpu.SMEM)
HBM = pl.BlockSpec(memory_space=pltpu.HBM)
SPLIT = 4


def dot(left, right, dims=ROWS):
    return lax.dot_general(left, right, dims, preferred_element_type=F32)


def pieces_of(value, count):
    parts = []
    for _ in range(count):
        part = value.astype(BF16)
        value = value - part.astype(F32)
        parts.append(part)
    return parts


def iota(shape, axis):
    return lax.broadcasted_iota(jnp.int32, shape, axis).astype(F32)


def hot(mask):
    return mask.astype(F32).astype(BF16)


def room(mebibytes):
    return pltpu.CompilerParams(vmem_limit_bytes=mebibytes << 20)


def cost(flops, moved):
    return pl.CostEstimate(flops=int(flops), bytes_accessed=int(moved), transcendentals=0)


def cut_kernel(place, refs, slab, *rest):
    outs, came = rest[:3], rest[3]
    layers = came.shape[1]
    per_vox = outs[2].shape[1] // layers
    core = place[0]
    copies = []
    for which, out in enumerate(outs):
        source, side = (slab, 1 - core) if which == 2 else (refs, core)
        first = layers // 2 if which == 1 else 0
        for z in range(out.shape[1] // per_vox):
            at = pl.multiple_of((2 * (first + z) + side) * per_vox, per_vox)
            copy = pltpu.make_async_copy(
                source.at[:, pl.ds(at, per_vox)],
                out.at[:, pl.ds(z * per_vox, per_vox)],
                came.at[which, z],
            )
            copy.start()
            copies.append(copy)
    for copy in copies:
        copy.wait()


def cut(place, refs, slab, layers, per_vox):
    shapes = [
        (layers // 2, refs.shape[0]),
        (layers // 2, refs.shape[0]),
        (layers, slab.shape[0]),
    ]
    return pl.pallas_call(
        cut_kernel,
        in_specs=[SMEM, HBM, HBM],
        out_specs=[VMEM] * 3,
        out_shape=[jax.ShapeDtypeStruct((r, n * per_vox), BF16) for n, r in shapes],
        scratch_shapes=[pltpu.SemaphoreType.DMA((3, layers))],
        compiler_params=room(16),
        cost_estimate=cost(0, 4 * sum(n * r for n, r in shapes) * per_vox),
        name="cut",
    )(place, refs, slab)


def deal_kernel(place, slab, mate, *rest):
    outs, came = rest[:-1], rest[-1]
    rows = slab.shape[0]
    keep = outs[0].shape[1]
    per_vox = mate.shape[1] // (len(outs) + 1)
    copies = []
    for p, out in enumerate(outs):
        layer = place[2] ^ (p + 1)
        mine = pl.multiple_of((2 * layer + place[0]) * per_vox, per_vox)
        theirs = pl.multiple_of(layer * per_vox, per_vox)
        copies += [
            pltpu.make_async_copy(
                slab.at[:, pl.ds(mine, keep)], out.at[pl.ds(0, rows)], came.at[p, 0]
            ),
            pltpu.make_async_copy(
                mate.at[:, pl.ds(theirs, keep)], out.at[pl.ds(rows, rows)], came.at[p, 1]
            ),
        ]
    for copy in copies:
        copy.start()
    for copy in copies:
        copy.wait()


def deal(place, slab, mate, layers, keep):
    rows = slab.shape[0]
    anywhere = pl.BlockSpec(memory_space=pl.ANY)
    peers = layers - 1
    return pl.pallas_call(
        deal_kernel,
        in_specs=[SMEM, HBM, anywhere],
        out_specs=[VMEM] * peers,
        out_shape=[jax.ShapeDtypeStruct((2 * rows, keep), BF16)] * peers,
        scratch_shapes=[pltpu.SemaphoreType.DMA((peers, 2))],
        compiler_params=room(16),
        cost_estimate=cost(0, 8 * rows * peers * keep),
        name="deal",
    )(place, slab, mate)


def brief_kernel(live, refs, wedge, owner, offset, wedge_id, out, sums):
    masks = wedge.shape[0]
    per_ref = refs.shape[0]
    slots = owner.shape[1]

    @pl.when(pl.program_id(0) == 0)
    def _():
        sums[...] = jnp.zeros_like(sums)

    wide = refs[...].astype(F32)
    high, low = pieces_of(wide * wide, 2)
    lined = jnp.concatenate(pieces_of(wedge[...], 3), axis=0)
    sums[...] += dot(lined, high, LANES) + dot(lined, low, LANES)

    @pl.when(pl.program_id(0) == pl.num_programs(0) - 1)
    def _():
        out[...] = jnp.zeros_like(out)
        out[0:1, :] = jnp.full((1, out.shape[1]), -1.0, F32)
        out[0:1, :slots] = owner[...].astype(F32)
        out[1:2, :slots] = offset[...].astype(F32)
        out[2:3, :slots] = wedge_id[...].astype(F32)
        out[3:4, :slots] = (iota((1, slots), 1) < live[0].astype(F32)).astype(F32)
        out[8 : 8 + masks, :per_ref] = (
            sums[:masks] + sums[masks : 2 * masks] + sums[2 * masks : 3 * masks]
        )


def brief(live, refs, wedge, owner, offset, wedge_id, tile):
    per_ref, voxels = refs.shape
    masks = wedge.shape[0]
    slots = owner.shape[1]
    height = -(-(8 + masks) // 8) * 8
    row = pl.BlockSpec((1, slots), lambda t, s: (0, 0))
    return pl.pallas_call(
        brief_kernel,
        grid_spec=pltpu.PrefetchScalarGridSpec(
            num_scalar_prefetch=1,
            grid=(voxels // tile,),
            in_specs=[
                pl.BlockSpec((per_ref, tile), lambda t, s: (0, t)),
                pl.BlockSpec((masks, tile), lambda t, s: (0, t)),
                row,
                row,
                row,
            ],
            out_specs=pl.BlockSpec((height, 128), lambda t, s: (0, 0)),
            scratch_shapes=[pltpu.VMEM((3 * masks, per_ref), F32)],
        ),
        out_shape=jax.ShapeDtypeStruct((height, 128), F32),
        cost_estimate=cost(12 * masks * per_ref * voxels, 2 * voxels * (per_ref + 2 * masks)),
        compiler_params=room(16),
        name="brief",
    )(live, refs, wedge, owner, offset, wedge_id)


def lists_kernel(place, *rest):
    notes, out = rest[:-1], rest[-1]
    cap = out.shape[1]
    slots = notes[0].shape[1]
    earlier = hot(iota((slots, slots), 0) < iota((slots, slots), 1))
    before = jnp.zeros((1, 1), F32)
    total = jnp.zeros(out.shape, F32)
    for note in notes:
        info = note[0:4, :]
        named = jnp.logical_and(info[0:1] == place[3].astype(F32), info[3:4] > 0.0)
        chosen = named.astype(F32)
        rank = dot(jnp.broadcast_to(chosen, (8, slots)).astype(BF16), earlier)[0:1] + before
        order = hot(jnp.logical_and(iota((cap, slots), 0) == rank, named))
        listed = jnp.concatenate(
            [info[1:2] * chosen, info[2:3] * chosen, chosen, jnp.zeros((5, slots), F32)], axis=0
        )
        total = total + dot(listed.astype(BF16), order, LANES)
        before = before + jnp.sum(chosen, axis=1, keepdims=True)
    out[...] = total


def lists_of(place, notes, cap):
    return pl.pallas_call(
        lists_kernel,
        in_specs=[SMEM] + [VMEM] * len(notes),
        out_specs=VMEM,
        out_shape=jax.ShapeDtypeStruct((8, cap), F32),
        cost_estimate=cost(1 << 22, 1 << 18),
        compiler_params=room(8),
        name="lists",
    )(place, *notes)


def columns_of(listed):
    cap = listed.shape[1]
    eye = hot(iota((cap, cap), 0) == iota((cap, cap), 1))
    return dot(eye, listed.astype(BF16), LANES)


def select_kernel(sources, place, *rest):
    blocks, pairs, wedge, out = rest[:sources], rest[sources:-4], rest[-4], rest[-3]
    rows_hot, wedge_hot = rest[-2:]
    bunches, height, depth = rows_hot.shape
    count = 2 * len(pairs)
    cap = wedge_hot.shape[0] // count
    bunch = height // cap
    rows = depth // bunch
    masks = wedge.shape[0]

    @pl.when(pl.program_id(0) == 0)
    def _():
        rows_hot[...] = jnp.zeros_like(rows_hot)
        for g in range(count):
            columns = columns_of(pairs[g // 2][g % 2])
            n, at = g // bunch, g % bunch
            rows_hot[n, at * cap : (at + 1) * cap, at * rows : (at + 1) * rows] = hot(
                iota((cap, rows), 1) == columns[:, 0:1]
            )
            marks = (iota((cap, masks), 1) == columns[:, 1:2]).astype(F32)
            wedge_hot[g * cap : (g + 1) * cap, :] = jnp.concatenate([marks] * 3, axis=1).astype(
                BF16
            )

    tile = out.shape[1] // pl.num_programs(0)
    at = pl.multiple_of(pl.program_id(0) * tile, 128)

    def part_of(ref):
        if ref.shape[1] == tile:
            return ref[...]
        return ref[:, pl.ds(at, tile)]

    lined = jnp.concatenate(pieces_of(part_of(wedge), 3), axis=0)
    weights = dot(wedge_hot[...], lined)
    taken = 0
    for n in range(bunches):
        stack, have = [], 0
        while have < depth:
            stack.append(part_of(blocks[taken]))
            have += blocks[taken].shape[0]
            taken += 1
        values = dot(rows_hot[n], jnp.concatenate(stack, axis=0) if len(stack) > 1 else stack[0])
        part = slice(n * height, (n + 1) * height)
        out[part, pl.ds(at, tile)] = (weights[part] * values).astype(BF16)


def select(place, blocks, block_specs, pairs, wedge, wedge_spec, rows, tile, steps):
    count = 2 * len(pairs)
    cap = pairs[0].shape[2]
    masks = wedge.shape[0]
    bunch = max(n for n in (2, 4) if count % n == 0 and n * rows <= 256)
    return pl.pallas_call(
        functools.partial(select_kernel, len(blocks)),
        grid_spec=pltpu.PrefetchScalarGridSpec(
            num_scalar_prefetch=1,
            grid=(steps,),
            in_specs=[
                *block_specs,
                *[pl.BlockSpec((2, 8, cap), lambda t, s: (0, 0, 0))] * len(pairs),
                wedge_spec,
            ],
            out_specs=VMEM,
            scratch_shapes=[
                pltpu.VMEM((count // bunch, bunch * cap, bunch * rows), BF16),
                pltpu.VMEM((count * cap, 3 * masks), BF16),
            ],
        ),
        out_shape=jax.ShapeDtypeStruct((count * cap, steps * tile), BF16),
        cost_estimate=cost(
            4 * count * cap * 256 * steps * tile, 2 * count * (cap + rows) * steps * tile
        ),
        compiler_params=room(32),
        name="select",
    )(place, *blocks, *pairs, wedge)


def correl_kernel(blocks, tile, scaled, *rest):
    refs, out, table = rest[:-2], rest[-2], rest[-1]
    per_ref, span = refs[0].shape
    out[...] = jnp.zeros_like(out)
    for side in range(2):

        def step(t, carry, side=side):
            at = pl.multiple_of(t * tile, tile)
            for p in range(blocks):
                table[p * per_ref : (p + 1) * per_ref, :] = refs[2 * p + side][:, pl.ds(at, tile)]
            rows = scaled[:, pl.ds(pl.multiple_of(side * span + t * tile, tile), tile)]
            out[...] += dot(rows, table[...], LANES)
            return carry

        lax.fori_loop(0, span // tile, step, 0)


def correl(scaled, tables, tile):
    height, span = scaled.shape
    blocks = len(tables[0])
    count = blocks * tables[0][0].shape[0]
    refs = [tables[i][p] for p in range(blocks) for i in range(2)]
    return pl.pallas_call(
        functools.partial(correl_kernel, blocks, tile),
        in_specs=[VMEM] * (1 + len(refs)),
        out_specs=VMEM,
        out_shape=jax.ShapeDtypeStruct((height, count), F32),
        scratch_shapes=[pltpu.VMEM((count, tile), BF16)],
        compiler_params=room(24),
        cost_estimate=cost(2 * height * count * span, 2 * span * (height + count)),
        name="correl",
    )(scaled, *refs)


def weigh_kernel(scale, masks, own, got, pair, *rest):
    notes, out = rest[:-1], rest[-1]
    count, cap = out.shape[1], out.shape[2]
    per_ref = count // len(notes)
    lanes = notes[0].shape[1]
    norms = jnp.zeros((3 * masks, count), F32)
    for p, note in enumerate(notes):
        parts = jnp.concatenate(pieces_of(note[8 : 8 + masks, :], 3), axis=0)
        shifted = hot(
            jnp.logical_and(
                iota((lanes, count), 0) + float(p * per_ref) == iota((lanes, count), 1),
                iota((lanes, count), 0) < float(per_ref),
            )
        )
        norms = norms + dot(parts, shifted)
    norms = norms.astype(BF16)
    for side in range(2):
        columns = columns_of(pair[side])
        marks = (iota((cap, masks), 1) == columns[:, 1:2]).astype(F32)
        wedge_hot = jnp.concatenate([marks] * 3, axis=1).astype(BF16)
        mine = own[side * cap : (side + 1) * cap, :] + got[(1 - side) * cap : (2 - side) * cap, :]
        score = (mine - 0.5 * dot(wedge_hot, norms)) * scale
        score = jnp.exp(score - jnp.max(score, axis=1, keepdims=True))
        share = score / jnp.sum(score, axis=1, keepdims=True) * columns[:, 2:3]
        out[side] = share.T.astype(BF16)


def weigh(own, got, pair, notes, masks, scale):
    cap, count = own.shape[0] // 2, own.shape[1]
    return pl.pallas_call(
        functools.partial(weigh_kernel, scale, masks),
        in_specs=[VMEM] * (3 + len(notes)),
        out_specs=VMEM,
        out_shape=jax.ShapeDtypeStruct((2, count, cap), BF16),
        cost_estimate=cost(1 << 24, 1 << 18),
        compiler_params=room(16),
        name="weigh",
    )(own, got, pair, *notes)


def blend_kernel(layers, parts, blocks, masks, starts, place, *rest):
    weights, rest = rest[:layers], rest[layers:]
    scaled, pairs = rest[:parts], rest[parts : -blocks - 1]
    outs, turned = rest[-blocks - 1 : -1], rest[-1]
    cap = weights[0].shape[2]
    per_ref, tile = outs[0].shape[1:] if not pairs else (outs[0].shape[0], starts[1])
    for g in range(2 * layers):
        turned[:, g * cap : (g + 1) * cap] = weights[g // 2][g % 2]

    def mix(at):
        first, sums = 0, 0.0
        for part in scaled:
            height = part.shape[0]
            sums = sums + dot(turned[:, first : first + height], part[:, pl.ds(at, tile)])
            first += height
        return sums.astype(BF16)

    if pairs:

        def step(t, carry):
            at = pl.multiple_of(t * tile, tile)
            sums = mix(at)
            for p, out in enumerate(outs):
                out[:, pl.ds(at, tile)] = sums[p * per_ref : (p + 1) * per_ref, :]
            return carry

        lax.fori_loop(0, starts[0], step, 0)
        total = jnp.zeros((turned.shape[0], masks), F32)
        for g in range(2 * layers):
            marks = hot(iota((masks, cap), 0) == pairs[g // 2][g % 2, 1:2, :])
            total = total + dot(turned[:, g * cap : (g + 1) * cap], marks, LANES)
        split = jnp.concatenate(pieces_of(total, 3), axis=1)
        split = jnp.concatenate(
            [split, jnp.zeros((split.shape[0], 128 - split.shape[1]), BF16)], axis=1
        )
        for p, out in enumerate(outs):
            out[:, starts[0] * tile :] = split[p * per_ref : (p + 1) * per_ref, :]
    else:
        stretch = scaled[0].shape[1] // starts[0]

        def step(t, carry):
            sums = mix(pl.multiple_of((place[2] ^ t) * stretch + stretch - tile, 128))
            for p, out in enumerate(outs):
                out[t] = sums[p * per_ref : (p + 1) * per_ref, :]
            return carry

        lax.fori_loop(0, starts[0], step, 0)


def blend(place, weights, pairs, scaled, masks, blocks, tile, steps):
    layers = len(weights)
    _, count, cap = weights[0].shape
    per_ref = count // blocks
    shape = (per_ref, steps * tile + 128) if pairs else (steps, per_ref, tile)
    return pl.pallas_call(
        functools.partial(blend_kernel, layers, len(scaled), blocks, masks, (steps, tile)),
        in_specs=[SMEM] + [VMEM] * (layers + len(scaled) + len(pairs)),
        out_specs=[VMEM] * blocks,
        out_shape=[jax.ShapeDtypeStruct(shape, BF16)] * blocks,
        scratch_shapes=[pltpu.VMEM((count, 2 * layers * cap), BF16)],
        compiler_params=room(24),
        cost_estimate=cost(
            4 * layers * cap * count * steps * tile, 2 * (2 * layers * cap + count) * steps * tile
        ),
        name="blend",
    )(place, *weights, *scaled, *pairs)


def fold_kernel(parts, *refs):
    sources, outs = refs[:parts], refs[parts:]
    for t, out in enumerate(outs):
        total = sources[0][t].astype(F32)
        for source in sources[1:]:
            total = total + source[t].astype(F32)
        out[...] = total.astype(BF16)


def fold(parts):
    layers, per_ref, tile = parts[0].shape
    return pl.pallas_call(
        functools.partial(fold_kernel, len(parts)),
        in_specs=[VMEM] * len(parts),
        out_specs=[VMEM] * layers,
        out_shape=[jax.ShapeDtypeStruct((per_ref, tile), BF16)] * layers,
        cost_estimate=cost(0, 2 * (len(parts) + 1) * layers * per_ref * tile),
        compiler_params=room(16),
        name="fold",
    )(*parts)


def finish_kernel(blocks, place, *rest):
    shares, apart = rest[:blocks], rest[blocks:-6]
    wedge, out, tables, held, came, went = rest[-6:]
    masks = wedge.shape[0]
    span = tables.shape[1]
    tile = held.shape[2]
    at = pl.multiple_of(place[1] * span, span)
    fetch = pltpu.make_async_copy(wedge.at[:, pl.ds(at, span)], tables, came)
    fetch.start()
    keep = span - tile
    mass = 0.0
    for part in shares:
        mass = mass + part[:, keep : keep + 3 * masks].astype(F32)
    mass = mass[:, :masks] + mass[:, masks : 2 * masks] + mass[:, 2 * masks : 3 * masks]
    fetch.wait()
    leaves = []
    for t in range(SPLIT):
        cols = slice(t * tile, (t + 1) * tile)
        below = jnp.ones(held.shape[1:], F32)
        for w in range(masks):
            below = below + mass[:, w : w + 1] * tables[w : w + 1, cols]
        total = 0.0
        for part in shares if t < SPLIT - 1 else apart:
            total = total + (part[:, cols] if t < SPLIT - 1 else part[...]).astype(F32)
        held[t] = total / below
        leave = pltpu.make_async_copy(held.at[t], out.at[:, pl.ds(t * tile, tile)], went.at[t])
        leave.start()
        leaves.append(leave)
    for leave in leaves:
        leave.wait()


def finish(place, shares, apart, wedge, tile):
    per_ref = shares[0].shape[0]
    masks = wedge.shape[0]
    blocks = len(shares)
    return pl.pallas_call(
        functools.partial(finish_kernel, blocks),
        in_specs=[SMEM] + [VMEM] * (blocks + len(apart)) + [HBM],
        out_specs=HBM,
        out_shape=jax.ShapeDtypeStruct((per_ref, SPLIT * tile), F32),
        scratch_shapes=[
            pltpu.VMEM((masks, SPLIT * tile), F32),
            pltpu.VMEM((SPLIT, per_ref, tile), F32),
            pltpu.SemaphoreType.DMA,
            pltpu.SemaphoreType.DMA((SPLIT,)),
        ],
        cost_estimate=cost(0, 8 * per_ref * SPLIT * tile),
        compiler_params=room(16),
        name="finish",
    )(place, *shares, *apart, wedge)


GRP = ("lay", "core")


def passed(values, axis, size):
    return [values[0]] + [
        lax.ppermute(values[p], axis, [(d, d ^ p) for d in range(size)]) for p in range(1, size)
    ]


def per_device(slab, pick_owner, pick_offset, wedge_id, live_count, references, wedge):
    slot_count, voxels = slab.shape
    masks = wedge.shape[0]
    layers = lax.axis_size("lay")
    groups = 2 * layers
    blocks = lax.axis_size("blk")
    per_vox = voxels // groups
    tile = per_vox // SPLIT
    keep = per_vox - tile
    half = voxels // 2
    cap = 2 * slot_count
    block = lax.axis_index("blk").astype(jnp.int32)
    core = lax.axis_index("core").astype(jnp.int32)
    layer = lax.axis_index("lay").astype(jnp.int32)
    place = jnp.stack([core, layer * 2 + core, layer, block])

    slab_hbm, refs_hbm = (
        pltpu.with_memory_space_constraint(value, pltpu.HBM) for value in (slab, references)
    )
    low, high, aside = cut(place, refs_hbm, slab_hbm, layers, per_vox)
    mate = lax.ppermute(aside, "core", [(0, 1), (1, 0)])
    if blocks == 4:
        over_x, over_y = [(b, b ^ 1) for b in range(4)], [(b, b ^ 2) for b in range(4)]
        low_x = lax.ppermute(low, "blk", over_x)
        high_y = lax.ppermute(high, "blk", over_y)
        high_x = lax.ppermute(high, "blk", over_x)
        low_y = lax.ppermute(low, "blk", over_y)
        low_xy = lax.ppermute(low_x, "blk", over_y)
        high_xy = lax.ppermute(high_y, "blk", over_x)
        tables = [[low, low_x, low_y, low_xy], [high, high_x, high_y, high_xy]]
    else:
        tables = [passed([s] * blocks, "blk", blocks) for s in (low, high)]
    far = deal(place, slab_hbm, mate, layers, keep)
    pieces = [None] * layers
    for p in range(1, layers):
        pieces[p] = lax.ppermute(far[p - 1], "lay", [(z, z ^ p) for z in range(layers)])
    note = brief(
        live_count,
        references,
        wedge,
        pick_owner.reshape(1, slot_count),
        pick_offset.reshape(1, slot_count),
        wedge_id.reshape(1, slot_count),
        2 * per_vox,
    )
    notes = passed([note] * blocks, "blk", blocks)
    listed = lists_of(place, notes, cap)
    pair = jnp.stack(passed([listed] * 2, "core", 2))

    scaled = select(
        place,
        [slab, mate],
        [
            pl.BlockSpec((slot_count, per_vox), lambda t, s: (0, 2 * t + s[0])),
            pl.BlockSpec((slot_count, per_vox), lambda t, s: (0, t)),
        ],
        [pair],
        wedge,
        pl.BlockSpec((masks, per_vox), lambda t, s: (0, 2 * t + s[0])),
        slot_count,
        per_vox,
        layers,
    )
    here = pl.BlockSpec((masks, per_vox), lambda t, s: (0, s[1]))
    near_rows = select(
        place,
        [slab, mate],
        [
            pl.BlockSpec((slot_count, per_vox), lambda t, s: (0, s[1])),
            pl.BlockSpec((slot_count, per_vox), lambda t, s: (0, s[2])),
        ],
        [pair],
        wedge,
        here,
        slot_count,
        keep // 2,
        2,
    )
    pairs = passed([pair] * layers, "lay", layers)
    sums = correl(scaled, tables, half // 8)
    got = lax.ppermute(sums, "core", [(0, 1), (1, 0)])
    weights = weigh(sums, got, pair, notes, masks, 1.0 / (32.0 * math.sqrt(voxels)))
    all_weights = passed([weights] * layers, "lay", layers)

    far_rows = select(
        place,
        pieces[1:],
        [VMEM] * (layers - 1),
        pairs[1:],
        wedge,
        here,
        slot_count,
        keep // 2,
        2,
    )

    apart = blend(place, all_weights[:1], [], [scaled], masks, blocks, tile, layers)
    apart = passed(apart, "blk", blocks)
    apart = fold(apart)
    apart = passed(apart, "lay", layers)

    shares = blend(
        place, all_weights, pairs, [near_rows, far_rows], masks, blocks, keep // 4, 4
    )
    shares = passed(shares, "blk", blocks)
    return finish(place, shares, apart, wedge, tile)


def solution(mesh):
    groups, blocks = mesh.shape["grp"], mesh.shape["blk"]
    fine = Mesh(mesh.devices.reshape(groups // 2, 2, blocks), ("lay", "core", "blk"))
    every = ("lay", "core", "blk")
    placed = (P(every, None), P(every, None), P(every), P(every), P(every), P("blk", None), P())

    return jax.shard_map(
        per_device, mesh=fine, in_specs=placed, out_specs=P("blk", GRP), check_vma=False
    )
```

```python
import functools
import math

import jax
import jax.numpy as jnp
from jax import lax
from jax.experimental import pallas as pl
from jax.experimental.pallas import tpu as pltpu
from jax.sharding import Mesh
from jax.sharding import PartitionSpec as P

F32 = jnp.float32
BF16 = jnp.bfloat16
ROWS = (((1,), (0,)), ((), ()))
LANES = (((1,), (1,)), ((), ()))
VMEM = pl.BlockSpec(memory_space=pltpu.VMEM)
SMEM = pl.BlockSpec(memory_space=pltpu.SMEM)
HBM = pl.BlockSpec(memory_space=pltpu.HBM)
APART = (5, 16)


def dot(left, right, dims=ROWS):
    return lax.dot_general(left, right, dims, preferred_element_type=F32)


def pieces_of(value, count):
    parts = []
    for _ in range(count):
        part = value.astype(BF16)
        value = value - part.astype(F32)
        parts.append(part)
    return parts


def iota(shape, axis):
    return lax.broadcasted_iota(jnp.int32, shape, axis).astype(F32)


def hot(mask):
    return mask.astype(F32).astype(BF16)


def room(mebibytes):
    return pltpu.CompilerParams(vmem_limit_bytes=mebibytes << 20)


def cost(flops, moved):
    return pl.CostEstimate(flops=int(flops), bytes_accessed=int(moved), transcendentals=0)


def cut_kernel(place, refs, slab, *rest):
    outs, came = rest[:3], rest[3]
    layers = came.shape[1]
    per_vox = outs[2].shape[1] // layers
    core = place[0]
    copies = []
    for which, out in enumerate(outs):
        source, side = (slab, 1 - core) if which == 2 else (refs, core)
        first = layers // 2 if which == 1 else 0
        for z in range(out.shape[1] // per_vox):
            at = pl.multiple_of((2 * (first + z) + side) * per_vox, per_vox)
            copy = pltpu.make_async_copy(
                source.at[:, pl.ds(at, per_vox)],
                out.at[:, pl.ds(z * per_vox, per_vox)],
                came.at[which, z],
            )
            copy.start()
            copies.append(copy)
    for copy in copies:
        copy.wait()


def cut(place, refs, slab, layers, per_vox):
    shapes = [
        (layers // 2, refs.shape[0]),
        (layers // 2, refs.shape[0]),
        (layers, slab.shape[0]),
    ]
    return pl.pallas_call(
        cut_kernel,
        in_specs=[SMEM, HBM, HBM],
        out_specs=[VMEM] * 3,
        out_shape=[jax.ShapeDtypeStruct((r, n * per_vox), BF16) for n, r in shapes],
        scratch_shapes=[pltpu.SemaphoreType.DMA((3, layers))],
        compiler_params=room(16),
        cost_estimate=cost(0, 4 * sum(n * r for n, r in shapes) * per_vox),
        name="cut",
    )(place, refs, slab)


def deal_kernel(place, slab, mate, *rest):
    outs, came = rest[:-1], rest[-1]
    rows = slab.shape[0]
    keep = outs[0].shape[1]
    per_vox = mate.shape[1] // (len(outs) + 1)
    copies = []
    for p, out in enumerate(outs):
        layer = place[2] ^ (p + 1)
        mine = pl.multiple_of((2 * layer + place[0]) * per_vox, per_vox)
        theirs = pl.multiple_of(layer * per_vox, per_vox)
        copies += [
            pltpu.make_async_copy(
                slab.at[:, pl.ds(mine, keep)], out.at[pl.ds(0, rows)], came.at[p, 0]
            ),
            pltpu.make_async_copy(
                mate.at[:, pl.ds(theirs, keep)], out.at[pl.ds(rows, rows)], came.at[p, 1]
            ),
        ]
    for copy in copies:
        copy.start()
    for copy in copies:
        copy.wait()


def deal(place, slab, mate, layers, keep):
    rows = slab.shape[0]
    anywhere = pl.BlockSpec(memory_space=pl.ANY)
    peers = layers - 1
    return pl.pallas_call(
        deal_kernel,
        in_specs=[SMEM, HBM, anywhere],
        out_specs=[VMEM] * peers,
        out_shape=[jax.ShapeDtypeStruct((2 * rows, keep), BF16)] * peers,
        scratch_shapes=[pltpu.SemaphoreType.DMA((peers, 2))],
        compiler_params=room(16),
        cost_estimate=cost(0, 8 * rows * peers * keep),
        name="deal",
    )(place, slab, mate)


def brief_kernel(live, refs, wedge, owner, offset, wedge_id, out, sums):
    masks = wedge.shape[0]
    per_ref = refs.shape[0]
    slots = owner.shape[1]

    @pl.when(pl.program_id(0) == 0)
    def _():
        sums[...] = jnp.zeros_like(sums)

    wide = refs[...].astype(F32)
    high, low = pieces_of(wide * wide, 2)
    lined = jnp.concatenate(pieces_of(wedge[...], 3), axis=0)
    sums[...] += dot(lined, high, LANES) + dot(lined, low, LANES)

    @pl.when(pl.program_id(0) == pl.num_programs(0) - 1)
    def _():
        out[...] = jnp.zeros_like(out)
        out[0:1, :] = jnp.full((1, out.shape[1]), -1.0, F32)
        out[0:1, :slots] = owner[...].astype(F32)
        out[1:2, :slots] = offset[...].astype(F32)
        out[2:3, :slots] = wedge_id[...].astype(F32)
        out[3:4, :slots] = (iota((1, slots), 1) < live[0].astype(F32)).astype(F32)
        out[8 : 8 + masks, :per_ref] = (
            sums[:masks] + sums[masks : 2 * masks] + sums[2 * masks : 3 * masks]
        )


def brief(live, refs, wedge, owner, offset, wedge_id, tile):
    per_ref, voxels = refs.shape
    masks = wedge.shape[0]
    slots = owner.shape[1]
    height = -(-(8 + masks) // 8) * 8
    row = pl.BlockSpec((1, slots), lambda t, s: (0, 0))
    return pl.pallas_call(
        brief_kernel,
        grid_spec=pltpu.PrefetchScalarGridSpec(
            num_scalar_prefetch=1,
            grid=(voxels // tile,),
            in_specs=[
                pl.BlockSpec((per_ref, tile), lambda t, s: (0, t)),
                pl.BlockSpec((masks, tile), lambda t, s: (0, t)),
                row,
                row,
                row,
            ],
            out_specs=pl.BlockSpec((height, 128), lambda t, s: (0, 0)),
            scratch_shapes=[pltpu.VMEM((3 * masks, per_ref), F32)],
        ),
        out_shape=jax.ShapeDtypeStruct((height, 128), F32),
        cost_estimate=cost(12 * masks * per_ref * voxels, 2 * voxels * (per_ref + 2 * masks)),
        compiler_params=room(16),
        name="brief",
    )(live, refs, wedge, owner, offset, wedge_id)


def lists_kernel(place, *rest):
    notes, out = rest[:-1], rest[-1]
    cap = out.shape[1]
    slots = notes[0].shape[1]
    earlier = hot(iota((slots, slots), 0) < iota((slots, slots), 1))
    before = jnp.zeros((1, 1), F32)
    total = jnp.zeros(out.shape, F32)
    for note in notes:
        info = note[0:4, :]
        named = jnp.logical_and(info[0:1] == place[3].astype(F32), info[3:4] > 0.0)
        chosen = named.astype(F32)
        rank = dot(jnp.broadcast_to(chosen, (8, slots)).astype(BF16), earlier)[0:1] + before
        order = hot(jnp.logical_and(iota((cap, slots), 0) == rank, named))
        listed = jnp.concatenate(
            [info[1:2] * chosen, info[2:3] * chosen, chosen, jnp.zeros((5, slots), F32)], axis=0
        )
        total = total + dot(listed.astype(BF16), order, LANES)
        before = before + jnp.sum(chosen, axis=1, keepdims=True)
    out[...] = total


def lists_of(place, notes, cap):
    return pl.pallas_call(
        lists_kernel,
        in_specs=[SMEM] + [VMEM] * len(notes),
        out_specs=VMEM,
        out_shape=jax.ShapeDtypeStruct((8, cap), F32),
        cost_estimate=cost(1 << 22, 1 << 18),
        compiler_params=room(8),
        name="lists",
    )(place, *notes)


def columns_of(listed):
    cap = listed.shape[1]
    eye = hot(iota((cap, cap), 0) == iota((cap, cap), 1))
    return dot(eye, listed.astype(BF16), LANES)


def select_kernel(sources, place, *rest):
    blocks, pairs, wedge, out = rest[:sources], rest[sources:-4], rest[-4], rest[-3]
    rows_hot, wedge_hot = rest[-2:]
    bunches, height, depth = rows_hot.shape
    count = 2 * len(pairs)
    cap = wedge_hot.shape[0] // count
    bunch = height // cap
    rows = depth // bunch
    masks = wedge.shape[0]

    @pl.when(pl.program_id(0) == 0)
    def _():
        rows_hot[...] = jnp.zeros_like(rows_hot)
        for g in range(count):
            columns = columns_of(pairs[g // 2][g % 2])
            n, at = g // bunch, g % bunch
            rows_hot[n, at * cap : (at + 1) * cap, at * rows : (at + 1) * rows] = hot(
                iota((cap, rows), 1) == columns[:, 0:1]
            )
            marks = (iota((cap, masks), 1) == columns[:, 1:2]).astype(F32)
            wedge_hot[g * cap : (g + 1) * cap, :] = jnp.concatenate([marks] * 3, axis=1).astype(
                BF16
            )

    tile = out.shape[1] // pl.num_programs(0)
    at = pl.multiple_of(pl.program_id(0) * tile, 128)

    def part_of(ref):
        if ref.shape[1] == tile:
            return ref[...]
        return ref[:, pl.ds(at, tile)]

    lined = jnp.concatenate(pieces_of(part_of(wedge), 3), axis=0)
    weights = dot(wedge_hot[...], lined)
    taken = 0
    for n in range(bunches):
        stack, have = [], 0
        while have < depth:
            stack.append(part_of(blocks[taken]))
            have += blocks[taken].shape[0]
            taken += 1
        values = dot(rows_hot[n], jnp.concatenate(stack, axis=0) if len(stack) > 1 else stack[0])
        part = slice(n * height, (n + 1) * height)
        out[part, pl.ds(at, tile)] = (weights[part] * values).astype(BF16)


def select(place, blocks, block_specs, pairs, wedge, wedge_spec, rows, tile, steps):
    count = 2 * len(pairs)
    cap = pairs[0].shape[2]
    masks = wedge.shape[0]
    bunch = max(n for n in (2, 4) if count % n == 0 and n * rows <= 256)
    return pl.pallas_call(
        functools.partial(select_kernel, len(blocks)),
        grid_spec=pltpu.PrefetchScalarGridSpec(
            num_scalar_prefetch=1,
            grid=(steps,),
            in_specs=[
                *block_specs,
                *[pl.BlockSpec((2, 8, cap), lambda t, s: (0, 0, 0))] * len(pairs),
                wedge_spec,
            ],
            out_specs=VMEM,
            scratch_shapes=[
                pltpu.VMEM((count // bunch, bunch * cap, bunch * rows), BF16),
                pltpu.VMEM((count * cap, 3 * masks), BF16),
            ],
        ),
        out_shape=jax.ShapeDtypeStruct((count * cap, steps * tile), BF16),
        cost_estimate=cost(
            4 * count * cap * 256 * steps * tile, 2 * count * (cap + rows) * steps * tile
        ),
        compiler_params=room(32),
        name="select",
    )(place, *blocks, *pairs, wedge)


def correl_kernel(blocks, tile, scaled, *rest):
    refs, out, table = rest[:-2], rest[-2], rest[-1]
    per_ref, span = refs[0].shape
    out[...] = jnp.zeros_like(out)
    for side in range(2):

        def step(t, carry, side=side):
            at = pl.multiple_of(t * tile, tile)
            for p in range(blocks):
                table[p * per_ref : (p + 1) * per_ref, :] = refs[2 * p + side][:, pl.ds(at, tile)]
            rows = scaled[:, pl.ds(pl.multiple_of(side * span + t * tile, tile), tile)]
            out[...] += dot(rows, table[...], LANES)
            return carry

        lax.fori_loop(0, span // tile, step, 0)


def correl(scaled, tables, tile):
    height, span = scaled.shape
    blocks = len(tables[0])
    count = blocks * tables[0][0].shape[0]
    refs = [tables[i][p] for p in range(blocks) for i in range(2)]
    return pl.pallas_call(
        functools.partial(correl_kernel, blocks, tile),
        in_specs=[VMEM] * (1 + len(refs)),
        out_specs=VMEM,
        out_shape=jax.ShapeDtypeStruct((height, count), F32),
        scratch_shapes=[pltpu.VMEM((count, tile), BF16)],
        compiler_params=room(24),
        cost_estimate=cost(2 * height * count * span, 2 * span * (height + count)),
        name="correl",
    )(scaled, *refs)


def weigh_kernel(scale, masks, own, got, pair, *rest):
    notes, out = rest[:-1], rest[-1]
    count, cap = out.shape[1], out.shape[2]
    per_ref = count // len(notes)
    lanes = notes[0].shape[1]
    norms = jnp.zeros((3 * masks, count), F32)
    for p, note in enumerate(notes):
        parts = jnp.concatenate(pieces_of(note[8 : 8 + masks, :], 3), axis=0)
        shifted = hot(
            jnp.logical_and(
                iota((lanes, count), 0) + float(p * per_ref) == iota((lanes, count), 1),
                iota((lanes, count), 0) < float(per_ref),
            )
        )
        norms = norms + dot(parts, shifted)
    norms = norms.astype(BF16)
    for side in range(2):
        columns = columns_of(pair[side])
        marks = (iota((cap, masks), 1) == columns[:, 1:2]).astype(F32)
        wedge_hot = jnp.concatenate([marks] * 3, axis=1).astype(BF16)
        mine = own[side * cap : (side + 1) * cap, :] + got[(1 - side) * cap : (2 - side) * cap, :]
        score = (mine - 0.5 * dot(wedge_hot, norms)) * scale
        score = jnp.exp(score - jnp.max(score, axis=1, keepdims=True))
        share = score / jnp.sum(score, axis=1, keepdims=True) * columns[:, 2:3]
        out[side] = share.T.astype(BF16)


def weigh(own, got, pair, notes, masks, scale):
    cap, count = own.shape[0] // 2, own.shape[1]
    return pl.pallas_call(
        functools.partial(weigh_kernel, scale, masks),
        in_specs=[VMEM] * (3 + len(notes)),
        out_specs=VMEM,
        out_shape=jax.ShapeDtypeStruct((2, count, cap), BF16),
        cost_estimate=cost(1 << 24, 1 << 18),
        compiler_params=room(16),
        name="weigh",
    )(own, got, pair, *notes)


def blend_kernel(layers, parts, blocks, masks, starts, place, *rest):
    weights, rest = rest[:layers], rest[layers:]
    scaled, pairs = rest[:parts], rest[parts : -blocks - 1]
    outs, turned = rest[-blocks - 1 : -1], rest[-1]
    cap = weights[0].shape[2]
    per_ref, tile = outs[0].shape[1:] if not pairs else (outs[0].shape[0], starts[1])
    for g in range(2 * layers):
        turned[:, g * cap : (g + 1) * cap] = weights[g // 2][g % 2]

    def mix(at):
        first, sums = 0, 0.0
        for part in scaled:
            height = part.shape[0]
            sums = sums + dot(turned[:, first : first + height], part[:, pl.ds(at, tile)])
            first += height
        return sums.astype(BF16)

    if pairs:

        def step(t, carry):
            at = pl.multiple_of(t * tile, tile)
            sums = mix(at)
            for p, out in enumerate(outs):
                out[:, pl.ds(at, tile)] = sums[p * per_ref : (p + 1) * per_ref, :]
            return carry

        lax.fori_loop(0, starts[0], step, 0)
        total = jnp.zeros((turned.shape[0], masks), F32)
        for g in range(2 * layers):
            marks = hot(iota((masks, cap), 0) == pairs[g // 2][g % 2, 1:2, :])
            total = total + dot(turned[:, g * cap : (g + 1) * cap], marks, LANES)
        split = jnp.concatenate(pieces_of(total, 3), axis=1)
        split = jnp.concatenate(
            [split, jnp.zeros((split.shape[0], 128 - split.shape[1]), BF16)], axis=1
        )
        for p, out in enumerate(outs):
            out[:, starts[0] * tile :] = split[p * per_ref : (p + 1) * per_ref, :]
    else:
        stretch = scaled[0].shape[1] // starts[0]

        def step(t, carry):
            sums = mix(pl.multiple_of((place[2] ^ t) * stretch + stretch - tile, 128))
            for p, out in enumerate(outs):
                out[t] = sums[p * per_ref : (p + 1) * per_ref, :]
            return carry

        lax.fori_loop(0, starts[0], step, 0)


def blend(place, weights, pairs, scaled, masks, blocks, tile, steps):
    layers = len(weights)
    _, count, cap = weights[0].shape
    per_ref = count // blocks
    shape = (per_ref, steps * tile + 128) if pairs else (steps, per_ref, tile)
    return pl.pallas_call(
        functools.partial(blend_kernel, layers, len(scaled), blocks, masks, (steps, tile)),
        in_specs=[SMEM] + [VMEM] * (layers + len(scaled) + len(pairs)),
        out_specs=[VMEM] * blocks,
        out_shape=[jax.ShapeDtypeStruct(shape, BF16)] * blocks,
        scratch_shapes=[pltpu.VMEM((count, 2 * layers * cap), BF16)],
        compiler_params=room(24),
        cost_estimate=cost(
            4 * layers * cap * count * steps * tile, 2 * (2 * layers * cap + count) * steps * tile
        ),
        name="blend",
    )(place, *weights, *scaled, *pairs)


def fold_kernel(parts, *refs):
    sources, outs = refs[:parts], refs[parts:]
    for t, out in enumerate(outs):
        total = sources[0][t].astype(F32)
        for source in sources[1:]:
            total = total + source[t].astype(F32)
        out[...] = total.astype(BF16)


def fold(parts):
    layers, per_ref, tile = parts[0].shape
    return pl.pallas_call(
        functools.partial(fold_kernel, len(parts)),
        in_specs=[VMEM] * len(parts),
        out_specs=[VMEM] * layers,
        out_shape=[jax.ShapeDtypeStruct((per_ref, tile), BF16)] * layers,
        cost_estimate=cost(0, 2 * (len(parts) + 1) * layers * per_ref * tile),
        compiler_params=room(16),
        name="fold",
    )(*parts)


def finish_kernel(blocks, place, *rest):
    shares, apart = rest[:blocks], rest[blocks:-6]
    wedge, out, tables, held, came, went = rest[-6:]
    masks = wedge.shape[0]
    span = tables.shape[1]
    keep = span - apart[0].shape[1]
    at = pl.multiple_of(place[1] * span, span)
    fetch = pltpu.make_async_copy(wedge.at[:, pl.ds(at, span)], tables, came)
    fetch.start()
    mass = 0.0
    for part in shares:
        mass = mass + part[:, keep : keep + 3 * masks].astype(F32)
    mass = mass[:, :masks] + mass[:, masks : 2 * masks] + mass[:, 2 * masks : 3 * masks]
    fetch.wait()
    leaves = []
    half = keep // 256 * 128
    for i, (first, end) in enumerate(((0, half), (half, keep), (keep, span))):
        below = jnp.ones((held.shape[0], end - first), F32)
        for w in range(masks):
            below = below + mass[:, w : w + 1] * tables[w : w + 1, first:end]
        total = 0.0
        for part in apart if i == 2 else shares:
            total = total + (part[...] if i == 2 else part[:, first:end]).astype(F32)
        held[:, first:end] = total / below
        leave = pltpu.make_async_copy(
            held.at[:, pl.ds(first, end - first)], out.at[:, pl.ds(first, end - first)], went.at[i]
        )
        leave.start()
        leaves.append(leave)
    for leave in leaves:
        leave.wait()


def finish(place, shares, apart, wedge, span):
    per_ref = shares[0].shape[0]
    masks = wedge.shape[0]
    blocks = len(shares)
    return pl.pallas_call(
        functools.partial(finish_kernel, blocks),
        in_specs=[SMEM] + [VMEM] * (blocks + len(apart)) + [HBM],
        out_specs=HBM,
        out_shape=jax.ShapeDtypeStruct((per_ref, span), F32),
        scratch_shapes=[
            pltpu.VMEM((masks, span), F32),
            pltpu.VMEM((per_ref, span), F32),
            pltpu.SemaphoreType.DMA,
            pltpu.SemaphoreType.DMA((3,)),
        ],
        compiler_params=room(16),
        cost_estimate=cost(0, 8 * per_ref * span),
        name="finish",
    )(place, *shares, *apart, wedge)


GRP = ("lay", "core")


def passed(values, axis, size):
    return [values[0]] + [
        lax.ppermute(values[p], axis, [(d, d ^ p) for d in range(size)]) for p in range(1, size)
    ]


def per_device(slab, pick_owner, pick_offset, wedge_id, live_count, references, wedge):
    slot_count, voxels = slab.shape
    masks = wedge.shape[0]
    layers = lax.axis_size("lay")
    groups = 2 * layers
    blocks = lax.axis_size("blk")
    per_vox = voxels // groups
    tile = per_vox * APART[0] // APART[1]
    keep = per_vox - tile
    steps = 2 if keep % 256 == 0 else 1
    half = voxels // 2
    cap = 2 * slot_count
    block = lax.axis_index("blk").astype(jnp.int32)
    core = lax.axis_index("core").astype(jnp.int32)
    layer = lax.axis_index("lay").astype(jnp.int32)
    place = jnp.stack([core, layer * 2 + core, layer, block])

    slab_hbm, refs_hbm = (
        pltpu.with_memory_space_constraint(value, pltpu.HBM) for value in (slab, references)
    )
    low, high, aside = cut(place, refs_hbm, slab_hbm, layers, per_vox)
    mate = lax.ppermute(aside, "core", [(0, 1), (1, 0)])
    if blocks == 4:
        over_x, over_y = [(b, b ^ 1) for b in range(4)], [(b, b ^ 2) for b in range(4)]
        low_x = lax.ppermute(low, "blk", over_x)
        high_y = lax.ppermute(high, "blk", over_y)
        high_x = lax.ppermute(high, "blk", over_x)
        low_y = lax.ppermute(low, "blk", over_y)
        low_xy = lax.ppermute(low_x, "blk", over_y)
        high_xy = lax.ppermute(high_y, "blk", over_x)
        tables = [[low, low_x, low_y, low_xy], [high, high_x, high_y, high_xy]]
    else:
        tables = [passed([s] * blocks, "blk", blocks) for s in (low, high)]
    far = deal(place, slab_hbm, mate, layers, keep)
    pieces = [None] * layers
    for p in range(1, layers):
        pieces[p] = lax.ppermute(far[p - 1], "lay", [(z, z ^ p) for z in range(layers)])
    note = brief(
        live_count,
        references,
        wedge,
        pick_owner.reshape(1, slot_count),
        pick_offset.reshape(1, slot_count),
        wedge_id.reshape(1, slot_count),
        2 * per_vox,
    )
    notes = passed([note] * blocks, "blk", blocks)
    listed = lists_of(place, notes, cap)
    pair = jnp.stack(passed([listed] * 2, "core", 2))

    scaled = select(
        place,
        [slab, mate],
        [
            pl.BlockSpec((slot_count, per_vox), lambda t, s: (0, 2 * t + s[0])),
            pl.BlockSpec((slot_count, per_vox), lambda t, s: (0, t)),
        ],
        [pair],
        wedge,
        pl.BlockSpec((masks, per_vox), lambda t, s: (0, 2 * t + s[0])),
        slot_count,
        per_vox,
        layers,
    )
    here = pl.BlockSpec((masks, per_vox), lambda t, s: (0, s[1]))
    near_rows = select(
        place,
        [slab, mate],
        [
            pl.BlockSpec((slot_count, per_vox), lambda t, s: (0, s[1])),
            pl.BlockSpec((slot_count, per_vox), lambda t, s: (0, s[2])),
        ],
        [pair],
        wedge,
        here,
        slot_count,
        keep // steps,
        steps,
    )
    pairs = passed([pair] * layers, "lay", layers)
    sums = correl(scaled, tables, half // 8)
    got = lax.ppermute(sums, "core", [(0, 1), (1, 0)])
    weights = weigh(sums, got, pair, notes, masks, 1.0 / (32.0 * math.sqrt(voxels)))
    all_weights = passed([weights] * layers, "lay", layers)

    far_rows = select(
        place,
        pieces[1:],
        [VMEM] * (layers - 1),
        pairs[1:],
        wedge,
        here,
        slot_count,
        keep // steps,
        steps,
    )

    apart = blend(place, all_weights[:1], [], [scaled], masks, blocks, tile, layers)
    apart = passed(apart, "blk", blocks)
    apart = fold(apart)
    apart = passed(apart, "lay", layers)

    shares = blend(
        place, all_weights, pairs, [near_rows, far_rows], masks, blocks, keep // steps, steps
    )
    shares = passed(shares, "blk", blocks)
    return finish(place, shares, apart, wedge, per_vox)


def solution(mesh):
    groups, blocks = mesh.shape["grp"], mesh.shape["blk"]
    fine = Mesh(mesh.devices.reshape(groups // 2, 2, blocks), ("lay", "core", "blk"))
    every = ("lay", "core", "blk")
    placed = (P(every, None), P(every, None), P(every), P(every), P(every), P("blk", None), P())

    return jax.shard_map(
        per_device, mesh=fine, in_specs=placed, out_specs=P("blk", GRP), check_vma=False
    )
```

```python
import functools
import math

import jax
import jax.numpy as jnp
from jax import lax
from jax.experimental import pallas as pl
from jax.experimental.pallas import tpu as pltpu
from jax.sharding import Mesh
from jax.sharding import PartitionSpec as P

F32 = jnp.float32
BF16 = jnp.bfloat16
ROWS = (((1,), (0,)), ((), ()))
LANES = (((1,), (1,)), ((), ()))
VMEM = pl.BlockSpec(memory_space=pltpu.VMEM)
SMEM = pl.BlockSpec(memory_space=pltpu.SMEM)
HBM = pl.BlockSpec(memory_space=pltpu.HBM)
APART = (5, 16)


def dot(left, right, dims=ROWS):
    return lax.dot_general(left, right, dims, preferred_element_type=F32)


def pieces_of(value, count):
    parts = []
    for _ in range(count):
        part = value.astype(BF16)
        value = value - part.astype(F32)
        parts.append(part)
    return parts


def iota(shape, axis):
    return lax.broadcasted_iota(jnp.int32, shape, axis).astype(F32)


def hot(mask):
    return mask.astype(F32).astype(BF16)


def room(mebibytes):
    return pltpu.CompilerParams(vmem_limit_bytes=mebibytes << 20)


def cost(flops, moved):
    return pl.CostEstimate(flops=int(flops), bytes_accessed=int(moved), transcendentals=0)


def cut_kernel(place, refs, slab, *rest):
    outs, came = rest[:3], rest[3]
    layers = came.shape[1]
    per_vox = outs[2].shape[1] // layers
    core = place[0]
    copies = []
    for which, out in enumerate(outs):
        source, side = (slab, 1 - core) if which == 2 else (refs, core)
        first = layers // 2 if which == 1 else 0
        for z in range(out.shape[1] // per_vox):
            at = pl.multiple_of((2 * (first + z) + side) * per_vox, per_vox)
            copy = pltpu.make_async_copy(
                source.at[:, pl.ds(at, per_vox)],
                out.at[:, pl.ds(z * per_vox, per_vox)],
                came.at[which, z],
            )
            copy.start()
            copies.append(copy)
    for copy in copies:
        copy.wait()


def cut(place, refs, slab, layers, per_vox):
    shapes = [
        (layers // 2, refs.shape[0]),
        (layers // 2, refs.shape[0]),
        (layers, slab.shape[0]),
    ]
    return pl.pallas_call(
        cut_kernel,
        in_specs=[SMEM, HBM, HBM],
        out_specs=[VMEM] * 3,
        out_shape=[jax.ShapeDtypeStruct((r, n * per_vox), BF16) for n, r in shapes],
        scratch_shapes=[pltpu.SemaphoreType.DMA((3, layers))],
        compiler_params=room(16),
        cost_estimate=cost(0, 4 * sum(n * r for n, r in shapes) * per_vox),
        name="cut",
    )(place, refs, slab)


def deal_kernel(place, slab, mate, *rest):
    outs, came = rest[:-1], rest[-1]
    rows = slab.shape[0]
    keep = outs[0].shape[1]
    per_vox = mate.shape[1] // (len(outs) + 1)
    copies = []
    for p, out in enumerate(outs):
        layer = place[2] ^ (p + 1)
        mine = pl.multiple_of((2 * layer + place[0]) * per_vox, per_vox)
        theirs = pl.multiple_of(layer * per_vox, per_vox)
        copies += [
            pltpu.make_async_copy(
                slab.at[:, pl.ds(mine, keep)], out.at[pl.ds(0, rows)], came.at[p, 0]
            ),
            pltpu.make_async_copy(
                mate.at[:, pl.ds(theirs, keep)], out.at[pl.ds(rows, rows)], came.at[p, 1]
            ),
        ]
    for copy in copies:
        copy.start()
    for copy in copies:
        copy.wait()


def deal(place, slab, mate, layers, keep):
    rows = slab.shape[0]
    anywhere = pl.BlockSpec(memory_space=pl.ANY)
    peers = layers - 1
    return pl.pallas_call(
        deal_kernel,
        in_specs=[SMEM, HBM, anywhere],
        out_specs=[VMEM] * peers,
        out_shape=[jax.ShapeDtypeStruct((2 * rows, keep), BF16)] * peers,
        scratch_shapes=[pltpu.SemaphoreType.DMA((peers, 2))],
        compiler_params=room(16),
        cost_estimate=cost(0, 8 * rows * peers * keep),
        name="deal",
    )(place, slab, mate)


def brief_kernel(live, refs, wedge, owner, offset, wedge_id, out, sums):
    masks = wedge.shape[0]
    per_ref = refs.shape[0]
    slots = owner.shape[1]

    @pl.when(pl.program_id(0) == 0)
    def _():
        sums[...] = jnp.zeros_like(sums)

    wide = refs[...].astype(F32)
    high, low = pieces_of(wide * wide, 2)
    lined = jnp.concatenate(pieces_of(wedge[...], 3), axis=0)
    sums[...] += dot(lined, high, LANES) + dot(lined, low, LANES)

    @pl.when(pl.program_id(0) == pl.num_programs(0) - 1)
    def _():
        out[...] = jnp.zeros_like(out)
        out[0:1, :] = jnp.full((1, out.shape[1]), -1.0, F32)
        out[0:1, :slots] = owner[...].astype(F32)
        out[1:2, :slots] = offset[...].astype(F32)
        out[2:3, :slots] = wedge_id[...].astype(F32)
        out[3:4, :slots] = (iota((1, slots), 1) < live[0].astype(F32)).astype(F32)
        out[8 : 8 + masks, :per_ref] = (
            sums[:masks] + sums[masks : 2 * masks] + sums[2 * masks : 3 * masks]
        )


def brief(live, refs, wedge, owner, offset, wedge_id, tile):
    per_ref, voxels = refs.shape
    masks = wedge.shape[0]
    slots = owner.shape[1]
    height = -(-(8 + masks) // 8) * 8
    row = pl.BlockSpec((1, slots), lambda t, s: (0, 0))
    return pl.pallas_call(
        brief_kernel,
        grid_spec=pltpu.PrefetchScalarGridSpec(
            num_scalar_prefetch=1,
            grid=(voxels // tile,),
            in_specs=[
                pl.BlockSpec((per_ref, tile), lambda t, s: (0, t)),
                pl.BlockSpec((masks, tile), lambda t, s: (0, t)),
                row,
                row,
                row,
            ],
            out_specs=pl.BlockSpec((height, 128), lambda t, s: (0, 0)),
            scratch_shapes=[pltpu.VMEM((3 * masks, per_ref), F32)],
        ),
        out_shape=jax.ShapeDtypeStruct((height, 128), F32),
        cost_estimate=cost(12 * masks * per_ref * voxels, 2 * voxels * (per_ref + 2 * masks)),
        compiler_params=room(16),
        name="brief",
    )(live, refs, wedge, owner, offset, wedge_id)


def lists_kernel(place, *rest):
    notes, out = rest[:-1], rest[-1]
    cap = out.shape[1]
    slots = notes[0].shape[1]
    earlier = hot(iota((slots, slots), 0) < iota((slots, slots), 1))
    before = jnp.zeros((1, 1), F32)
    total = jnp.zeros(out.shape, F32)
    for note in notes:
        info = note[0:4, :]
        named = jnp.logical_and(info[0:1] == place[3].astype(F32), info[3:4] > 0.0)
        chosen = named.astype(F32)
        rank = dot(jnp.broadcast_to(chosen, (8, slots)).astype(BF16), earlier)[0:1] + before
        order = hot(jnp.logical_and(iota((cap, slots), 0) == rank, named))
        listed = jnp.concatenate(
            [info[1:2] * chosen, info[2:3] * chosen, chosen, jnp.zeros((5, slots), F32)], axis=0
        )
        total = total + dot(listed.astype(BF16), order, LANES)
        before = before + jnp.sum(chosen, axis=1, keepdims=True)
    out[...] = total


def lists_of(place, notes, cap):
    return pl.pallas_call(
        lists_kernel,
        in_specs=[SMEM] + [VMEM] * len(notes),
        out_specs=VMEM,
        out_shape=jax.ShapeDtypeStruct((8, cap), F32),
        cost_estimate=cost(1 << 22, 1 << 18),
        compiler_params=room(8),
        name="lists",
    )(place, *notes)


def columns_of(listed):
    cap = listed.shape[1]
    eye = hot(iota((cap, cap), 0) == iota((cap, cap), 1))
    return dot(eye, listed.astype(BF16), LANES)


def select_kernel(sources, place, *rest):
    blocks, pairs, wedge, out = rest[:sources], rest[sources:-4], rest[-4], rest[-3]
    rows_hot, wedge_hot = rest[-2:]
    bunches, height, depth = rows_hot.shape
    count = 2 * len(pairs)
    cap = wedge_hot.shape[0] // count
    bunch = height // cap
    rows = depth // bunch
    masks = wedge.shape[0]

    @pl.when(pl.program_id(0) == 0)
    def _():
        rows_hot[...] = jnp.zeros_like(rows_hot)
        for g in range(count):
            columns = columns_of(pairs[g // 2][g % 2])
            n, at = g // bunch, g % bunch
            rows_hot[n, at * cap : (at + 1) * cap, at * rows : (at + 1) * rows] = hot(
                iota((cap, rows), 1) == columns[:, 0:1]
            )
            marks = (iota((cap, masks), 1) == columns[:, 1:2]).astype(F32)
            wedge_hot[g * cap : (g + 1) * cap, :] = jnp.concatenate([marks] * 3, axis=1).astype(
                BF16
            )

    tile = out.shape[1] // pl.num_programs(0)
    at = pl.multiple_of(pl.program_id(0) * tile, 128)

    def part_of(ref):
        if ref.shape[1] == tile:
            return ref[...]
        return ref[:, pl.ds(at, tile)]

    lined = jnp.concatenate(pieces_of(part_of(wedge), 3), axis=0)
    weights = dot(wedge_hot[...], lined)
    taken = 0
    for n in range(bunches):
        stack, have = [], 0
        while have < depth:
            stack.append(part_of(blocks[taken]))
            have += blocks[taken].shape[0]
            taken += 1
        values = dot(rows_hot[n], jnp.concatenate(stack, axis=0) if len(stack) > 1 else stack[0])
        part = slice(n * height, (n + 1) * height)
        out[part, pl.ds(at, tile)] = (weights[part] * values).astype(BF16)


def select(place, blocks, block_specs, pairs, wedge, wedge_spec, rows, tile, steps):
    count = 2 * len(pairs)
    cap = pairs[0].shape[2]
    masks = wedge.shape[0]
    bunch = max(n for n in (2, 4) if count % n == 0 and n * rows <= 256)
    return pl.pallas_call(
        functools.partial(select_kernel, len(blocks)),
        grid_spec=pltpu.PrefetchScalarGridSpec(
            num_scalar_prefetch=1,
            grid=(steps,),
            in_specs=[
                *block_specs,
                *[pl.BlockSpec((2, 8, cap), lambda t, s: (0, 0, 0))] * len(pairs),
                wedge_spec,
            ],
            out_specs=VMEM,
            scratch_shapes=[
                pltpu.VMEM((count // bunch, bunch * cap, bunch * rows), BF16),
                pltpu.VMEM((count * cap, 3 * masks), BF16),
            ],
        ),
        out_shape=jax.ShapeDtypeStruct((count * cap, steps * tile), BF16),
        cost_estimate=cost(
            4 * count * cap * 256 * steps * tile, 2 * count * (cap + rows) * steps * tile
        ),
        compiler_params=room(32),
        name="select",
    )(place, *blocks, *pairs, wedge)


def correl_kernel(blocks, tile, first, steps, shifts, scaled, *rest):
    refs, seeds, out, table = rest[: 2 * blocks], rest[2 * blocks : -2], rest[-2], rest[-1]
    per_ref, span = refs[0].shape
    out[...] = seeds[0][...] if seeds else jnp.zeros_like(out)
    for side in range(2):

        def step(t, carry, side=side):
            at = first + t * tile
            for p in range(blocks):
                cols = pl.ds(pl.multiple_of(at - shifts[p], tile), tile)
                table[p * per_ref : (p + 1) * per_ref, :] = refs[2 * p + side][:, cols]
            rows = scaled[:, pl.ds(pl.multiple_of(side * span + at, tile), tile)]
            out[...] += dot(rows, table[...], LANES)
            return carry

        lax.fori_loop(0, steps, step, 0)


def correl(scaled, tables, shifts, tile, first, steps, seeds):
    height = scaled.shape[0]
    blocks = len(tables[0])
    count = blocks * tables[0][0].shape[0]
    refs = [tables[i][p] for p in range(blocks) for i in range(2)]
    return pl.pallas_call(
        functools.partial(correl_kernel, blocks, tile, first, steps, shifts),
        in_specs=[VMEM] * (1 + len(refs) + len(seeds)),
        out_specs=VMEM,
        out_shape=jax.ShapeDtypeStruct((height, count), F32),
        scratch_shapes=[pltpu.VMEM((count, tile), BF16)],
        compiler_params=room(24),
        cost_estimate=cost(4 * height * count * steps * tile, 4 * steps * tile * (height + count)),
        name="correl",
    )(scaled, *refs, *seeds)


def weigh_kernel(scale, masks, own, got, pair, *rest):
    notes, out = rest[:-1], rest[-1]
    count, cap = out.shape[1], out.shape[2]
    per_ref = count // len(notes)
    lanes = notes[0].shape[1]
    norms = jnp.zeros((3 * masks, count), F32)
    for p, note in enumerate(notes):
        parts = jnp.concatenate(pieces_of(note[8 : 8 + masks, :], 3), axis=0)
        shifted = hot(
            jnp.logical_and(
                iota((lanes, count), 0) + float(p * per_ref) == iota((lanes, count), 1),
                iota((lanes, count), 0) < float(per_ref),
            )
        )
        norms = norms + dot(parts, shifted)
    norms = norms.astype(BF16)
    for side in range(2):
        columns = columns_of(pair[side])
        marks = (iota((cap, masks), 1) == columns[:, 1:2]).astype(F32)
        wedge_hot = jnp.concatenate([marks] * 3, axis=1).astype(BF16)
        mine = own[side * cap : (side + 1) * cap, :] + got[(1 - side) * cap : (2 - side) * cap, :]
        score = (mine - 0.5 * dot(wedge_hot, norms)) * scale
        score = jnp.exp(score - jnp.max(score, axis=1, keepdims=True))
        share = score / jnp.sum(score, axis=1, keepdims=True) * columns[:, 2:3]
        out[side] = share.T.astype(BF16)


def weigh(own, got, pair, notes, masks, scale):
    cap, count = own.shape[0] // 2, own.shape[1]
    return pl.pallas_call(
        functools.partial(weigh_kernel, scale, masks),
        in_specs=[VMEM] * (3 + len(notes)),
        out_specs=VMEM,
        out_shape=jax.ShapeDtypeStruct((2, count, cap), BF16),
        cost_estimate=cost(1 << 24, 1 << 18),
        compiler_params=room(16),
        name="weigh",
    )(own, got, pair, *notes)


def blend_kernel(layers, parts, blocks, masks, starts, place, *rest):
    weights, rest = rest[:layers], rest[layers:]
    scaled, pairs = rest[:parts], rest[parts : -blocks - 1]
    outs, turned = rest[-blocks - 1 : -1], rest[-1]
    cap = weights[0].shape[2]
    per_ref, tile = outs[0].shape[1:] if not pairs else (outs[0].shape[0], starts[1])
    for g in range(2 * layers):
        turned[:, g * cap : (g + 1) * cap] = weights[g // 2][g % 2]

    def mix(at):
        first, sums = 0, 0.0
        for part in scaled:
            height = part.shape[0]
            sums = sums + dot(turned[:, first : first + height], part[:, pl.ds(at, tile)])
            first += height
        return sums.astype(BF16)

    if pairs:

        def step(t, carry):
            at = pl.multiple_of(t * tile, tile)
            sums = mix(at)
            for p, out in enumerate(outs):
                out[:, pl.ds(at, tile)] = sums[p * per_ref : (p + 1) * per_ref, :]
            return carry

        lax.fori_loop(0, starts[0], step, 0)
        total = jnp.zeros((turned.shape[0], masks), F32)
        for g in range(2 * layers):
            marks = hot(iota((masks, cap), 0) == pairs[g // 2][g % 2, 1:2, :])
            total = total + dot(turned[:, g * cap : (g + 1) * cap], marks, LANES)
        split = jnp.concatenate(pieces_of(total, 3), axis=1)
        split = jnp.concatenate(
            [split, jnp.zeros((split.shape[0], 128 - split.shape[1]), BF16)], axis=1
        )
        for p, out in enumerate(outs):
            out[:, starts[0] * tile :] = split[p * per_ref : (p + 1) * per_ref, :]
    else:
        stretch = scaled[0].shape[1] // starts[0]

        def step(t, carry):
            sums = mix(pl.multiple_of((place[2] ^ t) * stretch + stretch - tile, 128))
            for p, out in enumerate(outs):
                out[t] = sums[p * per_ref : (p + 1) * per_ref, :]
            return carry

        lax.fori_loop(0, starts[0], step, 0)


def blend(place, weights, pairs, scaled, masks, blocks, tile, steps):
    layers = len(weights)
    _, count, cap = weights[0].shape
    per_ref = count // blocks
    shape = (per_ref, steps * tile + 128) if pairs else (steps, per_ref, tile)
    return pl.pallas_call(
        functools.partial(blend_kernel, layers, len(scaled), blocks, masks, (steps, tile)),
        in_specs=[SMEM] + [VMEM] * (layers + len(scaled) + len(pairs)),
        out_specs=[VMEM] * blocks,
        out_shape=[jax.ShapeDtypeStruct(shape, BF16)] * blocks,
        scratch_shapes=[pltpu.VMEM((count, 2 * layers * cap), BF16)],
        compiler_params=room(24),
        cost_estimate=cost(
            4 * layers * cap * count * steps * tile, 2 * (2 * layers * cap + count) * steps * tile
        ),
        name="blend",
    )(place, *weights, *scaled, *pairs)


def fold_kernel(parts, *refs):
    sources, outs = refs[:parts], refs[parts:]
    for t, out in enumerate(outs):
        total = sources[0][t].astype(F32)
        for source in sources[1:]:
            total = total + source[t].astype(F32)
        out[...] = total.astype(BF16)


def fold(parts):
    layers, per_ref, tile = parts[0].shape
    return pl.pallas_call(
        functools.partial(fold_kernel, len(parts)),
        in_specs=[VMEM] * len(parts),
        out_specs=[VMEM] * layers,
        out_shape=[jax.ShapeDtypeStruct((per_ref, tile), BF16)] * layers,
        cost_estimate=cost(0, 2 * (len(parts) + 1) * layers * per_ref * tile),
        compiler_params=room(16),
        name="fold",
    )(*parts)


def finish_kernel(blocks, place, *rest):
    shares, apart = rest[:blocks], rest[blocks:-4]
    wedge, out, held, went = rest[-4:]
    masks = wedge.shape[0]
    span = held.shape[1]
    keep = span - apart[0].shape[1]
    at = pl.multiple_of(place[1] * span, span)
    mass = 0.0
    for part in shares:
        mass = mass + part[:, keep : keep + 3 * masks].astype(F32)
    mass = mass[:, :masks] + mass[:, masks : 2 * masks] + mass[:, 2 * masks : 3 * masks]
    leaves = []
    half = keep // 256 * 128
    for i, (first, end) in enumerate(((0, half), (half, keep), (keep, span))):
        below = jnp.ones((held.shape[0], end - first), F32)
        for w in range(masks):
            row = wedge[w : w + 1, pl.ds(pl.multiple_of(at + first, 128), end - first)]
            below = below + mass[:, w : w + 1] * row
        total = 0.0
        for part in apart if i == 2 else shares:
            total = total + (part[...] if i == 2 else part[:, first:end]).astype(F32)
        held[:, first:end] = total / below
        leave = pltpu.make_async_copy(
            held.at[:, pl.ds(first, end - first)], out.at[:, pl.ds(first, end - first)], went.at[i]
        )
        leave.start()
        leaves.append(leave)
    for leave in leaves:
        leave.wait()


def finish(place, shares, apart, wedge, span):
    per_ref = shares[0].shape[0]
    blocks = len(shares)
    return pl.pallas_call(
        functools.partial(finish_kernel, blocks),
        in_specs=[SMEM] + [VMEM] * (blocks + len(apart) + 1),
        out_specs=HBM,
        out_shape=jax.ShapeDtypeStruct((per_ref, span), F32),
        scratch_shapes=[
            pltpu.VMEM((per_ref, span), F32),
            pltpu.SemaphoreType.DMA((3,)),
        ],
        compiler_params=room(16),
        cost_estimate=cost(0, 8 * per_ref * span),
        name="finish",
    )(place, *shares, *apart, wedge)


GRP = ("lay", "core")


def passed(values, axis, size):
    return [values[0]] + [
        lax.ppermute(values[p], axis, [(d, d ^ p) for d in range(size)]) for p in range(1, size)
    ]


def per_device(slab, pick_owner, pick_offset, wedge_id, live_count, references, wedge):
    slot_count, voxels = slab.shape
    masks = wedge.shape[0]
    layers = lax.axis_size("lay")
    groups = 2 * layers
    blocks = lax.axis_size("blk")
    per_vox = voxels // groups
    tile = per_vox * APART[0] // APART[1]
    keep = per_vox - tile
    steps = 2 if keep % 256 == 0 else 1
    half = voxels // 2
    cap = 2 * slot_count
    block = lax.axis_index("blk").astype(jnp.int32)
    core = lax.axis_index("core").astype(jnp.int32)
    layer = lax.axis_index("lay").astype(jnp.int32)
    place = jnp.stack([core, layer * 2 + core, layer, block])

    slab_hbm, refs_hbm = (
        pltpu.with_memory_space_constraint(value, pltpu.HBM) for value in (slab, references)
    )
    quarter = half // 8
    most = 3 * quarter
    low, high, aside = cut(place, refs_hbm, slab_hbm, layers, per_vox)
    mate = lax.ppermute(aside, "core", [(0, 1), (1, 0)])
    if blocks == 4:
        over_x, over_y = [(b, b ^ 1) for b in range(4)], [(b, b ^ 2) for b in range(4)]
        low_x = lax.ppermute(low, "blk", over_x)
        high_y = lax.ppermute(high, "blk", over_y)
        high_x = lax.ppermute(high, "blk", over_x)
        low_y = lax.ppermute(low, "blk", over_y)
        low_xy = lax.ppermute(low_x[:, :most], "blk", over_y)
        high_xy = lax.ppermute(high_y[:, :most], "blk", over_x)
        low_end = lax.ppermute(low_x[:, most:], "blk", over_y)
        high_end = lax.ppermute(high_y[:, most:], "blk", over_x)
        tables = [[low, low_x, low_y, low_xy], [high, high_x, high_y, high_xy]]
        ends = [[low, low_x, low_y, low_end], [high, high_x, high_y, high_end]]
        shifts = [0, 0, 0, most]
    else:
        tables = [passed([s] * blocks, "blk", blocks) for s in (low, high)]
        ends, shifts = tables, [0] * blocks
    far = deal(place, slab_hbm, mate, layers, keep)
    pieces = [None] * layers
    for p in range(1, layers):
        pieces[p] = lax.ppermute(far[p - 1], "lay", [(z, z ^ p) for z in range(layers)])
    note = brief(
        live_count,
        references,
        wedge,
        pick_owner.reshape(1, slot_count),
        pick_offset.reshape(1, slot_count),
        wedge_id.reshape(1, slot_count),
        2 * per_vox,
    )
    notes = passed([note] * blocks, "blk", blocks)
    listed = lists_of(place, notes, cap)
    pair = jnp.stack(passed([listed] * 2, "core", 2))

    scaled = select(
        place,
        [slab, mate],
        [
            pl.BlockSpec((slot_count, per_vox), lambda t, s: (0, 2 * t + s[0])),
            pl.BlockSpec((slot_count, per_vox), lambda t, s: (0, t)),
        ],
        [pair],
        wedge,
        pl.BlockSpec((masks, per_vox), lambda t, s: (0, 2 * t + s[0])),
        slot_count,
        per_vox,
        layers,
    )
    here = pl.BlockSpec((masks, per_vox), lambda t, s: (0, s[1]))
    near_rows = select(
        place,
        [slab, mate],
        [
            pl.BlockSpec((slot_count, per_vox), lambda t, s: (0, s[1])),
            pl.BlockSpec((slot_count, per_vox), lambda t, s: (0, s[2])),
        ],
        [pair],
        wedge,
        here,
        slot_count,
        keep // steps,
        steps,
    )
    pairs = passed([pair] * layers, "lay", layers)
    sums = correl(scaled, tables, [0] * blocks, quarter, 0, 3, [])
    sums = correl(scaled, ends, shifts, quarter, most, 1, [sums])
    got = lax.ppermute(sums, "core", [(0, 1), (1, 0)])
    weights = weigh(sums, got, pair, notes, masks, 1.0 / (32.0 * math.sqrt(voxels)))
    all_weights = passed([weights] * layers, "lay", layers)

    far_rows = select(
        place,
        pieces[1:],
        [VMEM] * (layers - 1),
        pairs[1:],
        wedge,
        here,
        slot_count,
        keep // steps,
        steps,
    )

    apart = blend(place, all_weights[:1], [], [scaled], masks, blocks, tile, layers)
    apart = passed(apart, "blk", blocks)
    apart = fold(apart)
    apart = passed(apart, "lay", layers)

    shares = blend(
        place, all_weights, pairs, [near_rows, far_rows], masks, blocks, keep // steps, steps
    )
    shares = passed(shares, "blk", blocks)
    return finish(place, shares, apart, wedge, per_vox)


def solution(mesh):
    groups, blocks = mesh.shape["grp"], mesh.shape["blk"]
    fine = Mesh(mesh.devices.reshape(groups // 2, 2, blocks), ("lay", "core", "blk"))
    every = ("lay", "core", "blk")
    placed = (P(every, None), P(every, None), P(every), P(every), P(every), P("blk", None), P())

    return jax.shard_map(
        per_device, mesh=fine, in_specs=placed, out_specs=P("blk", GRP), check_vma=False
    )
```

```python
import functools
import math

import jax
import jax.numpy as jnp
from jax import lax
from jax.experimental import pallas as pl
from jax.experimental.pallas import tpu as pltpu
from jax.sharding import Mesh
from jax.sharding import PartitionSpec as P

F32 = jnp.float32
BF16 = jnp.bfloat16
ROWS = (((1,), (0,)), ((), ()))
LANES = (((1,), (1,)), ((), ()))
VMEM = pl.BlockSpec(memory_space=pltpu.VMEM)
SMEM = pl.BlockSpec(memory_space=pltpu.SMEM)
HBM = pl.BlockSpec(memory_space=pltpu.HBM)
APART = (5, 16)


def dot(left, right, dims=ROWS):
    return lax.dot_general(left, right, dims, preferred_element_type=F32)


def pieces_of(value, count):
    parts = []
    for _ in range(count):
        part = value.astype(BF16)
        value = value - part.astype(F32)
        parts.append(part)
    return parts


def iota(shape, axis):
    return lax.broadcasted_iota(jnp.int32, shape, axis).astype(F32)


def hot(mask):
    return mask.astype(F32).astype(BF16)


def room(mebibytes):
    return pltpu.CompilerParams(vmem_limit_bytes=mebibytes << 20)


def cost(flops, moved):
    return pl.CostEstimate(flops=int(flops), bytes_accessed=int(moved), transcendentals=0)


def cut_kernel(place, refs, slab, *rest):
    outs, came = rest[:3], rest[3]
    layers = came.shape[1]
    per_vox = outs[2].shape[1] // layers
    core = place[0]
    copies = []
    for which, out in enumerate(outs):
        source, side = (slab, 1 - core) if which == 2 else (refs, core)
        first = layers // 2 if which == 1 else 0
        for z in range(out.shape[1] // per_vox):
            at = pl.multiple_of((2 * (first + z) + side) * per_vox, per_vox)
            copy = pltpu.make_async_copy(
                source.at[:, pl.ds(at, per_vox)],
                out.at[:, pl.ds(z * per_vox, per_vox)],
                came.at[which, z],
            )
            copy.start()
            copies.append(copy)
    for copy in copies:
        copy.wait()


def cut(place, refs, slab, layers, per_vox):
    shapes = [
        (layers // 2, refs.shape[0]),
        (layers // 2, refs.shape[0]),
        (layers, slab.shape[0]),
    ]
    return pl.pallas_call(
        cut_kernel,
        in_specs=[SMEM, HBM, HBM],
        out_specs=[VMEM] * 3,
        out_shape=[jax.ShapeDtypeStruct((r, n * per_vox), BF16) for n, r in shapes],
        scratch_shapes=[pltpu.SemaphoreType.DMA((3, layers))],
        compiler_params=room(16),
        cost_estimate=cost(0, 4 * sum(n * r for n, r in shapes) * per_vox),
        name="cut",
    )(place, refs, slab)


def deal_kernel(place, slab, mate, *rest):
    outs, came = rest[:-1], rest[-1]
    rows = slab.shape[0]
    keep = outs[0].shape[1]
    per_vox = mate.shape[1] // (len(outs) + 1)
    copies = []
    for p, out in enumerate(outs):
        layer = place[2] ^ (p + 1)
        mine = pl.multiple_of((2 * layer + place[0]) * per_vox, per_vox)
        theirs = pl.multiple_of(layer * per_vox, per_vox)
        copies += [
            pltpu.make_async_copy(
                slab.at[:, pl.ds(mine, keep)], out.at[pl.ds(0, rows)], came.at[p, 0]
            ),
            pltpu.make_async_copy(
                mate.at[:, pl.ds(theirs, keep)], out.at[pl.ds(rows, rows)], came.at[p, 1]
            ),
        ]
    for copy in copies:
        copy.start()
    for copy in copies:
        copy.wait()


def deal(place, slab, mate, layers, keep):
    rows = slab.shape[0]
    anywhere = pl.BlockSpec(memory_space=pl.ANY)
    peers = layers - 1
    return pl.pallas_call(
        deal_kernel,
        in_specs=[SMEM, HBM, anywhere],
        out_specs=[VMEM] * peers,
        out_shape=[jax.ShapeDtypeStruct((2 * rows, keep), BF16)] * peers,
        scratch_shapes=[pltpu.SemaphoreType.DMA((peers, 2))],
        compiler_params=room(16),
        cost_estimate=cost(0, 8 * rows * peers * keep),
        name="deal",
    )(place, slab, mate)


def brief_kernel(live, refs, wedge, owner, offset, wedge_id, out, sums):
    masks = wedge.shape[0]
    per_ref = refs.shape[0]
    slots = owner.shape[1]

    @pl.when(pl.program_id(0) == 0)
    def _():
        sums[...] = jnp.zeros_like(sums)

    wide = refs[...].astype(F32)
    high, low = pieces_of(wide * wide, 2)
    lined = jnp.concatenate(pieces_of(wedge[...], 3), axis=0)
    sums[...] += dot(lined, high, LANES) + dot(lined, low, LANES)

    @pl.when(pl.program_id(0) == pl.num_programs(0) - 1)
    def _():
        out[...] = jnp.zeros_like(out)
        out[0:1, :] = jnp.full((1, out.shape[1]), -1.0, F32)
        out[0:1, :slots] = owner[...].astype(F32)
        out[1:2, :slots] = offset[...].astype(F32)
        out[2:3, :slots] = wedge_id[...].astype(F32)
        out[3:4, :slots] = (iota((1, slots), 1) < live[0].astype(F32)).astype(F32)
        out[8 : 8 + masks, :per_ref] = (
            sums[:masks] + sums[masks : 2 * masks] + sums[2 * masks : 3 * masks]
        )


def brief(live, refs, wedge, owner, offset, wedge_id, tile):
    per_ref, voxels = refs.shape
    masks = wedge.shape[0]
    slots = owner.shape[1]
    height = -(-(8 + masks) // 8) * 8
    row = pl.BlockSpec((1, slots), lambda t, s: (0, 0))
    return pl.pallas_call(
        brief_kernel,
        grid_spec=pltpu.PrefetchScalarGridSpec(
            num_scalar_prefetch=1,
            grid=(voxels // tile,),
            in_specs=[
                pl.BlockSpec((per_ref, tile), lambda t, s: (0, t)),
                pl.BlockSpec((masks, tile), lambda t, s: (0, t)),
                row,
                row,
                row,
            ],
            out_specs=pl.BlockSpec((height, 128), lambda t, s: (0, 0)),
            scratch_shapes=[pltpu.VMEM((3 * masks, per_ref), F32)],
        ),
        out_shape=jax.ShapeDtypeStruct((height, 128), F32),
        cost_estimate=cost(12 * masks * per_ref * voxels, 2 * voxels * (per_ref + 2 * masks)),
        compiler_params=room(16),
        name="brief",
    )(live, refs, wedge, owner, offset, wedge_id)


def lists_kernel(place, *rest):
    notes, out = rest[:-1], rest[-1]
    cap = out.shape[1]
    slots = notes[0].shape[1]
    earlier = hot(iota((slots, slots), 0) < iota((slots, slots), 1))
    before = jnp.zeros((1, 1), F32)
    total = jnp.zeros(out.shape, F32)
    for note in notes:
        info = note[0:4, :]
        named = jnp.logical_and(info[0:1] == place[3].astype(F32), info[3:4] > 0.0)
        chosen = named.astype(F32)
        rank = dot(jnp.broadcast_to(chosen, (8, slots)).astype(BF16), earlier)[0:1] + before
        order = hot(jnp.logical_and(iota((cap, slots), 0) == rank, named))
        listed = jnp.concatenate(
            [info[1:2] * chosen, info[2:3] * chosen, chosen, jnp.zeros((5, slots), F32)], axis=0
        )
        total = total + dot(listed.astype(BF16), order, LANES)
        before = before + jnp.sum(chosen, axis=1, keepdims=True)
    out[...] = total


def lists_of(place, notes, cap):
    return pl.pallas_call(
        lists_kernel,
        in_specs=[SMEM] + [VMEM] * len(notes),
        out_specs=VMEM,
        out_shape=jax.ShapeDtypeStruct((8, cap), F32),
        cost_estimate=cost(1 << 22, 1 << 18),
        compiler_params=room(8),
        name="lists",
    )(place, *notes)


def columns_of(listed):
    cap = listed.shape[1]
    eye = hot(iota((cap, cap), 0) == iota((cap, cap), 1))
    return dot(eye, listed.astype(BF16), LANES)


def select_kernel(sources, place, *rest):
    blocks, pairs, wedge, out = rest[:sources], rest[sources:-4], rest[-4], rest[-3]
    rows_hot, wedge_hot = rest[-2:]
    bunches, height, depth = rows_hot.shape
    count = 2 * len(pairs)
    cap = wedge_hot.shape[0] // count
    bunch = height // cap
    rows = depth // bunch
    masks = wedge.shape[0]

    @pl.when(pl.program_id(0) == 0)
    def _():
        rows_hot[...] = jnp.zeros_like(rows_hot)
        for g in range(count):
            columns = columns_of(pairs[g // 2][g % 2])
            n, at = g // bunch, g % bunch
            rows_hot[n, at * cap : (at + 1) * cap, at * rows : (at + 1) * rows] = hot(
                iota((cap, rows), 1) == columns[:, 0:1]
            )
            marks = (iota((cap, masks), 1) == columns[:, 1:2]).astype(F32)
            wedge_hot[g * cap : (g + 1) * cap, :] = jnp.concatenate([marks] * 3, axis=1).astype(
                BF16
            )

    tile = out.shape[1] // pl.num_programs(0)
    at = pl.multiple_of(pl.program_id(0) * tile, 128)

    def part_of(ref):
        if ref.shape[1] == tile:
            return ref[...]
        return ref[:, pl.ds(at, tile)]

    lined = jnp.concatenate(pieces_of(part_of(wedge), 3), axis=0)
    weights = dot(wedge_hot[...], lined)
    taken = 0
    for n in range(bunches):
        stack, have = [], 0
        while have < depth:
            stack.append(part_of(blocks[taken]))
            have += blocks[taken].shape[0]
            taken += 1
        values = dot(rows_hot[n], jnp.concatenate(stack, axis=0) if len(stack) > 1 else stack[0])
        part = slice(n * height, (n + 1) * height)
        out[part, pl.ds(at, tile)] = (weights[part] * values).astype(BF16)


def select(place, blocks, block_specs, pairs, wedge, wedge_spec, rows, tile, steps):
    count = 2 * len(pairs)
    cap = pairs[0].shape[2]
    masks = wedge.shape[0]
    bunch = max(n for n in (2, 4) if count % n == 0 and n * rows <= 256)
    return pl.pallas_call(
        functools.partial(select_kernel, len(blocks)),
        grid_spec=pltpu.PrefetchScalarGridSpec(
            num_scalar_prefetch=1,
            grid=(steps,),
            in_specs=[
                *block_specs,
                *[pl.BlockSpec((2, 8, cap), lambda t, s: (0, 0, 0))] * len(pairs),
                wedge_spec,
            ],
            out_specs=VMEM,
            scratch_shapes=[
                pltpu.VMEM((count // bunch, bunch * cap, bunch * rows), BF16),
                pltpu.VMEM((count * cap, 3 * masks), BF16),
            ],
        ),
        out_shape=jax.ShapeDtypeStruct((count * cap, steps * tile), BF16),
        cost_estimate=cost(
            4 * count * cap * 256 * steps * tile, 2 * count * (cap + rows) * steps * tile
        ),
        compiler_params=room(32),
        name="select",
    )(place, *blocks, *pairs, wedge)


def correl_kernel(blocks, tile, first, steps, shifts, scaled, *rest):
    refs, seeds, out, table = rest[: 2 * blocks], rest[2 * blocks : -2], rest[-2], rest[-1]
    per_ref, span = refs[0].shape
    out[...] = seeds[0][...] if seeds else jnp.zeros_like(out)
    for side in range(2):

        def step(t, carry, side=side):
            at = first + t * tile
            for p in range(blocks):
                cols = pl.ds(pl.multiple_of(at - shifts[p], tile), tile)
                table[p * per_ref : (p + 1) * per_ref, :] = refs[2 * p + side][:, cols]
            rows = scaled[:, pl.ds(pl.multiple_of(side * span + at, tile), tile)]
            out[...] += dot(rows, table[...], LANES)
            return carry

        lax.fori_loop(0, steps, step, 0)


def correl(scaled, tables, shifts, tile, first, steps, seeds):
    height = scaled.shape[0]
    blocks = len(tables[0])
    count = blocks * tables[0][0].shape[0]
    refs = [tables[i][p] for p in range(blocks) for i in range(2)]
    return pl.pallas_call(
        functools.partial(correl_kernel, blocks, tile, first, steps, shifts),
        in_specs=[VMEM] * (1 + len(refs) + len(seeds)),
        out_specs=VMEM,
        out_shape=jax.ShapeDtypeStruct((height, count), F32),
        scratch_shapes=[pltpu.VMEM((count, tile), BF16)],
        compiler_params=room(24),
        cost_estimate=cost(4 * height * count * steps * tile, 4 * steps * tile * (height + count)),
        name="correl",
    )(scaled, *refs, *seeds)


def weigh_kernel(scale, masks, blocks, place, own, got, pair, scaled, *rest):
    notes, out, outs, turned = rest[:blocks], rest[blocks], rest[blocks + 1 : -1], rest[-1]
    count, cap = out.shape[1], out.shape[2]
    per_ref = count // len(notes)
    lanes = notes[0].shape[1]
    norms = jnp.zeros((3 * masks, count), F32)
    for p, note in enumerate(notes):
        parts = jnp.concatenate(pieces_of(note[8 : 8 + masks, :], 3), axis=0)
        shifted = hot(
            jnp.logical_and(
                iota((lanes, count), 0) + float(p * per_ref) == iota((lanes, count), 1),
                iota((lanes, count), 0) < float(per_ref),
            )
        )
        norms = norms + dot(parts, shifted)
    norms = norms.astype(BF16)
    for side in range(2):
        columns = columns_of(pair[side])
        marks = (iota((cap, masks), 1) == columns[:, 1:2]).astype(F32)
        wedge_hot = jnp.concatenate([marks] * 3, axis=1).astype(BF16)
        mine = own[side * cap : (side + 1) * cap, :] + got[(1 - side) * cap : (2 - side) * cap, :]
        score = (mine - 0.5 * dot(wedge_hot, norms)) * scale
        score = jnp.exp(score - jnp.max(score, axis=1, keepdims=True))
        share = score / jnp.sum(score, axis=1, keepdims=True) * columns[:, 2:3]
        weights = share.T.astype(BF16)
        out[side] = weights
        turned[:, side * cap : (side + 1) * cap] = weights
    steps, _, tile = outs[0].shape
    stretch = scaled.shape[1] // steps

    def step(t, carry):
        at = pl.multiple_of((place[2] ^ t) * stretch + stretch - tile, 128)
        sums = dot(turned[...], scaled[:, pl.ds(at, tile)]).astype(BF16)
        for p, apart in enumerate(outs):
            apart[t] = sums[p * per_ref : (p + 1) * per_ref, :]
        return carry

    lax.fori_loop(0, steps, step, 0)


def weigh(place, own, got, pair, scaled, notes, masks, scale, layers, tile):
    cap, count = own.shape[0] // 2, own.shape[1]
    blocks = len(notes)
    shapes = [(2, count, cap)] + [(layers, count // blocks, tile)] * blocks
    return pl.pallas_call(
        functools.partial(weigh_kernel, scale, masks, blocks),
        in_specs=[SMEM] + [VMEM] * (4 + blocks),
        out_specs=[VMEM] * len(shapes),
        out_shape=[jax.ShapeDtypeStruct(shape, BF16) for shape in shapes],
        scratch_shapes=[pltpu.VMEM((count, 2 * cap), BF16)],
        compiler_params=room(24),
        cost_estimate=cost(4 * cap * count * layers * tile, 1 << 21),
        name="weigh",
    )(place, own, got, pair, scaled, *notes)


def blend_kernel(layers, parts, blocks, masks, starts, place, *rest):
    weights, rest = rest[:layers], rest[layers:]
    scaled, pairs = rest[:parts], rest[parts : -blocks - 1]
    outs, turned = rest[-blocks - 1 : -1], rest[-1]
    cap = weights[0].shape[2]
    per_ref, tile = outs[0].shape[1:] if not pairs else (outs[0].shape[0], starts[1])
    for g in range(2 * layers):
        turned[:, g * cap : (g + 1) * cap] = weights[g // 2][g % 2]

    def mix(at):
        first, sums = 0, 0.0
        for part in scaled:
            height = part.shape[0]
            sums = sums + dot(turned[:, first : first + height], part[:, pl.ds(at, tile)])
            first += height
        return sums.astype(BF16)

    if pairs:

        def step(t, carry):
            at = pl.multiple_of(t * tile, tile)
            sums = mix(at)
            for p, out in enumerate(outs):
                out[:, pl.ds(at, tile)] = sums[p * per_ref : (p + 1) * per_ref, :]
            return carry

        lax.fori_loop(0, starts[0], step, 0)
        total = jnp.zeros((turned.shape[0], masks), F32)
        for g in range(2 * layers):
            marks = hot(iota((masks, cap), 0) == pairs[g // 2][g % 2, 1:2, :])
            total = total + dot(turned[:, g * cap : (g + 1) * cap], marks, LANES)
        split = jnp.concatenate(pieces_of(total, 3), axis=1)
        split = jnp.concatenate(
            [split, jnp.zeros((split.shape[0], 128 - split.shape[1]), BF16)], axis=1
        )
        for p, out in enumerate(outs):
            out[:, starts[0] * tile :] = split[p * per_ref : (p + 1) * per_ref, :]
    else:
        stretch = scaled[0].shape[1] // starts[0]

        def step(t, carry):
            sums = mix(pl.multiple_of((place[2] ^ t) * stretch + stretch - tile, 128))
            for p, out in enumerate(outs):
                out[t] = sums[p * per_ref : (p + 1) * per_ref, :]
            return carry

        lax.fori_loop(0, starts[0], step, 0)


def blend(place, weights, pairs, scaled, masks, blocks, tile, steps):
    layers = len(weights)
    _, count, cap = weights[0].shape
    per_ref = count // blocks
    shape = (per_ref, steps * tile + 128) if pairs else (steps, per_ref, tile)
    return pl.pallas_call(
        functools.partial(blend_kernel, layers, len(scaled), blocks, masks, (steps, tile)),
        in_specs=[SMEM] + [VMEM] * (layers + len(scaled) + len(pairs)),
        out_specs=[VMEM] * blocks,
        out_shape=[jax.ShapeDtypeStruct(shape, BF16)] * blocks,
        scratch_shapes=[pltpu.VMEM((count, 2 * layers * cap), BF16)],
        compiler_params=room(24),
        cost_estimate=cost(
            4 * layers * cap * count * steps * tile, 2 * (2 * layers * cap + count) * steps * tile
        ),
        name="blend",
    )(place, *weights, *scaled, *pairs)


def fold_kernel(parts, *refs):
    sources, outs = refs[:parts], refs[parts:]
    for t, out in enumerate(outs):
        total = sources[0][t].astype(F32)
        for source in sources[1:]:
            total = total + source[t].astype(F32)
        out[...] = total.astype(BF16)


def fold(parts):
    layers, per_ref, tile = parts[0].shape
    return pl.pallas_call(
        functools.partial(fold_kernel, len(parts)),
        in_specs=[VMEM] * len(parts),
        out_specs=[VMEM] * layers,
        out_shape=[jax.ShapeDtypeStruct((per_ref, tile), BF16)] * layers,
        cost_estimate=cost(0, 2 * (len(parts) + 1) * layers * per_ref * tile),
        compiler_params=room(16),
        name="fold",
    )(*parts)


def finish_kernel(blocks, place, *rest):
    shares, apart = rest[:blocks], rest[blocks:-4]
    wedge, out, held, went = rest[-4:]
    masks = wedge.shape[0]
    span = held.shape[1]
    keep = span - apart[0].shape[1]
    at = pl.multiple_of(place[1] * span, span)
    mass = 0.0
    for part in shares:
        mass = mass + part[:, keep : keep + 3 * masks].astype(F32)
    mass = mass[:, :masks] + mass[:, masks : 2 * masks] + mass[:, 2 * masks : 3 * masks]
    leaves = []
    half = keep // 256 * 128
    for i, (first, end) in enumerate(((0, half), (half, keep), (keep, span))):
        below = jnp.ones((held.shape[0], end - first), F32)
        for w in range(masks):
            row = wedge[w : w + 1, pl.ds(pl.multiple_of(at + first, 128), end - first)]
            below = below + mass[:, w : w + 1] * row
        total = 0.0
        for part in apart if i == 2 else shares:
            total = total + (part[...] if i == 2 else part[:, first:end]).astype(F32)
        held[:, first:end] = total / below
        leave = pltpu.make_async_copy(
            held.at[:, pl.ds(first, end - first)], out.at[:, pl.ds(first, end - first)], went.at[i]
        )
        leave.start()
        leaves.append(leave)
    for leave in leaves:
        leave.wait()


def finish(place, shares, apart, wedge, span):
    per_ref = shares[0].shape[0]
    blocks = len(shares)
    return pl.pallas_call(
        functools.partial(finish_kernel, blocks),
        in_specs=[SMEM] + [VMEM] * (blocks + len(apart) + 1),
        out_specs=HBM,
        out_shape=jax.ShapeDtypeStruct((per_ref, span), F32),
        scratch_shapes=[
            pltpu.VMEM((per_ref, span), F32),
            pltpu.SemaphoreType.DMA((3,)),
        ],
        compiler_params=room(16),
        cost_estimate=cost(0, 8 * per_ref * span),
        name="finish",
    )(place, *shares, *apart, wedge)


GRP = ("lay", "core")


def passed(values, axis, size):
    return [values[0]] + [
        lax.ppermute(values[p], axis, [(d, d ^ p) for d in range(size)]) for p in range(1, size)
    ]


def per_device(slab, pick_owner, pick_offset, wedge_id, live_count, references, wedge):
    slot_count, voxels = slab.shape
    masks = wedge.shape[0]
    layers = lax.axis_size("lay")
    groups = 2 * layers
    blocks = lax.axis_size("blk")
    per_vox = voxels // groups
    tile = per_vox * APART[0] // APART[1]
    keep = per_vox - tile
    steps = 2 if keep % 256 == 0 else 1
    half = voxels // 2
    cap = 2 * slot_count
    block = lax.axis_index("blk").astype(jnp.int32)
    core = lax.axis_index("core").astype(jnp.int32)
    layer = lax.axis_index("lay").astype(jnp.int32)
    place = jnp.stack([core, layer * 2 + core, layer, block])

    slab_hbm, refs_hbm = (
        pltpu.with_memory_space_constraint(value, pltpu.HBM) for value in (slab, references)
    )
    quarter = half // 8
    most = 3 * quarter
    low, high, aside = cut(place, refs_hbm, slab_hbm, layers, per_vox)
    mate = lax.ppermute(aside, "core", [(0, 1), (1, 0)])
    if blocks == 4:
        over_x, over_y = [(b, b ^ 1) for b in range(4)], [(b, b ^ 2) for b in range(4)]
        low_x = lax.ppermute(low, "blk", over_x)
        high_y = lax.ppermute(high, "blk", over_y)
        high_x = lax.ppermute(high, "blk", over_x)
        low_y = lax.ppermute(low, "blk", over_y)
        low_xy = lax.ppermute(low_x[:, :most], "blk", over_y)
        high_xy = lax.ppermute(high_y[:, :most], "blk", over_x)
        low_end = lax.ppermute(low_x[:, most:], "blk", over_y)
        high_end = lax.ppermute(high_y[:, most:], "blk", over_x)
        tables = [[low, low_x, low_y, low_xy], [high, high_x, high_y, high_xy]]
        ends = [[low, low_x, low_y, low_end], [high, high_x, high_y, high_end]]
        shifts = [0, 0, 0, most]
    else:
        tables = [passed([s] * blocks, "blk", blocks) for s in (low, high)]
        ends, shifts = tables, [0] * blocks
    far = deal(place, slab_hbm, mate, layers, keep)
    pieces = [None] * layers
    for p in range(1, layers):
        pieces[p] = lax.ppermute(far[p - 1], "lay", [(z, z ^ p) for z in range(layers)])
    note = brief(
        live_count,
        references,
        wedge,
        pick_owner.reshape(1, slot_count),
        pick_offset.reshape(1, slot_count),
        wedge_id.reshape(1, slot_count),
        2 * per_vox,
    )
    notes = passed([note] * blocks, "blk", blocks)
    listed = lists_of(place, notes, cap)
    pair = jnp.stack(passed([listed] * 2, "core", 2))

    scaled = select(
        place,
        [slab, mate],
        [
            pl.BlockSpec((slot_count, per_vox), lambda t, s: (0, 2 * t + s[0])),
            pl.BlockSpec((slot_count, per_vox), lambda t, s: (0, t)),
        ],
        [pair],
        wedge,
        pl.BlockSpec((masks, per_vox), lambda t, s: (0, 2 * t + s[0])),
        slot_count,
        per_vox,
        layers,
    )
    here = pl.BlockSpec((masks, per_vox), lambda t, s: (0, s[1]))
    near_rows = select(
        place,
        [slab, mate],
        [
            pl.BlockSpec((slot_count, per_vox), lambda t, s: (0, s[1])),
            pl.BlockSpec((slot_count, per_vox), lambda t, s: (0, s[2])),
        ],
        [pair],
        wedge,
        here,
        slot_count,
        keep // steps,
        steps,
    )
    pairs = passed([pair] * layers, "lay", layers)
    sums = correl(scaled, tables, [0] * blocks, quarter, 0, 3, [])
    sums = correl(scaled, ends, shifts, quarter, most, 1, [sums])
    got = lax.ppermute(sums, "core", [(0, 1), (1, 0)])
    scale = 1.0 / (32.0 * math.sqrt(voxels))
    weights, *apart = weigh(
        place, sums, got, pair, scaled, notes, masks, scale, layers, tile
    )
    all_weights = passed([weights] * layers, "lay", layers)

    far_rows = select(
        place,
        pieces[1:],
        [VMEM] * (layers - 1),
        pairs[1:],
        wedge,
        here,
        slot_count,
        keep // steps,
        steps,
    )

    apart = passed(apart, "blk", blocks)
    apart = fold(apart)
    apart = passed(apart, "lay", layers)

    shares = blend(
        place, all_weights, pairs, [near_rows, far_rows], masks, blocks, keep // steps, steps
    )
    shares = passed(shares, "blk", blocks)
    return finish(place, shares, apart, wedge, per_vox)


def solution(mesh):
    groups, blocks = mesh.shape["grp"], mesh.shape["blk"]
    fine = Mesh(mesh.devices.reshape(groups // 2, 2, blocks), ("lay", "core", "blk"))
    every = ("lay", "core", "blk")
    placed = (P(every, None), P(every, None), P(every), P(every), P(every), P("blk", None), P())

    return jax.shard_map(
        per_device, mesh=fine, in_specs=placed, out_specs=P("blk", GRP), check_vma=False
    )
```

```python
import functools
import math

import jax
import jax.numpy as jnp
from jax import lax
from jax.experimental import pallas as pl
from jax.experimental.pallas import tpu as pltpu
from jax.sharding import Mesh
from jax.sharding import PartitionSpec as P

F32 = jnp.float32
BF16 = jnp.bfloat16
ROWS = (((1,), (0,)), ((), ()))
LANES = (((1,), (1,)), ((), ()))
VMEM = pl.BlockSpec(memory_space=pltpu.VMEM)
SMEM = pl.BlockSpec(memory_space=pltpu.SMEM)
HBM = pl.BlockSpec(memory_space=pltpu.HBM)
APART = (5, 16)


def dot(left, right, dims=ROWS):
    return lax.dot_general(left, right, dims, preferred_element_type=F32)


def pieces_of(value, count):
    parts = []
    for _ in range(count):
        part = value.astype(BF16)
        value = value - part.astype(F32)
        parts.append(part)
    return parts


def iota(shape, axis):
    return lax.broadcasted_iota(jnp.int32, shape, axis).astype(F32)


def hot(mask):
    return mask.astype(F32).astype(BF16)


def room(mebibytes):
    return pltpu.CompilerParams(vmem_limit_bytes=mebibytes << 20)


def cost(flops, moved):
    return pl.CostEstimate(flops=int(flops), bytes_accessed=int(moved), transcendentals=0)


def cut_kernel(place, refs, slab, *rest):
    outs, came = rest[:3], rest[3]
    layers = came.shape[1]
    per_vox = outs[2].shape[1] // layers
    core = place[0]
    copies = []
    for which, out in enumerate(outs):
        source, side = (slab, 1 - core) if which == 2 else (refs, core)
        first = layers // 2 if which == 1 else 0
        for z in range(out.shape[1] // per_vox):
            at = pl.multiple_of((2 * (first + z) + side) * per_vox, per_vox)
            copy = pltpu.make_async_copy(
                source.at[:, pl.ds(at, per_vox)],
                out.at[:, pl.ds(z * per_vox, per_vox)],
                came.at[which, z],
            )
            copy.start()
            copies.append(copy)
    for copy in copies:
        copy.wait()


def cut(place, refs, slab, layers, per_vox):
    shapes = [
        (layers // 2, refs.shape[0]),
        (layers // 2, refs.shape[0]),
        (layers, slab.shape[0]),
    ]
    return pl.pallas_call(
        cut_kernel,
        in_specs=[SMEM, HBM, HBM],
        out_specs=[VMEM] * 3,
        out_shape=[jax.ShapeDtypeStruct((r, n * per_vox), BF16) for n, r in shapes],
        scratch_shapes=[pltpu.SemaphoreType.DMA((3, layers))],
        compiler_params=room(16),
        cost_estimate=cost(0, 4 * sum(n * r for n, r in shapes) * per_vox),
        name="cut",
    )(place, refs, slab)


def deal_kernel(place, slab, mate, *rest):
    outs, came = rest[:-1], rest[-1]
    rows = slab.shape[0]
    keep = outs[0].shape[1]
    per_vox = mate.shape[1] // (len(outs) + 1)
    copies = []
    for p, out in enumerate(outs):
        layer = place[2] ^ (p + 1)
        mine = pl.multiple_of((2 * layer + place[0]) * per_vox, per_vox)
        theirs = pl.multiple_of(layer * per_vox, per_vox)
        copies += [
            pltpu.make_async_copy(
                slab.at[:, pl.ds(mine, keep)], out.at[pl.ds(0, rows)], came.at[p, 0]
            ),
            pltpu.make_async_copy(
                mate.at[:, pl.ds(theirs, keep)], out.at[pl.ds(rows, rows)], came.at[p, 1]
            ),
        ]
    for copy in copies:
        copy.start()
    for copy in copies:
        copy.wait()


def deal(place, slab, mate, layers, keep):
    rows = slab.shape[0]
    anywhere = pl.BlockSpec(memory_space=pl.ANY)
    peers = layers - 1
    return pl.pallas_call(
        deal_kernel,
        in_specs=[SMEM, HBM, anywhere],
        out_specs=[VMEM] * peers,
        out_shape=[jax.ShapeDtypeStruct((2 * rows, keep), BF16)] * peers,
        scratch_shapes=[pltpu.SemaphoreType.DMA((peers, 2))],
        compiler_params=room(16),
        cost_estimate=cost(0, 8 * rows * peers * keep),
        name="deal",
    )(place, slab, mate)


def brief_kernel(live, refs, wedge, owner, offset, wedge_id, out, sums):
    masks = wedge.shape[0]
    per_ref = refs.shape[0]
    slots = owner.shape[1]

    @pl.when(pl.program_id(0) == 0)
    def _():
        sums[...] = jnp.zeros_like(sums)

    wide = refs[...].astype(F32)
    high, low = pieces_of(wide * wide, 2)
    lined = jnp.concatenate(pieces_of(wedge[...], 3), axis=0)
    sums[...] += dot(lined, high, LANES) + dot(lined, low, LANES)

    @pl.when(pl.program_id(0) == pl.num_programs(0) - 1)
    def _():
        out[...] = jnp.zeros_like(out)
        out[0:1, :] = jnp.full((1, out.shape[1]), -1.0, F32)
        out[0:1, :slots] = owner[...].astype(F32)
        out[1:2, :slots] = offset[...].astype(F32)
        out[2:3, :slots] = wedge_id[...].astype(F32)
        out[3:4, :slots] = (iota((1, slots), 1) < live[0].astype(F32)).astype(F32)
        out[8 : 8 + masks, :per_ref] = (
            sums[:masks] + sums[masks : 2 * masks] + sums[2 * masks : 3 * masks]
        )


def brief(live, refs, wedge, owner, offset, wedge_id, tile):
    per_ref, voxels = refs.shape
    masks = wedge.shape[0]
    slots = owner.shape[1]
    height = -(-(8 + masks) // 8) * 8
    row = pl.BlockSpec((1, slots), lambda t, s: (0, 0))
    return pl.pallas_call(
        brief_kernel,
        grid_spec=pltpu.PrefetchScalarGridSpec(
            num_scalar_prefetch=1,
            grid=(voxels // tile,),
            in_specs=[
                pl.BlockSpec((per_ref, tile), lambda t, s: (0, t)),
                pl.BlockSpec((masks, tile), lambda t, s: (0, t)),
                row,
                row,
                row,
            ],
            out_specs=pl.BlockSpec((height, 128), lambda t, s: (0, 0)),
            scratch_shapes=[pltpu.VMEM((3 * masks, per_ref), F32)],
        ),
        out_shape=jax.ShapeDtypeStruct((height, 128), F32),
        cost_estimate=cost(12 * masks * per_ref * voxels, 2 * voxels * (per_ref + 2 * masks)),
        compiler_params=room(16),
        name="brief",
    )(live, refs, wedge, owner, offset, wedge_id)


def lists_kernel(place, *rest):
    notes, out = rest[:-1], rest[-1]
    cap = out.shape[1]
    slots = notes[0].shape[1]
    earlier = hot(iota((slots, slots), 0) < iota((slots, slots), 1))
    before = jnp.zeros((1, 1), F32)
    total = jnp.zeros(out.shape, F32)
    for note in notes:
        info = note[0:4, :]
        named = jnp.logical_and(info[0:1] == place[3].astype(F32), info[3:4] > 0.0)
        chosen = named.astype(F32)
        rank = dot(jnp.broadcast_to(chosen, (8, slots)).astype(BF16), earlier)[0:1] + before
        order = hot(jnp.logical_and(iota((cap, slots), 0) == rank, named))
        listed = jnp.concatenate(
            [info[1:2] * chosen, info[2:3] * chosen, chosen, jnp.zeros((5, slots), F32)], axis=0
        )
        total = total + dot(listed.astype(BF16), order, LANES)
        before = before + jnp.sum(chosen, axis=1, keepdims=True)
    out[...] = total


def lists_of(place, notes, cap):
    return pl.pallas_call(
        lists_kernel,
        in_specs=[SMEM] + [VMEM] * len(notes),
        out_specs=VMEM,
        out_shape=jax.ShapeDtypeStruct((8, cap), F32),
        cost_estimate=cost(1 << 22, 1 << 18),
        compiler_params=room(8),
        name="lists",
    )(place, *notes)


def columns_of(listed):
    cap = listed.shape[1]
    eye = hot(iota((cap, cap), 0) == iota((cap, cap), 1))
    return dot(eye, listed.astype(BF16), LANES)


def select_kernel(sources, place, *rest):
    blocks, pairs, wedge, out = rest[:sources], rest[sources:-4], rest[-4], rest[-3]
    rows_hot, wedge_hot = rest[-2:]
    bunches, height, depth = rows_hot.shape
    count = 2 * len(pairs)
    cap = wedge_hot.shape[0] // count
    bunch = height // cap
    rows = depth // bunch
    masks = wedge.shape[0]

    @pl.when(pl.program_id(0) == 0)
    def _():
        rows_hot[...] = jnp.zeros_like(rows_hot)
        for g in range(count):
            columns = columns_of(pairs[g // 2][g % 2])
            n, at = g // bunch, g % bunch
            rows_hot[n, at * cap : (at + 1) * cap, at * rows : (at + 1) * rows] = hot(
                iota((cap, rows), 1) == columns[:, 0:1]
            )
            marks = (iota((cap, masks), 1) == columns[:, 1:2]).astype(F32)
            wedge_hot[g * cap : (g + 1) * cap, :] = jnp.concatenate([marks] * 3, axis=1).astype(
                BF16
            )

    tile = out.shape[1] // pl.num_programs(0)
    at = pl.multiple_of(pl.program_id(0) * tile, 128)

    def part_of(ref):
        if ref.shape[1] == tile:
            return ref[...]
        return ref[:, pl.ds(at, tile)]

    lined = jnp.concatenate(pieces_of(part_of(wedge), 3), axis=0)
    weights = dot(wedge_hot[...], lined)
    taken = 0
    for n in range(bunches):
        stack, have = [], 0
        while have < depth:
            stack.append(part_of(blocks[taken]))
            have += blocks[taken].shape[0]
            taken += 1
        values = dot(rows_hot[n], jnp.concatenate(stack, axis=0) if len(stack) > 1 else stack[0])
        part = slice(n * height, (n + 1) * height)
        out[part, pl.ds(at, tile)] = (weights[part] * values).astype(BF16)


def select(place, blocks, block_specs, pairs, wedge, wedge_spec, rows, tile, steps):
    count = 2 * len(pairs)
    cap = pairs[0].shape[2]
    masks = wedge.shape[0]
    bunch = max(n for n in (2, 4) if count % n == 0 and n * rows <= 256)
    return pl.pallas_call(
        functools.partial(select_kernel, len(blocks)),
        grid_spec=pltpu.PrefetchScalarGridSpec(
            num_scalar_prefetch=1,
            grid=(steps,),
            in_specs=[
                *block_specs,
                *[pl.BlockSpec((2, 8, cap), lambda t, s: (0, 0, 0))] * len(pairs),
                wedge_spec,
            ],
            out_specs=VMEM,
            scratch_shapes=[
                pltpu.VMEM((count // bunch, bunch * cap, bunch * rows), BF16),
                pltpu.VMEM((count * cap, 3 * masks), BF16),
            ],
        ),
        out_shape=jax.ShapeDtypeStruct((count * cap, steps * tile), BF16),
        cost_estimate=cost(
            4 * count * cap * 256 * steps * tile, 2 * count * (cap + rows) * steps * tile
        ),
        compiler_params=room(32),
        name="select",
    )(place, *blocks, *pairs, wedge)


def correl_kernel(blocks, tile, first, steps, shifts, scaled, *rest):
    refs, seeds, out, table = rest[: 2 * blocks], rest[2 * blocks : -2], rest[-2], rest[-1]
    per_ref, span = refs[0].shape
    out[...] = seeds[0][...] if seeds else jnp.zeros_like(out)
    for side in range(2):

        def step(t, carry, side=side):
            at = first + t * tile
            for p in range(blocks):
                cols = pl.ds(pl.multiple_of(at - shifts[p], tile), tile)
                table[p * per_ref : (p + 1) * per_ref, :] = refs[2 * p + side][:, cols]
            rows = scaled[:, pl.ds(pl.multiple_of(side * span + at, tile), tile)]
            out[...] += dot(rows, table[...], LANES)
            return carry

        lax.fori_loop(0, steps, step, 0)


def correl(scaled, tables, shifts, tile, first, steps, seeds):
    height = scaled.shape[0]
    blocks = len(tables[0])
    count = blocks * tables[0][0].shape[0]
    refs = [tables[i][p] for p in range(blocks) for i in range(2)]
    return pl.pallas_call(
        functools.partial(correl_kernel, blocks, tile, first, steps, shifts),
        in_specs=[VMEM] * (1 + len(refs) + len(seeds)),
        out_specs=VMEM,
        out_shape=jax.ShapeDtypeStruct((height, count), F32),
        scratch_shapes=[pltpu.VMEM((count, tile), BF16)],
        compiler_params=room(24),
        cost_estimate=cost(4 * height * count * steps * tile, 4 * steps * tile * (height + count)),
        name="correl",
    )(scaled, *refs, *seeds)


def weigh_kernel(scale, masks, blocks, place, own, got, pair, scaled, *rest):
    notes, out, outs, turned = rest[:blocks], rest[blocks], rest[blocks + 1 : -1], rest[-1]
    count, cap = out.shape[1], out.shape[2]
    per_ref = count // len(notes)
    lanes = notes[0].shape[1]
    norms = jnp.zeros((3 * masks, count), F32)
    for p, note in enumerate(notes):
        parts = jnp.concatenate(pieces_of(note[8 : 8 + masks, :], 3), axis=0)
        shifted = hot(
            jnp.logical_and(
                iota((lanes, count), 0) + float(p * per_ref) == iota((lanes, count), 1),
                iota((lanes, count), 0) < float(per_ref),
            )
        )
        norms = norms + dot(parts, shifted)
    norms = norms.astype(BF16)
    for side in range(2):
        columns = columns_of(pair[side])
        marks = (iota((cap, masks), 1) == columns[:, 1:2]).astype(F32)
        wedge_hot = jnp.concatenate([marks] * 3, axis=1).astype(BF16)
        mine = own[side * cap : (side + 1) * cap, :] + got[(1 - side) * cap : (2 - side) * cap, :]
        score = (mine - 0.5 * dot(wedge_hot, norms)) * scale
        score = jnp.exp(score - jnp.max(score, axis=1, keepdims=True))
        share = score / jnp.sum(score, axis=1, keepdims=True) * columns[:, 2:3]
        weights = share.T.astype(BF16)
        out[side] = weights
        turned[:, side * cap : (side + 1) * cap] = weights
    steps, _, tile = outs[0].shape
    stretch = scaled.shape[1] // steps

    def step(t, carry):
        at = pl.multiple_of((place[2] ^ t) * stretch + stretch - tile, 128)
        sums = dot(turned[...], scaled[:, pl.ds(at, tile)]).astype(BF16)
        for p, apart in enumerate(outs):
            apart[t] = sums[p * per_ref : (p + 1) * per_ref, :]
        return carry

    lax.fori_loop(0, steps, step, 0)


def weigh(place, own, got, pair, scaled, notes, masks, scale, layers, tile):
    cap, count = own.shape[0] // 2, own.shape[1]
    blocks = len(notes)
    shapes = [(2, count, cap)] + [(layers, count // blocks, tile)] * blocks
    return pl.pallas_call(
        functools.partial(weigh_kernel, scale, masks, blocks),
        in_specs=[SMEM] + [VMEM] * (4 + blocks),
        out_specs=[VMEM] * len(shapes),
        out_shape=[jax.ShapeDtypeStruct(shape, BF16) for shape in shapes],
        scratch_shapes=[pltpu.VMEM((count, 2 * cap), BF16)],
        compiler_params=room(24),
        cost_estimate=cost(4 * cap * count * layers * tile, 1 << 21),
        name="weigh",
    )(place, own, got, pair, scaled, *notes)


def blend_kernel(layers, parts, blocks, masks, starts, place, *rest):
    weights, rest = rest[:layers], rest[layers:]
    scaled, pairs = rest[:parts], rest[parts : -blocks - 1]
    outs, turned = rest[-blocks - 1 : -1], rest[-1]
    cap = weights[0].shape[2]
    per_ref, tile = outs[0].shape[1:] if not pairs else (outs[0].shape[0], starts[1])
    for g in range(2 * layers):
        turned[:, g * cap : (g + 1) * cap] = weights[g // 2][g % 2]

    def mix(at):
        first, sums = 0, 0.0
        for part in scaled:
            height = part.shape[0]
            sums = sums + dot(turned[:, first : first + height], part[:, pl.ds(at, tile)])
            first += height
        return sums.astype(BF16)

    if pairs:

        def step(t, carry):
            at = pl.multiple_of(t * tile, tile)
            sums = mix(at)
            for p, out in enumerate(outs):
                out[:, pl.ds(at, tile)] = sums[p * per_ref : (p + 1) * per_ref, :]
            return carry

        lax.fori_loop(0, starts[0], step, 0)
        total = jnp.zeros((turned.shape[0], masks), F32)
        for g in range(2 * layers):
            marks = hot(iota((masks, cap), 0) == pairs[g // 2][g % 2, 1:2, :])
            total = total + dot(turned[:, g * cap : (g + 1) * cap], marks, LANES)
        split = jnp.concatenate(pieces_of(total, 3), axis=1)
        split = jnp.concatenate(
            [split, jnp.zeros((split.shape[0], 128 - split.shape[1]), BF16)], axis=1
        )
        for p, out in enumerate(outs):
            out[:, starts[0] * tile :] = split[p * per_ref : (p + 1) * per_ref, :]
    else:
        stretch = scaled[0].shape[1] // starts[0]

        def step(t, carry):
            sums = mix(pl.multiple_of((place[2] ^ t) * stretch + stretch - tile, 128))
            for p, out in enumerate(outs):
                out[t] = sums[p * per_ref : (p + 1) * per_ref, :]
            return carry

        lax.fori_loop(0, starts[0], step, 0)


def blend(place, weights, pairs, scaled, masks, blocks, tile, steps):
    layers = len(weights)
    _, count, cap = weights[0].shape
    per_ref = count // blocks
    shape = (per_ref, steps * tile + 128) if pairs else (steps, per_ref, tile)
    return pl.pallas_call(
        functools.partial(blend_kernel, layers, len(scaled), blocks, masks, (steps, tile)),
        in_specs=[SMEM] + [VMEM] * (layers + len(scaled) + len(pairs)),
        out_specs=[VMEM] * blocks,
        out_shape=[jax.ShapeDtypeStruct(shape, BF16)] * blocks,
        scratch_shapes=[pltpu.VMEM((count, 2 * layers * cap), BF16)],
        compiler_params=room(24),
        cost_estimate=cost(
            4 * layers * cap * count * steps * tile, 2 * (2 * layers * cap + count) * steps * tile
        ),
        name="blend",
    )(place, *weights, *scaled, *pairs)


def fold_kernel(parts, *refs):
    sources, outs = refs[:parts], refs[parts:]
    for t, out in enumerate(outs):
        total = sources[0][t].astype(F32)
        for source in sources[1:]:
            total = total + source[t].astype(F32)
        out[...] = total.astype(BF16)


def fold(parts):
    layers, per_ref, tile = parts[0].shape
    return pl.pallas_call(
        functools.partial(fold_kernel, len(parts)),
        in_specs=[VMEM] * len(parts),
        out_specs=[VMEM] * layers,
        out_shape=[jax.ShapeDtypeStruct((per_ref, tile), BF16)] * layers,
        cost_estimate=cost(0, 2 * (len(parts) + 1) * layers * per_ref * tile),
        compiler_params=room(16),
        name="fold",
    )(*parts)


def finish_kernel(blocks, place, *rest):
    shares, apart = rest[:blocks], rest[blocks:-4]
    wedge, out, held, went = rest[-4:]
    masks = wedge.shape[0]
    span = held.shape[1]
    keep = span - apart[0].shape[1]
    at = pl.multiple_of(place[1] * span, span)
    mass = 0.0
    for part in shares:
        mass = mass + part[:, keep : keep + 3 * masks].astype(F32)
    mass = mass[:, :masks] + mass[:, masks : 2 * masks] + mass[:, 2 * masks : 3 * masks]
    leaves = []
    third = keep // 384 * 128
    edges = [keep, (keep + span) // 256 * 128, span]
    ranges = [*zip(edges[:-1], edges[1:]), (0, third), (third, 2 * third), (2 * third, keep)]
    for i, (first, end) in enumerate(ranges):
        below = jnp.ones((held.shape[0], end - first), F32)
        for w in range(masks):
            row = wedge[w : w + 1, pl.ds(pl.multiple_of(at + first, 128), end - first)]
            below = below + mass[:, w : w + 1] * row
        total = 0.0
        for part in apart if first >= keep else shares:
            shift = keep if first >= keep else 0
            total = total + part[:, first - shift : end - shift].astype(F32)
        held[:, first:end] = total / below
        leave = pltpu.make_async_copy(
            held.at[:, pl.ds(first, end - first)], out.at[:, pl.ds(first, end - first)], went.at[i]
        )
        leave.start()
        leaves.append(leave)
    for leave in leaves:
        leave.wait()


def finish(place, shares, apart, wedge, span):
    per_ref = shares[0].shape[0]
    blocks = len(shares)
    return pl.pallas_call(
        functools.partial(finish_kernel, blocks),
        in_specs=[SMEM] + [VMEM] * (blocks + len(apart) + 1),
        out_specs=HBM,
        out_shape=jax.ShapeDtypeStruct((per_ref, span), F32),
        scratch_shapes=[
            pltpu.VMEM((per_ref, span), F32),
            pltpu.SemaphoreType.DMA((5,)),
        ],
        compiler_params=room(16),
        cost_estimate=cost(0, 8 * per_ref * span),
        name="finish",
    )(place, *shares, *apart, wedge)


GRP = ("lay", "core")


def passed(values, axis, size):
    return [values[0]] + [
        lax.ppermute(values[p], axis, [(d, d ^ p) for d in range(size)]) for p in range(1, size)
    ]


def per_device(slab, pick_owner, pick_offset, wedge_id, live_count, references, wedge):
    slot_count, voxels = slab.shape
    masks = wedge.shape[0]
    layers = lax.axis_size("lay")
    groups = 2 * layers
    blocks = lax.axis_size("blk")
    per_vox = voxels // groups
    tile = per_vox * APART[0] // APART[1]
    keep = per_vox - tile
    steps = 2 if keep % 256 == 0 else 1
    half = voxels // 2
    cap = 2 * slot_count
    block = lax.axis_index("blk").astype(jnp.int32)
    core = lax.axis_index("core").astype(jnp.int32)
    layer = lax.axis_index("lay").astype(jnp.int32)
    place = jnp.stack([core, layer * 2 + core, layer, block])

    slab_hbm, refs_hbm = (
        pltpu.with_memory_space_constraint(value, pltpu.HBM) for value in (slab, references)
    )
    quarter = half // 8
    most = 3 * quarter
    low, high, aside = cut(place, refs_hbm, slab_hbm, layers, per_vox)
    mate = lax.ppermute(aside, "core", [(0, 1), (1, 0)])
    if blocks == 4:
        over_x, over_y = [(b, b ^ 1) for b in range(4)], [(b, b ^ 2) for b in range(4)]
        low_x = lax.ppermute(low, "blk", over_x)
        high_y = lax.ppermute(high, "blk", over_y)
        high_x = lax.ppermute(high, "blk", over_x)
        low_y = lax.ppermute(low, "blk", over_y)
        low_xy = lax.ppermute(low_x[:, :most], "blk", over_y)
        high_xy = lax.ppermute(high_y[:, :most], "blk", over_x)
        low_end = lax.ppermute(low_x[:, most:], "blk", over_y)
        high_end = lax.ppermute(high_y[:, most:], "blk", over_x)
        tables = [[low, low_x, low_y, low_xy], [high, high_x, high_y, high_xy]]
        ends = [[low, low_x, low_y, low_end], [high, high_x, high_y, high_end]]
        shifts = [0, 0, 0, most]
    else:
        tables = [passed([s] * blocks, "blk", blocks) for s in (low, high)]
        ends, shifts = tables, [0] * blocks
    far = deal(place, slab_hbm, mate, layers, keep)
    pieces = [None] * layers
    for p in range(1, layers):
        pieces[p] = lax.ppermute(far[p - 1], "lay", [(z, z ^ p) for z in range(layers)])
    note = brief(
        live_count,
        references,
        wedge,
        pick_owner.reshape(1, slot_count),
        pick_offset.reshape(1, slot_count),
        wedge_id.reshape(1, slot_count),
        2 * per_vox,
    )
    notes = passed([note] * blocks, "blk", blocks)
    listed = lists_of(place, notes, cap)
    pair = jnp.stack(passed([listed] * 2, "core", 2))

    scaled = select(
        place,
        [slab, mate],
        [
            pl.BlockSpec((slot_count, per_vox), lambda t, s: (0, 2 * t + s[0])),
            pl.BlockSpec((slot_count, per_vox), lambda t, s: (0, t)),
        ],
        [pair],
        wedge,
        pl.BlockSpec((masks, per_vox), lambda t, s: (0, 2 * t + s[0])),
        slot_count,
        per_vox,
        layers,
    )
    here = pl.BlockSpec((masks, per_vox), lambda t, s: (0, s[1]))
    near_rows = select(
        place,
        [slab, mate],
        [
            pl.BlockSpec((slot_count, per_vox), lambda t, s: (0, s[1])),
            pl.BlockSpec((slot_count, per_vox), lambda t, s: (0, s[2])),
        ],
        [pair],
        wedge,
        here,
        slot_count,
        keep // steps,
        steps,
    )
    pairs = passed([pair] * layers, "lay", layers)
    sums = correl(scaled, tables, [0] * blocks, quarter, 0, 3, [])
    sums = correl(scaled, ends, shifts, quarter, most, 1, [sums])
    got = lax.ppermute(sums, "core", [(0, 1), (1, 0)])
    scale = 1.0 / (32.0 * math.sqrt(voxels))
    weights, *apart = weigh(
        place, sums, got, pair, scaled, notes, masks, scale, layers, tile
    )
    all_weights = passed([weights] * layers, "lay", layers)

    far_rows = select(
        place,
        pieces[1:],
        [VMEM] * (layers - 1),
        pairs[1:],
        wedge,
        here,
        slot_count,
        keep // steps,
        steps,
    )

    apart = passed(apart, "blk", blocks)
    apart = fold(apart)
    apart = passed(apart, "lay", layers)

    shares = blend(
        place, all_weights, pairs, [near_rows, far_rows], masks, blocks, keep // steps, steps
    )
    shares = passed(shares, "blk", blocks)
    return finish(place, shares, apart, wedge, per_vox)


def solution(mesh):
    groups, blocks = mesh.shape["grp"], mesh.shape["blk"]
    fine = Mesh(mesh.devices.reshape(groups // 2, 2, blocks), ("lay", "core", "blk"))
    every = ("lay", "core", "blk")
    placed = (P(every, None), P(every, None), P(every), P(every), P(every), P("blk", None), P())

    return jax.shard_map(
        per_device, mesh=fine, in_specs=placed, out_specs=P("blk", GRP), check_vma=False
    )
```
